32 devices in a mesh: gx: 2 (over x), yz: 16 (over z, y, core).
Axes of the slice: x: 2, y: 2, z: 4, core: 2. Of those that a mesh axis runs over, the one named last changes fastest.
Arguments:
- system_source_term: float32 [320, 4096], P(None, ('gx', 'yz')), may hold values from -200 to 200
- mass_plus_source: float32 [320, 4096], P(None, ('gx', 'yz')), may hold values from 1 to 4
- lifted_upwind_coupling: float32 [480, 4096], P(None, ('gx', 'yz')), may hold values from 0.5 to 2
- frozen_direction_derivative: float32 [75, 4096], P(None, ('gx', 'yz')), may hold values from -3 to 3
- first_solve_matrix: float32 [320, 320], replicated, may hold values from -0.3125 to 0.3125
- final_solve_matrix: float32 [320, 320], replicated, may hold values from -0.3125 to 0.3125
- middle_cell_matrices: float32 [320, 4096], P(None, ('gx', 'yz')), may hold values from 0.3 to 3
- adjacent_table_slots: int32 [6, 4096], P(None, ('gx', 'yz')), may hold values from 0 to 1264, as said below
- plane_outgoing_cells: int32 [32, 2, 16], P(('gx', 'yz')), may hold values from 0 to 127
- band_outgoing_cells: int32 [32, 2, 16], P(('gx', 'yz')), may hold values from 0 to 127
- small_side_table_slot: int32 [32, 352], P(('gx', 'yz')), may hold values from 0 to 768, as said below
- proprietor_mortar_index: int32 [32, 352], P(('gx', 'yz')), may hold values from 0 to 80, as said below
- outgoing_quadrant_index: int32 [32, 352], P(('gx', 'yz')), may hold values from 0 to 3, as said below
- incoming_mortar_index: int32 [32, 352], P(('gx', 'yz')), may hold values from 0 to 80
- incoming_quadrant_index: int32 [32, 352], P(('gx', 'yz')), may hold values from 0 to 3, as said below
- coarse_mortar_table_slot: int32 [32, 80], P(('gx', 'yz')), may hold values from 0 to 767
Outputs:
- newton_update: float32 [320, 4096], P(None, ('gx', 'yz'))
The draws below stay inside these ranges and needn't reach their ends.
Inputs may be any that keep to these rules, and one draw needn't show every extreme that they name: `adjacent_table_slots`: column of the neighbour trace in the device's table; 1264 marks a boundary face. `small_side_table_slot`: 768 marks an empty slot, exactly where proprietor_mortar_index is 80. Send slot (m, c) of device (g, k) and receive slot (k, c) of device (g, m) hold the same tile: there proprietor_mortar_index, outgoing_quadrant_index equal incoming_mortar_index, incoming_quadrant_index here; 80 marks an empty slot; no position of an owner's hanging face is sent twice; the live hanging faces of an owner are its first ones; from one device to one owner go at most 22 tiles, a bound reached in every draw; in each gx plane one owner receives 4 * 80 tiles. `outgoing_quadrant_index`: 0 in empty slots. `incoming_quadrant_index`: 0 in empty slots.
All inputs are finite; a program needn't handle non-finite values.
Results may differ from the reference program's by a relative error of at most 0.0003.
Values sent between devices are 32-bit elements; how exact they have to be, the bound alone decides.
No kernel may reach another device: no remote copies, remote signals or barrier semaphores. Data moves between devices by JAX's collectives and lax.ppermute only.
A program may use at most 64 MiB of HBM per device.

```python
import math
import jax
import jax.numpy as jnp
import numpy as np
from jax import lax

CELL_DOF_SIZE = 320
FACE = 80
ELEM_DEV = 128
HANG = 80
ITERS = 2
CELL_TOTAL = 4096
HALO_SLOTS = 16
CAP = 22
TABLE = 1264
N_GX = 2
N_YZ = 16


def mortar_lists(key):
    subkeys = jax.random.split(jax.random.fold_in(key, 17), 4)
    period = N_YZ - 1
    slot_count = N_YZ * CAP
    devices = N_GX * N_YZ
    full_shape = (N_GX, N_YZ, 4 * HANG)
    live_count = jax.random.randint(subkeys[0], (N_GX, N_YZ), 1, 3 * HANG // 4 + 1)
    busiest = jax.random.randint(subkeys[1], (N_GX, 1), 0, N_YZ)
    owner_id = jnp.arange(N_YZ, dtype=jnp.int32)[None, :]
    live_count = jnp.where(owner_id == busiest, HANG, live_count)
    offsets = jax.random.randint(subkeys[2], (N_GX, N_YZ), 0, period)
    tile_id = jnp.arange(4 * HANG, dtype=jnp.int32)[None, None, :]
    plane_id = jnp.arange(N_GX, dtype=jnp.int32)[:, None, None]
    owner_three = owner_id[:, :, None]
    source = jnp.broadcast_to((owner_three + 1 + (offsets[:, :, None] + tile_id) % period) % N_YZ, full_shape)
    slot_id = jnp.broadcast_to(tile_id // period, full_shape)
    is_live = tile_id < 4 * live_count[:, :, None]
    hang_value = jnp.broadcast_to(jnp.where(is_live, tile_id // 4, HANG), full_shape).reshape(-1)
    pos_value = jnp.broadcast_to(jnp.where(is_live, tile_id % 4, 0), full_shape).reshape(-1)
    send_row = (plane_id * N_YZ + source).reshape(-1)
    send_col = jnp.broadcast_to(owner_three * CAP + slot_id, full_shape).reshape(-1)
    recv_row = jnp.broadcast_to(plane_id * N_YZ + owner_three, full_shape).reshape(-1)
    recv_col = (source * CAP + slot_id).reshape(-1)
    unused = jnp.full((devices, slot_count), HANG, jnp.int32)
    zeros_int = jnp.zeros((devices, slot_count), jnp.int32)
    proprietor_mortar_index = unused.at[send_row, send_col].set(hang_value)
    outgoing_quadrant_index = zeros_int.at[send_row, send_col].set(pos_value)
    incoming_mortar_index = unused.at[recv_row, recv_col].set(hang_value)
    incoming_quadrant_index = zeros_int.at[recv_row, recv_col].set(pos_value)
    face_pick = jax.random.randint(subkeys[3], (devices, slot_count), 0, 6 * ELEM_DEV)
    small_side_table_slot = jnp.where(proprietor_mortar_index < HANG, face_pick, 6 * ELEM_DEV)
    return (small_side_table_slot, proprietor_mortar_index, outgoing_quadrant_index, incoming_mortar_index, incoming_quadrant_index)


def draw_small_side_table_slot(key, part):
    return mortar_lists(key)[0]


def draw_proprietor_mortar_index(key, part):
    return mortar_lists(key)[1]


def draw_outgoing_quadrant_index(key, part):
    return mortar_lists(key)[2]


def draw_incoming_mortar_index(key, part):
    return mortar_lists(key)[3]


def draw_incoming_quadrant_index(key, part):
    return mortar_lists(key)[4]


def draw_adjacent_table_slots(key, part):
    subkeys = jax.random.split(jax.random.fold_in(key, 3), 5)
    full_shape = (6, CELL_TOTAL)
    category = jax.random.randint(subkeys[0], full_shape, 0, 10)
    face_id = jnp.broadcast_to(jnp.arange(6, dtype=jnp.int32)[:, None], full_shape)
    opposite = face_id + 1 - 2 * (face_id % 2)
    local_column = opposite * ELEM_DEV + jax.random.randint(subkeys[1], full_shape, 0, ELEM_DEV)
    halo_base = 6 * ELEM_DEV + jnp.where(face_id < 2, 0, 2 * HALO_SLOTS) + jnp.where(face_id % 2 == 0, 0, HALO_SLOTS)
    halo_column = halo_base + jax.random.randint(subkeys[2], full_shape, 0, HALO_SLOTS)
    hang_column = 6 * ELEM_DEV + 4 * HALO_SLOTS + jax.random.randint(subkeys[3], full_shape, 0, HANG)
    reply_column = 6 * ELEM_DEV + 4 * HALO_SLOTS + HANG + jax.random.randint(subkeys[4], full_shape, 0, N_YZ * CAP)
    is_halo = (category == 4) | (face_id < 2) & (category == 3)
    chosen = jnp.where(category == 9, TABLE, reply_column)
    chosen = jnp.where(category == 5, hang_column, chosen)
    chosen = jnp.where(category < 5, local_column, chosen)
    chosen = jnp.where(is_halo, halo_column, chosen)
    return chosen.astype(jnp.int32)


def draw_system_source_term(key, part):
    subkeys = jax.random.split(jax.random.fold_in(key, 5), 3)
    columns = jnp.arange(CELL_TOTAL, dtype=jnp.int32)
    device_id = (columns // ELEM_DEV).astype(jnp.float32)
    rising = jnp.exp(jnp.log(3.0) * device_id / (N_GX * N_YZ - 1))
    row_scale = jnp.exp(jax.random.uniform(subkeys[1], (CELL_DOF_SIZE,), jnp.float32, jnp.log(0.3), jnp.log(3.0)))
    column_scale = jnp.exp(jax.random.uniform(subkeys[2], (CELL_TOTAL,), jnp.float32, jnp.log(0.3), jnp.log(3.0)))
    noise = jnp.clip(jax.random.normal(subkeys[0], (CELL_DOF_SIZE, CELL_TOTAL), jnp.float32), -4.0, 4.0)
    return noise * row_scale[:, None] * column_scale[None, :] * rising[None, :]


def plant(values, key, low, largest):
    index_at = [jax.random.randint(jax.random.fold_in(key, axis), (), 0, length) for axis, length in enumerate(values.shape)]
    longest = values.shape.index(max(values.shape))
    beside = index_at[:longest] + [(index_at[longest] + 1) % values.shape[longest]] + index_at[longest + 1:]
    return values.at[tuple(index_at)].set(low).at[tuple(beside)].set(largest)


def block_scale(own_key, dims, cuts, least, top_value):
    level, own = 1.0, jax.random.fold_in(own_key, 6)
    for dim, parts in cuts:
        heights = jnp.exp(jax.random.uniform(jax.random.fold_in(own, dim), (parts,), jnp.float32, least / len(cuts), top_value / len(cuts)))
        level = level * jnp.repeat(heights, dims[dim] // parts).reshape([-1 if axis == dim else 1 for axis in range(len(dims))])
    return level


def scatter_about(own_key, extent, width, limit, cuts=(), held_as=jnp.bfloat16):
    values = width * jax.random.normal(own_key, extent, jnp.float32)
    if cuts:
        values = values * block_scale(own_key, extent, cuts, -0.22, 0.18)
    return jnp.clip(values, -limit, limit).astype(held_as)


def setup_inputs(seed: int = 0) -> dict:
    arg_keys = jax.random.split(jax.random.key(seed), 17)
    return {
        "system_source_term": draw_system_source_term(jax.random.fold_in(arg_keys[16], 71), 0),
        "mass_plus_source": jnp.clip(jnp.exp(math.log(4.0) - 1.3862944 * jax.random.uniform(arg_keys[1], (CELL_DOF_SIZE, CELL_TOTAL), jnp.float32) ** block_scale(arg_keys[1], (CELL_DOF_SIZE, CELL_TOTAL), ((1, 32),), -0.2, 0.2)), 1.0, 4.0),
        "lifted_upwind_coupling": jnp.clip(jnp.exp(math.log(2.0) - 1.3862944 * jax.random.uniform(arg_keys[2], (6 * FACE, CELL_TOTAL), jnp.float32) ** block_scale(arg_keys[2], (6 * FACE, CELL_TOTAL), ((1, 32),), -0.2, 0.2)), 0.5, 2.0),
        "frozen_direction_derivative": scatter_about(arg_keys[3], (75, CELL_TOTAL), 0.5, 3.0, ((1, 32),), jnp.float32),
        "first_solve_matrix": scatter_about(arg_keys[4], (CELL_DOF_SIZE, CELL_DOF_SIZE), CELL_DOF_SIZE ** -0.5, 0.3125, (), jnp.float32),
        "final_solve_matrix": scatter_about(arg_keys[5], (CELL_DOF_SIZE, CELL_DOF_SIZE), CELL_DOF_SIZE ** -0.5, 0.3125, (), jnp.float32),
        "middle_cell_matrices": jnp.clip(jnp.exp(math.log(3.0) - 2.3025851 * jax.random.uniform(arg_keys[6], (CELL_DOF_SIZE, CELL_TOTAL), jnp.float32) ** block_scale(arg_keys[6], (CELL_DOF_SIZE, CELL_TOTAL), ((1, 32),), -0.2, 0.2)), 0.3, 3.0),
        "adjacent_table_slots": draw_adjacent_table_slots(jax.random.fold_in(arg_keys[16], 71), 0),
        "plane_outgoing_cells": plant(jax.random.randint(arg_keys[8], (N_GX * N_YZ, 2, HALO_SLOTS), 0, ELEM_DEV), jax.random.fold_in(arg_keys[8], 1), 0, ELEM_DEV - 1).astype(jnp.int32),
        "band_outgoing_cells": plant(jax.random.randint(arg_keys[9], (N_GX * N_YZ, 2, HALO_SLOTS), 0, ELEM_DEV), jax.random.fold_in(arg_keys[9], 1), 0, ELEM_DEV - 1).astype(jnp.int32),
        "small_side_table_slot": draw_small_side_table_slot(jax.random.fold_in(arg_keys[16], 71), 0),
        "proprietor_mortar_index": draw_proprietor_mortar_index(jax.random.fold_in(arg_keys[16], 71), 0),
        "outgoing_quadrant_index": draw_outgoing_quadrant_index(jax.random.fold_in(arg_keys[16], 71), 0),
        "incoming_mortar_index": draw_incoming_mortar_index(jax.random.fold_in(arg_keys[16], 71), 0),
        "incoming_quadrant_index": draw_incoming_quadrant_index(jax.random.fold_in(arg_keys[16], 71), 0),
        "coarse_mortar_table_slot": plant(jax.random.randint(arg_keys[15], (N_GX * N_YZ, HANG), 0, 6 * ELEM_DEV), jax.random.fold_in(arg_keys[15], 1), 0, (6 * ELEM_DEV) - 1).astype(jnp.int32),
    }


maximum_depth = lax.Precision.HIGHEST
epsilon = 1e-06

def gll_tables():
    inv_root = 1.0 / np.sqrt(5.0)
    gll_points = np.array([-1.0, -inv_root, inv_root, 1.0])
    weights = np.array([1.0, 5.0, 5.0, 1.0]) / 6.0

    def lagrange(points):
        values_at = np.ones((len(points), 4))
        for table_slot_index in range(4):
            for m in range(4):
                if m != table_slot_index:
                    values_at[:, table_slot_index] = values_at[:, table_slot_index] * (points - gll_points[m]) / (gll_points[table_slot_index] - gll_points[m])
        return values_at
    derivative = np.zeros((4, 4))
    for i in range(4):
        for table_slot_index in range(4):
            summed = 0.0
            for m in range(4):
                if m != table_slot_index:
                    product_term = 1.0 / (gll_points[table_slot_index] - gll_points[m])
                    for n in range(4):
                        if n != table_slot_index and n != m:
                            product_term = product_term * (gll_points[i] - gll_points[n]) / (gll_points[table_slot_index] - gll_points[n])
                    summed = summed + product_term
            derivative[i, table_slot_index] = summed
    halves = [lagrange((gll_points - 1.0) / 2.0), lagrange((gll_points + 1.0) / 2.0)]
    half_projections = [0.5 * (1.0 / weights)[:, None] * halve.T * weights[None, :] for halve in halves]
    interpolate = np.stack([np.kron(halves[q // 2], halves[q % 2]) for q in range(4)])
    projection = np.stack([np.kron(half_projections[q // 2], half_projections[q % 2]) for q in range(4)])
    return (jnp.asarray(derivative, jnp.float32), jnp.asarray(interpolate, jnp.float32), jnp.asarray(projection, jnp.float32))

def face_selector(face_id):
    selector = [slice(None)] * 5
    selector[face_id // 2 + 1] = 0 if face_id % 2 == 0 else 3
    return tuple(selector)

def own_traces(argument_array):
    local_count = argument_array.shape[1]
    cube_view = argument_array.reshape(5, 4, 4, 4, local_count)
    return jnp.concatenate([cube_view[face_selector(f)].reshape(80, local_count) for f in range(6)], axis=1)

def jacobian(argument_array, own_faces, near_faces, mass_plus_source, lifted_upwind_coupling, frozen_direction_derivative, derivative):
    local_count = argument_array.shape[1]
    cube_view = argument_array.reshape(5, 4, 4, 4, local_count)
    flux_blocks = frozen_direction_derivative.reshape(3, 5, 5, local_count)
    result = (mass_plus_source * argument_array).reshape(5, 4, 4, 4, local_count)
    contractions = ('mi,aijke->amjke', 'mj,aijke->aimke', 'mk,aijke->aijme')
    for direction in range(3):
        flux_term = jnp.einsum('abe,bijke->aijke', flux_blocks[direction], cube_view, precision=maximum_depth)
        result = result + jnp.einsum(contractions[direction], derivative, flux_term, precision=maximum_depth)
    for face_id in range(6):
        first_col = face_id * local_count
        face_jump = lifted_upwind_coupling[face_id * 80:(face_id + 1) * 80] * (own_faces[:, first_col:first_col + local_count] - near_faces[:, first_col:first_col + local_count])
        result = result.at[face_selector(face_id)].add(face_jump.reshape(5, 4, 4, local_count))
    return result.reshape(320, local_count)

def solve_cell_system(argument_array, first_solve_matrix, final_solve_matrix, middle_cell_matrices):
    interior_share = jnp.dot(first_solve_matrix, argument_array, precision=maximum_depth, preferred_element_type=jnp.float32)
    return jnp.dot(final_solve_matrix, middle_cell_matrices * interior_share, precision=maximum_depth, preferred_element_type=jnp.float32)

def mortar_sums(received, incoming_mortar_index, incoming_quadrant_index, projection, hang_count):
    slot_count = received.shape[1]
    face_values = received.reshape(5, 16, slot_count)
    candidates = jnp.einsum('qmn,anc->qamc', projection, face_values, precision=maximum_depth)
    selector_q = (incoming_quadrant_index[None, :] == jnp.arange(4, dtype=jnp.int32)[:, None]).astype(jnp.float32)
    projected = lax.optimization_barrier(jnp.sum(candidates * selector_q[:, None, None, :], axis=0)).reshape(80, slot_count)
    onehot = (incoming_mortar_index[:, None] == jnp.arange(hang_count, dtype=jnp.int32)[None, :]).astype(jnp.float32)
    return jnp.dot(projected, onehot, precision=maximum_depth, preferred_element_type=jnp.float32)

def fine_replies(coarse_cols, outgoing_quadrant_index, interpolate):
    slot_count = coarse_cols.shape[1]
    face_values = coarse_cols.reshape(5, 16, slot_count)
    candidates = jnp.einsum('qmn,anc->qamc', interpolate, face_values, precision=maximum_depth)
    selector_q = (outgoing_quadrant_index[None, :] == jnp.arange(4, dtype=jnp.int32)[:, None]).astype(jnp.float32)
    return lax.optimization_barrier(jnp.sum(candidates * selector_q[:, None, None, :], axis=0)).reshape(80, slot_count)

def least_squares(beta_norm, columns):
    steps_count = len(columns)
    zero_value = jnp.zeros((), jnp.float32)
    target = [beta_norm] + [zero_value] * steps_count
    rotations = []
    upper_rows = []
    for table_slot_index in range(steps_count):
        column = list(columns[table_slot_index])
        for i in range(len(rotations)):
            cos_value, sine_value = rotations[i]
            first_new = cos_value * column[i] + sine_value * column[i + 1]
            second = cos_value * column[i + 1] - sine_value * column[i]
            column[i] = first_new
            column[i + 1] = second
        radius = jnp.sqrt(column[table_slot_index] * column[table_slot_index] + column[table_slot_index + 1] * column[table_slot_index + 1])
        cos_value = column[table_slot_index] / radius
        sine_value = column[table_slot_index + 1] / radius
        column[table_slot_index] = radius
        rotations.append((cos_value, sine_value))
        target[table_slot_index + 1] = -sine_value * target[table_slot_index]
        target[table_slot_index] = cos_value * target[table_slot_index]
        upper_rows.append(column[:table_slot_index + 1])
    coeffs = [zero_value] * steps_count
    for table_slot_index in reversed(range(steps_count)):
        running = target[table_slot_index]
        for k in range(table_slot_index + 1, steps_count):
            running = running - upper_rows[k][table_slot_index] * coeffs[k]
        coeffs[table_slot_index] = running / upper_rows[table_slot_index][table_slot_index]
    return coeffs

def reference(system_source_term, mass_plus_source, lifted_upwind_coupling, frozen_direction_derivative, first_solve_matrix, final_solve_matrix, middle_cell_matrices, adjacent_table_slots, plane_outgoing_cells, band_outgoing_cells, small_side_table_slot, proprietor_mortar_index, outgoing_quadrant_index, incoming_mortar_index, incoming_quadrant_index, coarse_mortar_table_slot):
    derivative, interpolate, projection = gll_tables()
    devices = N_GX * N_YZ
    slot_count = N_YZ * CAP

    def split_devices(array):
        return array.reshape(array.shape[0], devices, ELEM_DEV).transpose(1, 0, 2)

    def join_devices(array):
        return array.transpose(1, 0, 2).reshape(array.shape[1], devices * ELEM_DEV)
    diag_dev = split_devices(mass_plus_source)
    coef_dev = split_devices(lifted_upwind_coupling)
    flux_dev = split_devices(frozen_direction_derivative)
    near_index = split_devices(adjacent_table_slots).reshape(devices, 6 * ELEM_DEV)

    def pick_pairs(face_table, chosen, first_face):
        return jnp.stack([face_table[:, first_face * ELEM_DEV + chosen[0]], face_table[:, (first_face + 1) * ELEM_DEV + chosen[1]]])

    def take_columns(face_table, column_index):
        return jnp.take(face_table, column_index, axis=1, mode='fill', fill_value=0.0)

    def operator_action(argument_array):
        fields = split_devices(argument_array)
        own_faces = jax.vmap(own_traces)(fields)
        slab_send = jax.vmap(lambda a, b: pick_pairs(a, b, 0))(own_faces, plane_outgoing_cells)
        side_send = jax.vmap(lambda a, b: pick_pairs(a, b, 2))(own_faces, band_outgoing_cells)
        slab_grid = slab_send.reshape(N_GX, N_YZ, 2, 80, HALO_SLOTS)
        side_grid = side_send.reshape(N_GX, N_YZ, 2, 80, HALO_SLOTS)
        blank = jnp.zeros((1, N_YZ, 80, HALO_SLOTS), jnp.float32)
        slab_lower = jnp.concatenate([blank, slab_grid[:-1, :, 1]], axis=0).reshape(devices, 80, HALO_SLOTS)
        slab_upper = jnp.concatenate([slab_grid[1:, :, 0], blank], axis=0).reshape(devices, 80, HALO_SLOTS)
        side_lower = jnp.roll(side_grid[:, :, 1], 1, axis=1).reshape(devices, 80, HALO_SLOTS)
        side_upper = jnp.roll(side_grid[:, :, 0], -1, axis=1).reshape(devices, 80, HALO_SLOTS)
        fine_send = jax.vmap(take_columns)(own_faces, small_side_table_slot)
        fine_recv = fine_send.reshape(N_GX, N_YZ, 80, N_YZ, CAP).transpose(0, 3, 2, 1, 4).reshape(devices, 80, slot_count)
        hang_sum = jax.vmap(lambda a, b, c: mortar_sums(a, b, c, projection, HANG))(fine_recv, incoming_mortar_index, incoming_quadrant_index)
        coarse = jax.vmap(lambda a, b: jnp.take(a, b, axis=1))(own_faces, coarse_mortar_table_slot)
        all_coarse = coarse.reshape(N_GX, N_YZ, 80, HANG).transpose(0, 2, 1, 3).reshape(N_GX, 80, N_YZ * HANG)
        owner_of_slot = jnp.arange(slot_count, dtype=jnp.int32) // CAP
        column_index = jnp.where(proprietor_mortar_index < HANG, owner_of_slot[None, :] * HANG + proprietor_mortar_index, N_YZ * HANG)
        column_index = column_index.reshape(N_GX, N_YZ, slot_count)
        coarse_cols = jax.vmap(lambda a, b: jax.vmap(lambda c: take_columns(a, c))(b))(all_coarse, column_index)
        coarse_cols = coarse_cols.reshape(devices, 80, slot_count)
        replies = jax.vmap(lambda a, b: fine_replies(a, b, interpolate))(coarse_cols, outgoing_quadrant_index)
        trace_table = jnp.concatenate([own_faces, slab_lower, slab_upper, side_lower, side_upper, hang_sum, replies], axis=2)
        near_faces = jax.vmap(take_columns)(trace_table, near_index)
        result = jax.vmap(lambda a, b, c, d, e, f: jacobian(a, b, c, d, e, f, derivative))(fields, own_faces, near_faces, diag_dev, coef_dev, flux_dev)
        return join_devices(result)
    defect_array = solve_cell_system(system_source_term, first_solve_matrix, final_solve_matrix, middle_cell_matrices)
    beta_norm = jnp.sqrt(jnp.sum(defect_array * defect_array) + epsilon)
    arnoldi_directions = [defect_array / beta_norm]
    columns = []
    for table_slot_index in range(ITERS):
        scratch_storage = solve_cell_system(operator_action(arnoldi_directions[table_slot_index]), first_solve_matrix, final_solve_matrix, middle_cell_matrices)
        column = []
        for i in range(table_slot_index + 1):
            coefficient = jnp.sum(scratch_storage * arnoldi_directions[i])
            scratch_storage = scratch_storage - coefficient * arnoldi_directions[i]
            column.append(coefficient)
        new_norm = jnp.sqrt(jnp.sum(scratch_storage * scratch_storage) + epsilon)
        column.append(new_norm)
        columns.append(column)
        arnoldi_directions.append(scratch_storage / new_norm)
    coeffs = least_squares(beta_norm, columns)
    newton_update = coeffs[0] * arnoldi_directions[0]
    for table_slot_index in range(1, ITERS):
        newton_update = newton_update + coeffs[table_slot_index] * arnoldi_directions[table_slot_index]
    return newton_update
```

```python
import functools

import jax
import jax.numpy as jnp
import numpy as np
from jax import lax
from jax.experimental import pallas as pl
from jax.experimental.pallas import tpu as pltpu
from jax.sharding import PartitionSpec as P

EPS = 1e-06
NODES = 4
VARS = 5
TILE = VARS * NODES * NODES
DOFS = TILE * NODES
FACES = 6
HALF = 32
K2_SCALE = 2.0**-20
F32 = jnp.float32
BF16 = jnp.bfloat16


def gll_tables():
    root = 1.0 / np.sqrt(5.0)
    points = np.array([-1.0, -root, root, 1.0])
    weights = np.array([1.0, 5.0, 5.0, 1.0]) / 6.0

    def lagrange(at):
        values = np.ones((len(at), 4))
        for j in range(4):
            for m in range(4):
                if m != j:
                    values[:, j] = values[:, j] * (at - points[m]) / (points[j] - points[m])
        return values

    derivative = np.zeros((4, 4))
    for i in range(4):
        for j in range(4):
            total = 0.0
            for m in range(4):
                if m != j:
                    term = 1.0 / (points[j] - points[m])
                    for n in range(4):
                        if n != j and n != m:
                            term = term * (points[i] - points[n]) / (points[j] - points[n])
                    total = total + term
            derivative[i, j] = total
    halves = [lagrange((points - 1.0) / 2.0), lagrange((points + 1.0) / 2.0)]
    projections = [0.5 * (1.0 / weights)[:, None] * h.T * weights[None, :] for h in halves]
    interpolate = [np.kron(halves[q // 2], halves[q % 2]) for q in range(4)]
    project = [np.kron(projections[q // 2], projections[q % 2]) for q in range(4)]
    return derivative, interpolate, project


def pieces(matrix):
    value = np.asarray(matrix, np.float32)
    high = value.astype(jnp.bfloat16)
    low = (value - high.astype(np.float32)).astype(jnp.bfloat16)
    return high, low


def constant_matrices():
    derivative, interpolate, project = gll_tables()
    eye_vars = np.eye(VARS)
    blocks = [np.kron(eye_vars, m) for m in project + interpolate] + [np.eye(TILE)]
    tiles = np.concatenate(pieces(np.concatenate(blocks, axis=1)), axis=0)
    eye = np.eye(4)
    volume = np.concatenate(
        [
            np.kron(derivative, np.kron(eye, eye)),
            np.kron(eye, np.kron(derivative, eye)),
            np.kron(eye, np.kron(eye, derivative)),
        ],
        axis=1,
    )
    volume = np.concatenate(pieces(volume), axis=0)
    return jnp.asarray(tiles), jnp.asarray(volume)


def split(x):
    high = x.astype(BF16)
    low = (x - high.astype(F32)).astype(BF16)
    return high, low


def mm(a, b):
    return jnp.dot(a, b, preferred_element_type=F32)


def mm3(a_high, a_low, b):
    columns = b.shape[1]
    b_high, b_low = split(b)
    first = mm(a_high, jnp.concatenate([b_high, b_low], axis=1))
    return first[:, :columns] + (first[:, columns:] + mm(a_low, b_high))


def solve_cells(x, first_ref, final_ref, mid_ref):
    inner = mm3(first_ref[0], first_ref[1], x)
    return mm3(final_ref[0], final_ref[1], mid_ref[...] * inner)


def face_rows(ref, face):
    end = NODES - 1 if face % 2 else 0
    if face // 2 == 0:
        return jnp.concatenate(
            [ref[pl.ds(a * 64 + end * 16, 16), :] for a in range(VARS)], axis=0
        )
    if face // 2 == 1:
        return jnp.concatenate(
            [ref[pl.ds(g * 16 + end * 4, 4), :] for g in range(VARS * 4)], axis=0
        )
    return ref[pl.ds(end, TILE, stride=4), :]


def add_to_face(ref, face, value):
    end = NODES - 1 if face % 2 else 0
    if face // 2 == 0:
        for a in range(VARS):
            ref[pl.ds(a * 64 + end * 16, 16), :] += value[a * 16 : a * 16 + 16]
    elif face // 2 == 1:
        for g in range(VARS * 4):
            ref[pl.ds(g * 16 + end * 4, 4), :] += value[g * 4 : g * 4 + 4]
    else:
        ref[pl.ds(end, TILE, stride=4), :] += value


def all_traces(ref):
    return jnp.concatenate([face_rows(ref, f) for f in range(FACES)], axis=1)


def two_pieces(x):
    high, low = split(x)
    return jnp.concatenate([high, low], axis=0)


def one_hot(condition):
    return jnp.where(condition, 1.0, 0.0).astype(BF16)


def lane_row(length):
    return lax.broadcasted_iota(jnp.int32, (1, length), 1)


def pack_send(field_ref, send_hot_ref, codes, tiles_ref, send_ref, slab_ref):
    groups = send_ref.shape[0]
    lanes = groups * 2 * HALF
    gathered = mm(two_pieces(all_traces(field_ref)), send_hot_ref[...])
    high, low = gathered[:TILE], gathered[TILE:]
    slab_ref[...] = high[:, lanes:] + low[:, lanes:]
    high, low = high[:, :lanes].astype(BF16), low[:, :lanes].astype(BF16)
    masks = [one_hot(codes == q) for q in range(9)]
    high_stack = jnp.concatenate([high * m for m in masks], axis=0)
    low_stack = jnp.concatenate([low * m for m in masks], axis=0)
    result = mm(tiles_ref[...], high_stack)
    result = result[:TILE] + (result[TILE:] + mm(tiles_ref[:TILE], low_stack))
    left = lane_row(128) < 2 * HALF
    middle = TILE // 2
    for pair in range(groups // 2):
        block = result[:, pair * 128 : pair * 128 + 128]
        top, bottom = block[:middle], block[middle:]
        send_ref[2 * pair] = jnp.where(left, top, pltpu.roll(bottom, 64, 1))
        send_ref[2 * pair + 1] = jnp.where(left, pltpu.roll(top, 64, 1), bottom)


def unpack_received(recv_ref):
    left = lane_row(128) < 2 * HALF
    blocks = []
    for pair in range(recv_ref.shape[0] // 2):
        even, odd = recv_ref[2 * pair], recv_ref[2 * pair + 1]
        top = jnp.where(left, even, pltpu.roll(odd, 64, 1))
        bottom = jnp.where(left, pltpu.roll(even, 64, 1), odd)
        blocks.append(jnp.concatenate([top, bottom], axis=0))
    return jnp.concatenate(blocks, axis=1)


def place_lanes(rows, groups, cap):
    lane = lane_row(groups * 2 * HALF)
    within = lane % HALF
    target = jnp.where(within < cap, (lane // (2 * HALF)) * cap + within, -1)
    slots = lax.broadcasted_iota(jnp.int32, (rows.shape[1], lane.shape[1]), 0)
    return mm(rows, one_hot(slots == target))


def index_tables(
    place, devices, cap, halo, hang, elements, small, outq, inc, inq, coarse, band, plane
):
    gx_index, gx_size, yz_index, groups = devices
    traces = FACES * elements
    as_f = lambda x: x.astype(F32)
    coarse_hot = one_hot(
        lax.broadcasted_iota(jnp.int32, (hang, inc.shape[1]), 0) == inc
    )
    high, low = coarse // 8, coarse % 8
    pad = jnp.zeros((6, hang), F32)
    pick = mm(jnp.concatenate([as_f(high), as_f(low), pad], axis=0).astype(BF16), coarse_hot)
    rows = jnp.concatenate(
        [
            as_f(small // 8),
            as_f(small % 8),
            jnp.where(inc < hang, pick[0:1], float(traces // 8)),
            jnp.where(inc < hang, pick[1:2], 0.0),
            as_f(outq),
            as_f(inq),
            as_f(inc),
            jnp.zeros_like(pick[0:1]),
        ],
        axis=0,
    ).astype(BF16)
    placed = place_lanes(rows, groups, cap).astype(jnp.int32)
    lane = lane_row(groups * 2 * HALF)
    group, within, second = lane // (2 * HALF), lane % HALF, (lane // HALF) % 2
    is_slot = within < cap
    step = halo // 2
    side = (within >= cap) & (within < cap + step)
    position = within - cap + step * second
    up = lax.rem(yz_index + 1, groups)
    down = lax.rem(yz_index + groups - 1, groups)
    lower_columns = jnp.zeros_like(lane) + traces
    upper_columns = lower_columns
    for j in range(halo):
        lower_columns = jnp.where(position == j, 2 * elements + band[0, 0, j], lower_columns)
        upper_columns = jnp.where(position == j, 3 * elements + band[0, 1, j], upper_columns)
    side_send = jnp.where(
        group == up, upper_columns, jnp.where(group == down, lower_columns, traces)
    )
    fine_id = placed[0:1] * 8 + placed[1:2]
    coarse_id = placed[2:3] * 8 + placed[3:4]
    slot_id = jnp.where(second == 0, fine_id, coarse_id)
    send_id = jnp.where(is_slot, slot_id, jnp.where(side, side_send, traces))
    codes = jnp.where(
        is_slot, jnp.where(second == 0, placed[4:5], 4 + placed[5:6]), 8
    )
    slab_lane = lane_row(128)
    slab_id = jnp.zeros_like(slab_lane) + traces
    for j in range(halo):
        slab_id = jnp.where(slab_lane == j, plane[0, 0, j], slab_id)
        slab_id = jnp.where(slab_lane == halo + j, elements + plane[0, 1, j], slab_id)
    send_id = jnp.concatenate([send_id, slab_id], axis=1)

    first_hang = traces + 4 * halo
    side_recv = jnp.where(
        group == down,
        traces + 2 * halo + position,
        jnp.where(group == up, traces + 3 * halo + position, -1),
    )
    mortar = placed[6:7]
    fine_recv = jnp.where(mortar < hang, first_hang + mortar, -1)
    reply_recv = first_hang + hang + group * cap + within
    recv_id = jnp.where(
        is_slot, jnp.where(second == 0, fine_recv, reply_recv), jnp.where(side, side_recv, -1)
    )
    from_upper = (slab_lane < halo) & (gx_index < gx_size - 1)
    from_lower = (slab_lane >= halo) & (slab_lane < 2 * halo) & (gx_index > 0)
    slab_recv = jnp.where(
        from_upper,
        traces + halo + slab_lane,
        jnp.where(from_lower, traces + slab_lane - halo, -1),
    )
    recv_id = jnp.concatenate([recv_id, slab_recv], axis=1)
    return send_id, codes, recv_id


def start_kernel(
    gx_size,
    source_ref,
    first_ref,
    final_ref,
    mid_ref,
    small_ref,
    outq_ref,
    inc_ref,
    inq_ref,
    coarse_ref,
    band_ref,
    plane_ref,
    where_ref,
    tiles_ref,
    field_ref,
    send_ref,
    slab_ref,
    send_hot_ref,
    codes_ref,
    recv_id_ref,
    first_out_ref,
    final_out_ref,
):
    elements = source_ref.shape[1]
    groups = send_ref.shape[0]
    for ref, out in ((first_ref, first_out_ref), (final_ref, final_out_ref)):
        out[0], out[1] = split(ref[...])
    field_ref[...] = solve_cells(source_ref[...], first_out_ref, final_out_ref, mid_ref)
    send_id, codes, recv_id = index_tables(
        None,
        (where_ref[0], gx_size, where_ref[1], groups),
        small_ref.shape[1] // groups,
        band_ref.shape[2],
        coarse_ref.shape[1],
        elements,
        small_ref[...],
        outq_ref[...],
        inc_ref[...],
        inq_ref[...],
        coarse_ref[...],
        band_ref,
        plane_ref,
    )
    columns = lax.broadcasted_iota(jnp.int32, (FACES * elements, send_id.shape[1]), 0)
    send_hot_ref[...] = one_hot(columns == send_id)
    codes_ref[...] = jnp.broadcast_to(codes, codes_ref.shape)
    recv_id_ref[...] = jnp.broadcast_to(recv_id, recv_id_ref.shape)
    pack_send(field_ref, send_hot_ref, codes, tiles_ref, send_ref, slab_ref)


def local_part(
    field_ref, mass_ref, coupling_ref, flux_ref, adjacent_ref, volume_ref, local_ref
):
    elements = field_ref.shape[1]
    traces = all_traces(field_ref)
    columns = lax.broadcasted_iota(jnp.int32, (FACES * elements, elements), 0)
    stacked = two_pieces(traces)
    parts = []
    for a in range(VARS):
        flux = []
        for d in range(3):
            total = None
            for b in range(VARS):
                row = d * 25 + a * VARS + b
                term = flux_ref[row : row + 1, :] * field_ref[b * 64 : b * 64 + 64, :]
                total = term if total is None else total + term
            flux.append(total)
        parts.append(jnp.concatenate(flux, axis=0))
    derived = mm3(volume_ref[:64], volume_ref[64:], jnp.concatenate(parts, axis=1))
    for a in range(VARS):
        rows = slice(a * 64, a * 64 + 64)
        local_ref[rows, :] = (
            mass_ref[rows, :] * field_ref[rows, :]
            + derived[:, a * elements : (a + 1) * elements]
        )
    for f in range(FACES):
        near = mm(stacked, one_hot(columns == adjacent_ref[f : f + 1, :]))
        near = near[:TILE] + near[TILE:]
        own = traces[:, f * elements : (f + 1) * elements]
        add_to_face(
            local_ref, f, coupling_ref[f * TILE : (f + 1) * TILE, :] * (own - near)
        )


def first_local_kernel(
    field_ref,
    mass_ref,
    coupling_ref,
    flux_ref,
    adjacent_ref,
    volume_ref,
    recv_id_ref,
    local_ref,
    recv_hot_ref,
):
    local_part(field_ref, mass_ref, coupling_ref, flux_ref, adjacent_ref, volume_ref, local_ref)
    elements = field_ref.shape[1]
    ids = jnp.transpose(recv_id_ref[...])[:, 0:1]
    for f in range(FACES):
        recv_hot_ref[:, f * elements : (f + 1) * elements] = one_hot(
            ids == adjacent_ref[f : f + 1, :]
        )


def total_of(x):
    return jnp.sum(jnp.sum(x, axis=0, keepdims=True), axis=1, keepdims=True)


def put(values):
    lane = lane_row(128)
    row = jnp.zeros((1, 128), F32)
    for position, value in values:
        row = jnp.where(lane == position, value, row)
    return row


def second_local_kernel(
    field_ref,
    mass_ref,
    coupling_ref,
    flux_ref,
    adjacent_ref,
    volume_ref,
    start_ref,
    local_ref,
    partial_ref,
):
    local_part(field_ref, mass_ref, coupling_ref, flux_ref, adjacent_ref, volume_ref, local_ref)
    k0, k1 = start_ref[...], field_ref[...]
    partial_ref[...] = put(
        [(0, total_of(k0 * k0)), (1, total_of(k0 * k1)), (2, total_of(k1 * k1))]
    )


def finish_product(
    recv_ref, slab_ref, recv_hot_ref, coupling_ref, local_ref, first_ref, final_ref, mid_ref, work_ref
):
    elements = local_ref.shape[1]
    received = jnp.concatenate([unpack_received(recv_ref), slab_ref[...]], axis=1)
    near = mm(two_pieces(received), recv_hot_ref[...])
    near = near[:TILE] + near[TILE:]
    work_ref[...] = local_ref[...]
    for f in range(FACES):
        add_to_face(
            work_ref,
            f,
            -coupling_ref[f * TILE : (f + 1) * TILE, :] * near[:, f * elements : (f + 1) * elements],
        )
    return solve_cells(work_ref[...], first_ref, final_ref, mid_ref)


def middle_kernel(
    recv_ref,
    slab_in_ref,
    recv_hot_ref,
    coupling_ref,
    local_ref,
    first_ref,
    final_ref,
    mid_ref,
    send_hot_ref,
    codes_ref,
    tiles_ref,
    field_ref,
    send_ref,
    slab_ref,
    work_ref,
):
    field_ref[...] = finish_product(
        recv_ref, slab_in_ref, recv_hot_ref, coupling_ref, local_ref, first_ref, final_ref, mid_ref, work_ref
    )
    pack_send(field_ref, send_hot_ref, codes_ref[0:1, :], tiles_ref, send_ref, slab_ref)


def last_kernel(
    recv_ref,
    slab_in_ref,
    recv_hot_ref,
    coupling_ref,
    local_ref,
    first_ref,
    final_ref,
    mid_ref,
    start_ref,
    field_ref,
    partial_ref,
    out_ref,
    work_ref,
):
    k2 = K2_SCALE * finish_product(
        recv_ref, slab_in_ref, recv_hot_ref, coupling_ref, local_ref, first_ref, final_ref, mid_ref, work_ref
    )
    row = partial_ref[...] + put(
        [
            (3, total_of(k2 * start_ref[...])),
            (4, total_of(k2 * field_ref[...])),
            (5, total_of(k2 * k2)),
        ]
    )
    out_ref[...] = jnp.broadcast_to(row.reshape(1, 1, 128), out_ref.shape)


def combine_kernel(rows_ref, start_ref, field_ref, out_ref):
    totals = jnp.sum(rows_ref[:, 0, :], axis=0, keepdims=True)
    lane = lane_row(128)
    g00, g01, g11, g02, g12, g22 = [
        jnp.sum(jnp.where(lane == i, totals, 0.0), axis=1, keepdims=True) for i in range(6)
    ]
    scale = 1.0 / K2_SCALE
    beta = jnp.sqrt(g00 + EPS)
    n00, n01, n11 = g00 / beta / beta, g01 / beta / beta, g11 / beta / beta
    h00 = n01
    w_sq = jnp.maximum(n11 - 2.0 * h00 * n01 + h00 * h00 * n00, 0.0)
    h10 = jnp.sqrt(w_sq + EPS)
    unit = beta * h10
    s = scale / unit
    t = h00 * K2_SCALE
    x0 = (g02 - t * g01) * s / beta
    x1 = ((g12 - t * g11) * s - h00 * ((g02 - t * g01) * s)) / unit
    xx = (((g22 - t * g12) - t * (g12 - t * g11)) * s) * s
    v01 = (n01 - h00 * n00) / h10
    v11 = w_sq / h10 / h10
    h01 = x0
    h11 = x1 - h01 * v01
    rest = xx - 2.0 * h01 * x0 + h01 * h01 * n00
    rest = rest - 2.0 * h11 * h11 + h11 * h11 * v11
    h21 = jnp.sqrt(jnp.maximum(rest, 0.0) + EPS)
    radius0 = jnp.sqrt(h00 * h00 + h10 * h10)
    c0, s0 = h00 / radius0, h10 / radius0
    target1 = -s0 * beta
    target0 = c0 * beta
    upper = c0 * h01 + s0 * h11
    lower = c0 * h11 - s0 * h01
    radius1 = jnp.sqrt(lower * lower + h21 * h21)
    y1 = (lower / radius1) * target1 / radius1
    y0 = (target0 - upper * y1) / radius0
    along1 = y1 / unit
    along0 = y0 / beta - along1 * h00
    out_ref[...] = along0 * start_ref[...] + along1 * field_ref[...]


def vmem(count):
    return [pl.BlockSpec(memory_space=pltpu.VMEM)] * count


def call(kernel, outs, args, smem=(), scratch=(), flops=0):
    specs = [
        pl.BlockSpec(memory_space=pltpu.SMEM if i in smem else pltpu.VMEM)
        for i in range(len(args))
    ]
    return pl.pallas_call(
        kernel,
        out_shape=outs,
        in_specs=specs,
        out_specs=jax.tree.map(lambda _: pl.BlockSpec(memory_space=pltpu.VMEM), outs),
        scratch_shapes=list(scratch),
        cost_estimate=pl.CostEstimate(
            flops=flops, bytes_accessed=sum(a.size * a.dtype.itemsize for a in args), transcendentals=0
        ),
        compiler_params=pltpu.CompilerParams(vmem_limit_bytes=48 * 2**20),
    )(*args)


def on_device(
    source,
    mass,
    coupling,
    flux,
    first,
    final,
    mid,
    adjacent,
    plane,
    band,
    small,
    proprietor,
    outq,
    inc,
    inq,
    coarse,
):
    del proprietor
    tiles, volume = constant_matrices()
    gx_size, groups = lax.axis_size("gx"), lax.axis_size("yz")
    elements = source.shape[1]
    traces = FACES * elements
    lanes = groups * 2 * HALF
    struct = jax.ShapeDtypeStruct
    field = struct((DOFS, elements), F32)
    send = struct((groups, TILE // 2, 128), F32)
    slab = struct((TILE, 128), F32)
    where = jnp.stack([lax.axis_index("gx"), lax.axis_index("yz")]).astype(jnp.int32)

    k0, send0, slab0, send_hot, codes, recv_id, first2, final2 = call(
        functools.partial(start_kernel, gx_size),
        (
            field,
            send,
            slab,
            struct((traces, lanes + 128), BF16),
            struct((8, lanes), jnp.int32),
            struct((8, lanes + 128), jnp.int32),
            struct((2, DOFS, DOFS), BF16),
            struct((2, DOFS, DOFS), BF16),
        ),
        (source, first, final, mid, small, outq, inc, inq, coarse, band, plane, where, tiles),
        smem=(9, 10, 11),
        flops=10**9,
    )

    up = [(i, i + 1) for i in range(gx_size - 1)]
    down = [(j, i) for i, j in up]

    def exchange(send, slab):
        if gx_size == 2:
            slab = lax.ppermute(slab, "gx", up + down)
        else:
            halo = plane.shape[2]
            lower = lax.ppermute(slab, "gx", up)
            upper = lax.ppermute(slab, "gx", down)
            slab = jnp.where(lane_row(128) < halo, upper, lower)
        return lax.all_to_all(send, "yz", 0, 0, tiled=True), slab

    recv0, slab0 = exchange(send0, slab0)
    local0, recv_hot = call(
        first_local_kernel,
        (field, struct((lanes + 128, traces), BF16)),
        (k0, mass, coupling, flux, adjacent, volume, recv_id),
        flops=10**9,
    )
    work = pltpu.VMEM((DOFS, elements), F32)
    k1, send1, slab1 = call(
        middle_kernel,
        (field, send, slab),
        (recv0, slab0, recv_hot, coupling, local0, first2, final2, mid, send_hot, codes, tiles),
        scratch=[work],
        flops=10**9,
    )
    recv1, slab1 = exchange(send1, slab1)
    local1, partial = call(
        second_local_kernel,
        (field, struct((1, 128), F32)),
        (k1, mass, coupling, flux, adjacent, volume, k0),
        flops=10**9,
    )
    rows = call(
        last_kernel,
        struct((gx_size * groups, 1, 128), F32),
        (recv1, slab1, recv_hot, coupling, local1, first2, final2, mid, k0, k1, partial),
        scratch=[work],
        flops=10**9,
    )
    rows = lax.all_to_all(rows, ("gx", "yz"), 0, 0, tiled=True)
    return call(combine_kernel, field, (rows, k0, k1), flops=10**6)


def solution(mesh):
    by_column = P(None, ("gx", "yz"))
    by_row = P(("gx", "yz"), None)
    by_plane = P(("gx", "yz"), None, None)
    return jax.shard_map(
        on_device,
        mesh=mesh,
        in_specs=(by_column,) * 4
        + (P(), P())
        + (by_column,) * 2
        + (by_plane,) * 2
        + (by_row,) * 6,
        out_specs=by_column,
        check_vma=False,
    )
```

```python
import functools

import jax
import jax.numpy as jnp
import numpy as np
from jax import lax
from jax.experimental import pallas as pl
from jax.experimental.pallas import tpu as pltpu
from jax.sharding import PartitionSpec as P

EPS = 1e-06
NODES = 4
VARS = 5
TILE = VARS * NODES * NODES
DOFS = TILE * NODES
FACES = 6
HALF = 32
K2_SCALE = 2.0**-20
F32 = jnp.float32
BF16 = jnp.bfloat16


def gll_tables():
    root = 1.0 / np.sqrt(5.0)
    points = np.array([-1.0, -root, root, 1.0])
    weights = np.array([1.0, 5.0, 5.0, 1.0]) / 6.0

    def lagrange(at):
        values = np.ones((len(at), 4))
        for j in range(4):
            for m in range(4):
                if m != j:
                    values[:, j] = values[:, j] * (at - points[m]) / (points[j] - points[m])
        return values

    derivative = np.zeros((4, 4))
    for i in range(4):
        for j in range(4):
            total = 0.0
            for m in range(4):
                if m != j:
                    term = 1.0 / (points[j] - points[m])
                    for n in range(4):
                        if n != j and n != m:
                            term = term * (points[i] - points[n]) / (points[j] - points[n])
                    total = total + term
            derivative[i, j] = total
    halves = [lagrange((points - 1.0) / 2.0), lagrange((points + 1.0) / 2.0)]
    projections = [0.5 * (1.0 / weights)[:, None] * h.T * weights[None, :] for h in halves]
    interpolate = [np.kron(halves[q // 2], halves[q % 2]) for q in range(4)]
    project = [np.kron(projections[q // 2], projections[q % 2]) for q in range(4)]
    return derivative, interpolate, project


def pieces(matrix):
    value = np.asarray(matrix, np.float32)
    high = value.astype(jnp.bfloat16)
    low = (value - high.astype(np.float32)).astype(jnp.bfloat16)
    return high, low


def constant_matrices():
    derivative, interpolate, project = gll_tables()
    eye_vars = np.eye(VARS)
    blocks = [np.kron(eye_vars, m) for m in project + interpolate] + [np.eye(TILE)]
    tiles = np.concatenate(pieces(np.concatenate(blocks, axis=1)), axis=0)
    eye = np.eye(4)
    volume = np.concatenate(
        [
            np.kron(derivative, np.kron(eye, eye)),
            np.kron(eye, np.kron(derivative, eye)),
            np.kron(eye, np.kron(eye, derivative)),
        ],
        axis=1,
    )
    volume = np.concatenate(pieces(volume), axis=0)
    return jnp.asarray(tiles), jnp.asarray(volume)


def split(x):
    high = x.astype(BF16)
    low = (x - high.astype(F32)).astype(BF16)
    return high, low


def mm(a, b):
    return jnp.dot(a, b, preferred_element_type=F32)


def mm3(a_high, a_low, b):
    columns = b.shape[1]
    b_high, b_low = split(b)
    first = mm(a_high, jnp.concatenate([b_high, b_low], axis=1))
    return first[:, :columns] + (first[:, columns:] + mm(a_low, b_high))


def solve_cells(x, first_ref, final_ref, mid_ref):
    inner = mm3(first_ref[0], first_ref[1], x)
    return mm3(final_ref[0], final_ref[1], mid_ref[...] * inner)


def face_rows(ref, face):
    end = NODES - 1 if face % 2 else 0
    if face // 2 == 0:
        return jnp.concatenate(
            [ref[pl.ds(a * 64 + end * 16, 16), :] for a in range(VARS)], axis=0
        )
    if face // 2 == 1:
        return jnp.concatenate(
            [ref[pl.ds(g * 16 + end * 4, 4), :] for g in range(VARS * 4)], axis=0
        )
    return ref[pl.ds(end, TILE, stride=4), :]


def add_to_face(ref, face, value):
    end = NODES - 1 if face % 2 else 0
    if face // 2 == 0:
        for a in range(VARS):
            ref[pl.ds(a * 64 + end * 16, 16), :] += value[a * 16 : a * 16 + 16]
    elif face // 2 == 1:
        for g in range(VARS * 4):
            ref[pl.ds(g * 16 + end * 4, 4), :] += value[g * 4 : g * 4 + 4]
    else:
        ref[pl.ds(end, TILE, stride=4), :] += value


def all_traces(ref):
    return jnp.concatenate([face_rows(ref, f) for f in range(FACES)], axis=1)


def two_pieces(x):
    high, low = split(x)
    return jnp.concatenate([high, low], axis=0)


def one_hot(condition):
    return jnp.where(condition, 1.0, 0.0).astype(BF16)


def lane_row(length):
    return lax.broadcasted_iota(jnp.int32, (1, length), 1)


def pack_send(field_ref, send_hot_ref, codes, tiles_ref, send_ref, slab_ref):
    groups = send_ref.shape[0]
    lanes = groups * 2 * HALF
    gathered = mm(two_pieces(all_traces(field_ref)), send_hot_ref[...])
    high, low = gathered[:TILE], gathered[TILE:]
    slab_ref[...] = high[:, lanes:] + low[:, lanes:]
    high, low = high[:, :lanes].astype(BF16), low[:, :lanes].astype(BF16)
    masks = [one_hot(codes == q) for q in range(9)]
    high_stack = jnp.concatenate([high * m for m in masks], axis=0)
    low_stack = jnp.concatenate([low * m for m in masks], axis=0)
    result = mm(tiles_ref[...], high_stack)
    result = result[:TILE] + (result[TILE:] + mm(tiles_ref[:TILE], low_stack))
    left = lane_row(128) < 2 * HALF
    middle = TILE // 2
    for pair in range(groups // 2):
        block = result[:, pair * 128 : pair * 128 + 128]
        top, bottom = block[:middle], block[middle:]
        send_ref[2 * pair] = jnp.where(left, top, pltpu.roll(bottom, 64, 1))
        send_ref[2 * pair + 1] = jnp.where(left, pltpu.roll(top, 64, 1), bottom)


def unpack_received(recv_ref):
    left = lane_row(128) < 2 * HALF
    blocks = []
    for pair in range(recv_ref.shape[0] // 2):
        even, odd = recv_ref[2 * pair], recv_ref[2 * pair + 1]
        top = jnp.where(left, even, pltpu.roll(odd, 64, 1))
        bottom = jnp.where(left, pltpu.roll(even, 64, 1), odd)
        blocks.append(jnp.concatenate([top, bottom], axis=0))
    return jnp.concatenate(blocks, axis=1)


def place_lanes(rows, groups, cap):
    lane = lane_row(groups * 2 * HALF)
    within = lane % HALF
    target = jnp.where(within < cap, (lane // (2 * HALF)) * cap + within, -1)
    slots = lax.broadcasted_iota(jnp.int32, (rows.shape[1], lane.shape[1]), 0)
    return mm(rows, one_hot(slots == target))


def index_tables(cap, small, outq, inc, inq, coarse, band, plane, elements, sizes):
    gx_size, groups = sizes
    gx_index, yz_index = lax.axis_index("gx"), lax.axis_index("yz")
    hang, halo = coarse.shape[1], band.shape[1]
    traces = FACES * elements
    as_f = lambda x: x.astype(F32)
    coarse_hot = one_hot(
        lax.broadcasted_iota(jnp.int32, (hang, inc.shape[1]), 0) == inc
    )
    pad = jnp.zeros((6, hang), F32)
    pick = mm(
        jnp.concatenate([as_f(coarse // 8), as_f(coarse % 8), pad], axis=0).astype(BF16),
        coarse_hot,
    )
    rows = jnp.concatenate(
        [
            as_f(small // 8),
            as_f(small % 8),
            jnp.where(inc < hang, pick[0:1], float(traces // 8)),
            jnp.where(inc < hang, pick[1:2], 0.0),
            as_f(outq),
            as_f(inq),
            as_f(inc),
            jnp.zeros_like(pick[0:1]),
        ],
        axis=0,
    ).astype(BF16)
    placed = place_lanes(rows, groups, cap).astype(jnp.int32)
    lane = lane_row(groups * 2 * HALF)
    group, within, second = lane // (2 * HALF), lane % HALF, (lane // HALF) % 2
    is_slot = within < cap
    step = halo // 2
    side = (within >= cap) & (within < cap + step)
    position = within - cap + step * second
    up = lax.rem(yz_index + 1, groups)
    down = lax.rem(yz_index + groups - 1, groups)
    slab_lane = lane_row(128)
    target = jnp.concatenate(
        [
            jnp.where(side, position, -1),
            jnp.where(slab_lane < 2 * halo, slab_lane % halo, -1),
        ],
        axis=1,
    )
    slots = lax.broadcasted_iota(jnp.int32, (halo, target.shape[1]), 0)
    halo_rows = jnp.concatenate([as_f(band), as_f(plane), jnp.zeros((4, halo), F32)], axis=0)
    edge = mm(halo_rows.astype(BF16), one_hot(slots == target)).astype(jnp.int32)
    lanes = lane.shape[1]
    side_send = jnp.where(
        group == up,
        3 * elements + edge[1:2, :lanes],
        jnp.where(group == down, 2 * elements + edge[0:1, :lanes], traces),
    )
    slot_id = jnp.where(
        second == 0, placed[0:1] * 8 + placed[1:2], placed[2:3] * 8 + placed[3:4]
    )
    send_id = jnp.where(is_slot, slot_id, jnp.where(side, side_send, traces))
    codes = jnp.where(
        is_slot, jnp.where(second == 0, placed[4:5], 4 + placed[5:6]), 8
    )
    slab_id = jnp.where(
        slab_lane < halo,
        edge[2:3, lanes:],
        jnp.where(slab_lane < 2 * halo, elements + edge[3:4, lanes:], traces),
    )
    send_id = jnp.concatenate([send_id, slab_id], axis=1)

    first_hang = traces + 4 * halo
    side_recv = jnp.where(
        group == down,
        traces + 2 * halo + position,
        jnp.where(group == up, traces + 3 * halo + position, -1),
    )
    mortar = placed[6:7]
    fine_recv = jnp.where(mortar < hang, first_hang + mortar, -1)
    reply_recv = first_hang + hang + group * cap + within
    recv_id = jnp.where(
        is_slot, jnp.where(second == 0, fine_recv, reply_recv), jnp.where(side, side_recv, -1)
    )
    from_upper = (slab_lane < halo) & (gx_index < gx_size - 1)
    from_lower = (slab_lane >= halo) & (slab_lane < 2 * halo) & (gx_index > 0)
    slab_recv = jnp.where(
        from_upper,
        traces + halo + slab_lane,
        jnp.where(from_lower, traces + slab_lane - halo, -1),
    )
    recv_id = jnp.concatenate([recv_id, slab_recv], axis=1)
    return send_id, codes, recv_id


class Loads:
    def __init__(self, sources, buffers, sems):
        self.buffers = list(buffers)
        self.copies = [
            pltpu.make_async_copy(s, b, sems.at[i])
            for i, (s, b) in enumerate(zip(sources, buffers))
        ]
        for copy in self.copies:
            copy.start()

    def __getitem__(self, i):
        if self.copies[i] is not None:
            self.copies[i].wait()
            self.copies[i] = None
        return self.buffers[i]


def start_kernel(sizes, *refs):
    loads = Loads(refs[:12], refs[20:32], refs[40])
    tables = [loads[i] for i in range(7)]
    outs, stage, sems = refs[12:20], refs[32:40], refs[41]
    field, send, slab, send_hot, codes_ref, recv_id_ref, first2, final2 = stage
    copies = [pltpu.make_async_copy(s, o, sems.at[i]) for i, (s, o) in enumerate(zip(stage, outs))]
    elements = field.shape[1]
    groups = send.shape[0]
    small, outq, inc, inq, coarse, band, plane = tables
    send_id, codes, recv_id = index_tables(
        small.shape[1] // groups,
        small[...],
        outq[...],
        inc[...],
        inq[...],
        coarse[...],
        band[0],
        plane[0],
        elements,
        sizes,
    )
    codes_ref[...] = jnp.broadcast_to(codes, codes_ref.shape)
    copies[4].start()
    recv_id_ref[...] = jnp.broadcast_to(recv_id, recv_id_ref.shape)
    copies[5].start()
    columns = lax.broadcasted_iota(jnp.int32, (FACES * elements, send_id.shape[1]), 0)
    send_hot[...] = one_hot(columns == send_id)
    copies[3].start()
    first2[0], first2[1] = split(loads[7][...])
    copies[6].start()
    final2[0], final2[1] = split(loads[8][...])
    copies[7].start()
    field[...] = solve_cells(loads[9][...], first2, final2, loads[10])
    copies[0].start()
    pack_send(field, send_hot, codes, loads[11], send, slab)
    copies[1].start()
    copies[2].start()
    for copy in copies:
        copy.wait()


def local_part(
    field_ref, mass_ref, coupling_ref, flux_ref, adjacent_ref, volume_ref, local_ref
):
    elements = field_ref.shape[1]
    traces = all_traces(field_ref)
    columns = lax.broadcasted_iota(jnp.int32, (FACES * elements, elements), 0)
    stacked = two_pieces(traces)
    parts = []
    for a in range(VARS):
        flux = []
        for d in range(3):
            total = None
            for b in range(VARS):
                row = d * 25 + a * VARS + b
                term = flux_ref[row : row + 1, :] * field_ref[b * 64 : b * 64 + 64, :]
                total = term if total is None else total + term
            flux.append(total)
        parts.append(jnp.concatenate(flux, axis=0))
    derived = mm3(volume_ref[:64], volume_ref[64:], jnp.concatenate(parts, axis=1))
    for a in range(VARS):
        rows = slice(a * 64, a * 64 + 64)
        local_ref[rows, :] = (
            mass_ref[rows, :] * field_ref[rows, :]
            + derived[:, a * elements : (a + 1) * elements]
        )
    for f in range(FACES):
        near = mm(stacked, one_hot(columns == adjacent_ref[f : f + 1, :]))
        near = near[:TILE] + near[TILE:]
        own = traces[:, f * elements : (f + 1) * elements]
        add_to_face(
            local_ref, f, coupling_ref[f * TILE : (f + 1) * TILE, :] * (own - near)
        )


def first_local_kernel(*refs):
    loads = Loads(refs[:7], refs[9:16], refs[18])
    (local_out, hot_out), (local, recv_hot), sems = refs[7:9], refs[16:18], refs[19]
    elements = local.shape[1]
    ids = jnp.transpose(loads[0][...])[:, 0:1]
    adjacent = loads[1]
    for f in range(FACES):
        recv_hot[:, f * elements : (f + 1) * elements] = one_hot(ids == adjacent[f : f + 1, :])
    hot_copy = pltpu.make_async_copy(recv_hot, hot_out, sems.at[0])
    hot_copy.start()
    local_part(loads[2], loads[3], loads[4], loads[5], adjacent, loads[6], local)
    copy = pltpu.make_async_copy(local, local_out, sems.at[1])
    copy.start()
    copy.wait()
    hot_copy.wait()


def total_of(x):
    return jnp.sum(jnp.sum(x, axis=0, keepdims=True), axis=1, keepdims=True)


def put(values):
    lane = lane_row(128)
    row = jnp.zeros((1, 128), F32)
    for position, value in values:
        row = jnp.where(lane == position, value, row)
    return row


def second_local_kernel(*refs):
    loads = Loads(refs[:7], refs[9:16], refs[18])
    (local_out, partial_out), (local, partial), sems = refs[7:9], refs[16:18], refs[19]
    adjacent = loads[0]
    local_part(loads[1], loads[2], loads[3], loads[4], adjacent, loads[5], local)
    copy = pltpu.make_async_copy(local, local_out, sems.at[0])
    copy.start()
    k0, k1 = loads[6][...], loads[1][...]
    partial[...] = put(
        [(0, total_of(k0 * k0)), (1, total_of(k0 * k1)), (2, total_of(k1 * k1))]
    )
    row_copy = pltpu.make_async_copy(partial, partial_out, sems.at[1])
    row_copy.start()
    copy.wait()
    row_copy.wait()


def finish_product(recv_ref, slab_ref, loads, work_ref):
    received = jnp.concatenate([unpack_received(recv_ref), slab_ref[...]], axis=1)
    near = mm(two_pieces(received), loads[0][...])
    near = near[:TILE] + near[TILE:]
    coupling, local = loads[1], loads[2]
    elements = local.shape[1]
    work_ref[...] = local[...]
    for f in range(FACES):
        add_to_face(
            work_ref,
            f,
            -coupling[f * TILE : (f + 1) * TILE, :] * near[:, f * elements : (f + 1) * elements],
        )
    inner = mm3(loads[3][0], loads[3][1], work_ref[...])
    return mm3(loads[5][0], loads[5][1], loads[4][...] * inner)


def middle_kernel(*refs):
    recv, slab_in = refs[:2]
    loads = Loads(refs[2:11], refs[14:23], refs[27])
    outs, stage, work, sems = refs[11:14], refs[23:26], refs[26], refs[28]
    copies = [pltpu.make_async_copy(s, o, sems.at[i]) for i, (s, o) in enumerate(zip(stage, outs))]
    field, send, slab = stage
    field[...] = finish_product(recv, slab_in, loads, work)
    copies[0].start()
    pack_send(field, loads[6], loads[7][0:1, :], loads[8], send, slab)
    copies[1].start()
    copies[2].start()
    for copy in copies:
        copy.wait()


def last_kernel(*refs):
    recv, slab_in = refs[:2]
    loads = Loads(refs[2:11], refs[12:21], refs[22])
    out, work = refs[11], refs[21]
    k2 = K2_SCALE * finish_product(recv, slab_in, loads, work)
    row = loads[8][...] + put(
        [
            (3, total_of(k2 * loads[6][...])),
            (4, total_of(k2 * loads[7][...])),
            (5, total_of(k2 * k2)),
        ]
    )
    out[...] = jnp.broadcast_to(row.reshape(1, 1, 128), out.shape)


def combine_kernel(rows_ref, start_ref, field_ref, out_ref, sems):
    del sems
    totals = jnp.sum(rows_ref[:, 0, :], axis=0, keepdims=True)
    lane = lane_row(128)
    g00, g01, g11, g02, g12, g22 = [
        jnp.sum(jnp.where(lane == i, totals, 0.0), axis=1, keepdims=True) for i in range(6)
    ]
    scale = 1.0 / K2_SCALE
    beta = jnp.sqrt(g00 + EPS)
    n00, n01, n11 = g00 / beta / beta, g01 / beta / beta, g11 / beta / beta
    h00 = n01
    w_sq = jnp.maximum(n11 - 2.0 * h00 * n01 + h00 * h00 * n00, 0.0)
    h10 = jnp.sqrt(w_sq + EPS)
    unit = beta * h10
    s = scale / unit
    t = h00 * K2_SCALE
    x0 = (g02 - t * g01) * s / beta
    x1 = ((g12 - t * g11) * s - h00 * ((g02 - t * g01) * s)) / unit
    xx = (((g22 - t * g12) - t * (g12 - t * g11)) * s) * s
    v01 = (n01 - h00 * n00) / h10
    v11 = w_sq / h10 / h10
    h01 = x0
    h11 = x1 - h01 * v01
    rest = xx - 2.0 * h01 * x0 + h01 * h01 * n00
    rest = rest - 2.0 * h11 * h11 + h11 * h11 * v11
    h21 = jnp.sqrt(jnp.maximum(rest, 0.0) + EPS)
    radius0 = jnp.sqrt(h00 * h00 + h10 * h10)
    c0, s0 = h00 / radius0, h10 / radius0
    target1 = -s0 * beta
    target0 = c0 * beta
    upper = c0 * h01 + s0 * h11
    lower = c0 * h11 - s0 * h01
    radius1 = jnp.sqrt(lower * lower + h21 * h21)
    y1 = (lower / radius1) * target1 / radius1
    y0 = (target0 - upper * y1) / radius0
    along1 = y1 / unit
    along0 = y0 / beta - along1 * h00
    out_ref[...] = along0 * start_ref[...] + along1 * field_ref[...]


def call(kernel, outs, args, held=0, staged=True, scratch=()):
    in_vmem, in_place = pl.BlockSpec(memory_space=pltpu.VMEM), pl.BlockSpec(memory_space=pl.ANY)
    moved = args[held:]
    buffers = [pltpu.VMEM(a.shape, a.dtype) for a in moved]
    out_list = jax.tree.leaves(outs)
    if staged:
        buffers += [pltpu.VMEM(o.shape, o.dtype) for o in out_list]
    buffers += list(scratch)
    buffers.append(pltpu.SemaphoreType.DMA((max(len(moved), 1),)))
    if staged:
        buffers.append(pltpu.SemaphoreType.DMA((len(out_list),)))
    return pl.pallas_call(
        kernel,
        out_shape=outs,
        in_specs=[in_vmem] * held + [in_place] * len(moved),
        out_specs=jax.tree.map(lambda _: in_place if staged else in_vmem, outs),
        scratch_shapes=buffers,
        cost_estimate=pl.CostEstimate(
            flops=10**9,
            bytes_accessed=sum(a.size * a.dtype.itemsize for a in args),
            transcendentals=0,
        ),
        compiler_params=pltpu.CompilerParams(vmem_limit_bytes=40 * 2**20),
    )(*args)


def on_device(
    source,
    mass,
    coupling,
    flux,
    first,
    final,
    mid,
    adjacent,
    plane,
    band,
    small,
    proprietor,
    outq,
    inc,
    inq,
    coarse,
):
    del proprietor
    tiles, volume = constant_matrices()
    gx_size, groups = lax.axis_size("gx"), lax.axis_size("yz")
    elements = source.shape[1]
    traces = FACES * elements
    lanes = groups * 2 * HALF
    struct = jax.ShapeDtypeStruct
    field = struct((DOFS, elements), F32)
    send = struct((groups, TILE // 2, 128), F32)
    slab = struct((TILE, 128), F32)

    k0, send0, slab0, send_hot, codes, recv_id, first2, final2 = call(
        functools.partial(start_kernel, (gx_size, groups)),
        (
            field,
            send,
            slab,
            struct((traces, lanes + 128), BF16),
            struct((8, lanes), jnp.int32),
            struct((8, lanes + 128), jnp.int32),
            struct((2, DOFS, DOFS), BF16),
            struct((2, DOFS, DOFS), BF16),
        ),
        (small, outq, inc, inq, coarse, band, plane, first, final, source, mid, tiles),
    )

    up = [(i, i + 1) for i in range(gx_size - 1)]
    down = [(j, i) for i, j in up]

    def exchange(send, slab):
        if gx_size == 2:
            slab = lax.ppermute(slab, "gx", up + down)
        else:
            halo = plane.shape[2]
            lower = lax.ppermute(slab, "gx", up)
            upper = lax.ppermute(slab, "gx", down)
            slab = jnp.where(lane_row(128) < halo, upper, lower)
        return lax.all_to_all(send, "yz", 0, 0, tiled=True), slab

    recv0, slab0 = exchange(send0, slab0)
    local0, recv_hot = call(
        first_local_kernel,
        (field, struct((lanes + 128, traces), BF16)),
        (recv_id, adjacent, k0, mass, coupling, flux, volume),
    )
    work = pltpu.VMEM((DOFS, elements), F32)
    solve_args = (coupling, local0, first2, mid, final2)
    k1, send1, slab1 = call(
        middle_kernel,
        (field, send, slab),
        (recv0, slab0, recv_hot) + solve_args + (send_hot, codes, tiles),
        held=2,
        scratch=[work],
    )
    recv1, slab1 = exchange(send1, slab1)
    local1, partial = call(
        second_local_kernel,
        (field, struct((1, 128), F32)),
        (adjacent, k1, mass, coupling, flux, volume, k0),
    )
    solve_args = (coupling, local1, first2, mid, final2)
    rows = call(
        last_kernel,
        struct((gx_size * groups, 1, 128), F32),
        (recv1, slab1, recv_hot) + solve_args + (k0, k1, partial),
        held=2,
        staged=False,
        scratch=[work],
    )
    rows = lax.all_to_all(rows, ("gx", "yz"), 0, 0, tiled=True)
    return call(combine_kernel, field, (rows, k0, k1), held=3, staged=False)


def solution(mesh):
    by_column = P(None, ("gx", "yz"))
    by_row = P(("gx", "yz"), None)
    by_plane = P(("gx", "yz"), None, None)
    return jax.shard_map(
        on_device,
        mesh=mesh,
        in_specs=(by_column,) * 4
        + (P(), P())
        + (by_column,) * 2
        + (by_plane,) * 2
        + (by_row,) * 6,
        out_specs=by_column,
        check_vma=False,
    )
```

```python
import functools

import jax
import jax.numpy as jnp
import numpy as np
from jax import lax
from jax.experimental import pallas as pl
from jax.experimental.pallas import tpu as pltpu
from jax.sharding import PartitionSpec as P

EPS = 1e-06
NODES = 4
VARS = 5
TILE = VARS * NODES * NODES
DOFS = TILE * NODES
FACES = 6
HALF = 32
K2_SCALE = 2.0**-20
F32 = jnp.float32
BF16 = jnp.bfloat16


def gll_tables():
    root = 1.0 / np.sqrt(5.0)
    points = np.array([-1.0, -root, root, 1.0])
    weights = np.array([1.0, 5.0, 5.0, 1.0]) / 6.0

    def lagrange(at):
        values = np.ones((len(at), 4))
        for j in range(4):
            for m in range(4):
                if m != j:
                    values[:, j] = values[:, j] * (at - points[m]) / (points[j] - points[m])
        return values

    derivative = np.zeros((4, 4))
    for i in range(4):
        for j in range(4):
            total = 0.0
            for m in range(4):
                if m != j:
                    term = 1.0 / (points[j] - points[m])
                    for n in range(4):
                        if n != j and n != m:
                            term = term * (points[i] - points[n]) / (points[j] - points[n])
                    total = total + term
            derivative[i, j] = total
    halves = [lagrange((points - 1.0) / 2.0), lagrange((points + 1.0) / 2.0)]
    projections = [0.5 * (1.0 / weights)[:, None] * h.T * weights[None, :] for h in halves]
    interpolate = [np.kron(halves[q // 2], halves[q % 2]) for q in range(4)]
    project = [np.kron(projections[q // 2], projections[q % 2]) for q in range(4)]
    return derivative, interpolate, project


def pieces(matrix):
    value = np.asarray(matrix, np.float32)
    high = value.astype(jnp.bfloat16)
    low = (value - high.astype(np.float32)).astype(jnp.bfloat16)
    return high, low


def constant_matrices():
    derivative, interpolate, project = gll_tables()
    eye_vars = np.eye(VARS)
    blocks = [np.kron(eye_vars, m) for m in project + interpolate] + [np.eye(TILE)]
    tiles = np.concatenate(pieces(np.concatenate(blocks, axis=1)), axis=0)
    eye = np.eye(4)
    volume = np.concatenate(
        [
            np.kron(derivative, np.kron(eye, eye)),
            np.kron(eye, np.kron(derivative, eye)),
            np.kron(eye, np.kron(eye, derivative)),
        ],
        axis=1,
    )
    volume = np.concatenate(pieces(volume), axis=0)
    return jnp.asarray(tiles), jnp.asarray(volume)


def split(x):
    high = x.astype(BF16)
    low = (x - high.astype(F32)).astype(BF16)
    return high, low


def mm(a, b):
    return jnp.dot(a, b, preferred_element_type=F32)


def mm3(a_high, a_low, b):
    columns = b.shape[1]
    b_high, b_low = split(b)
    first = mm(a_high, jnp.concatenate([b_high, b_low], axis=1))
    return first[:, :columns] + (first[:, columns:] + mm(a_low, b_high))


def solve_cells(x, first_ref, final_ref, mid_ref):
    inner = mm3(first_ref[0], first_ref[1], x)
    return mm3(final_ref[0], final_ref[1], mid_ref[...] * inner)


def face_rows(ref, face):
    end = NODES - 1 if face % 2 else 0
    if face // 2 == 0:
        return jnp.concatenate(
            [ref[pl.ds(a * 64 + end * 16, 16), :] for a in range(VARS)], axis=0
        )
    if face // 2 == 1:
        return jnp.concatenate(
            [ref[pl.ds(g * 16 + end * 4, 4), :] for g in range(VARS * 4)], axis=0
        )
    return ref[pl.ds(end, TILE, stride=4), :]


def add_to_face(ref, face, value):
    end = NODES - 1 if face % 2 else 0
    if face // 2 == 0:
        for a in range(VARS):
            ref[pl.ds(a * 64 + end * 16, 16), :] += value[a * 16 : a * 16 + 16]
    elif face // 2 == 1:
        for g in range(VARS * 4):
            ref[pl.ds(g * 16 + end * 4, 4), :] += value[g * 4 : g * 4 + 4]
    else:
        ref[pl.ds(end, TILE, stride=4), :] += value


def all_traces(ref):
    return jnp.concatenate([face_rows(ref, f) for f in range(FACES)], axis=1)


def two_pieces(x):
    high, low = split(x)
    return jnp.concatenate([high, low], axis=0)


def one_hot(condition):
    return jnp.where(condition, 1.0, 0.0).astype(BF16)


def lane_row(length):
    return lax.broadcasted_iota(jnp.int32, (1, length), 1)


def pack_send(field_ref, send_hot_ref, codes, tiles_ref, send_ref, slab_ref):
    groups = send_ref.shape[0]
    lanes = groups * 2 * HALF
    gathered = mm(two_pieces(all_traces(field_ref)), send_hot_ref[...])
    high, low = gathered[:TILE], gathered[TILE:]
    slab_ref[...] = high[:, lanes:] + low[:, lanes:]
    high, low = high[:, :lanes].astype(BF16), low[:, :lanes].astype(BF16)
    masks = [one_hot(codes == q) for q in range(9)]
    high_stack = jnp.concatenate([high * m for m in masks], axis=0)
    low_stack = jnp.concatenate([low * m for m in masks], axis=0)
    result = mm(tiles_ref[...], high_stack)
    result = result[:TILE] + (result[TILE:] + mm(tiles_ref[:TILE], low_stack))
    left = lane_row(128) < 2 * HALF
    middle = TILE // 2
    for pair in range(groups // 2):
        block = result[:, pair * 128 : pair * 128 + 128]
        top, bottom = block[:middle], block[middle:]
        send_ref[2 * pair] = jnp.where(left, top, pltpu.roll(bottom, 64, 1))
        send_ref[2 * pair + 1] = jnp.where(left, pltpu.roll(top, 64, 1), bottom)


def unpack_received(recv_ref):
    left = lane_row(128) < 2 * HALF
    blocks = []
    for pair in range(recv_ref.shape[0] // 2):
        even, odd = recv_ref[2 * pair], recv_ref[2 * pair + 1]
        top = jnp.where(left, even, pltpu.roll(odd, 64, 1))
        bottom = jnp.where(left, pltpu.roll(even, 64, 1), odd)
        blocks.append(jnp.concatenate([top, bottom], axis=0))
    return jnp.concatenate(blocks, axis=1)


def place_lanes(rows, groups, cap):
    lane = lane_row(groups * 2 * HALF)
    within = lane % HALF
    target = jnp.where(within < cap, (lane // (2 * HALF)) * cap + within, -1)
    slots = lax.broadcasted_iota(jnp.int32, (rows.shape[1], lane.shape[1]), 0)
    return mm(rows, one_hot(slots == target))


def index_tables(cap, small, outq, inc, inq, coarse, band, plane, elements, sizes):
    gx_size, groups = sizes
    gx_index, yz_index = lax.axis_index("gx"), lax.axis_index("yz")
    hang, halo = coarse.shape[1], band.shape[1]
    traces = FACES * elements
    as_f = lambda x: x.astype(F32)
    coarse_hot = one_hot(
        lax.broadcasted_iota(jnp.int32, (hang, inc.shape[1]), 0) == inc
    )
    pad = jnp.zeros((6, hang), F32)
    pick = mm(
        jnp.concatenate([as_f(coarse // 8), as_f(coarse % 8), pad], axis=0).astype(BF16),
        coarse_hot,
    )
    rows = jnp.concatenate(
        [
            as_f(small // 8),
            as_f(small % 8),
            jnp.where(inc < hang, pick[0:1], float(traces // 8)),
            jnp.where(inc < hang, pick[1:2], 0.0),
            as_f(outq),
            as_f(inq),
            as_f(inc),
            jnp.zeros_like(pick[0:1]),
        ],
        axis=0,
    ).astype(BF16)
    placed = place_lanes(rows, groups, cap).astype(jnp.int32)
    lane = lane_row(groups * 2 * HALF)
    group, within, second = lane // (2 * HALF), lane % HALF, (lane // HALF) % 2
    is_slot = within < cap
    step = halo // 2
    side = (within >= cap) & (within < cap + step)
    position = within - cap + step * second
    up = lax.rem(yz_index + 1, groups)
    down = lax.rem(yz_index + groups - 1, groups)
    slab_lane = lane_row(128)
    target = jnp.concatenate(
        [
            jnp.where(side, position, -1),
            jnp.where(slab_lane < 2 * halo, slab_lane % halo, -1),
        ],
        axis=1,
    )
    slots = lax.broadcasted_iota(jnp.int32, (halo, target.shape[1]), 0)
    halo_rows = jnp.concatenate([as_f(band), as_f(plane), jnp.zeros((4, halo), F32)], axis=0)
    edge = mm(halo_rows.astype(BF16), one_hot(slots == target)).astype(jnp.int32)
    lanes = lane.shape[1]
    side_send = jnp.where(
        group == up,
        3 * elements + edge[1:2, :lanes],
        jnp.where(group == down, 2 * elements + edge[0:1, :lanes], traces),
    )
    slot_id = jnp.where(
        second == 0, placed[0:1] * 8 + placed[1:2], placed[2:3] * 8 + placed[3:4]
    )
    send_id = jnp.where(is_slot, slot_id, jnp.where(side, side_send, traces))
    codes = jnp.where(
        is_slot, jnp.where(second == 0, placed[4:5], 4 + placed[5:6]), 8
    )
    slab_id = jnp.where(
        slab_lane < halo,
        edge[2:3, lanes:],
        jnp.where(slab_lane < 2 * halo, elements + edge[3:4, lanes:], traces),
    )
    send_id = jnp.concatenate([send_id, slab_id], axis=1)

    first_hang = traces + 4 * halo
    side_recv = jnp.where(
        group == down,
        traces + 2 * halo + position,
        jnp.where(group == up, traces + 3 * halo + position, -1),
    )
    mortar = placed[6:7]
    fine_recv = jnp.where(mortar < hang, first_hang + mortar, -1)
    reply_recv = first_hang + hang + group * cap + within
    recv_id = jnp.where(
        is_slot, jnp.where(second == 0, fine_recv, reply_recv), jnp.where(side, side_recv, -1)
    )
    from_upper = (slab_lane < halo) & (gx_index < gx_size - 1)
    from_lower = (slab_lane >= halo) & (slab_lane < 2 * halo) & (gx_index > 0)
    slab_recv = jnp.where(
        from_upper,
        traces + halo + slab_lane,
        jnp.where(from_lower, traces + slab_lane - halo, -1),
    )
    recv_id = jnp.concatenate([recv_id, slab_recv], axis=1)
    return send_id, codes, recv_id


class Loads:
    def __init__(self, sources, buffers, sems):
        self.buffers = list(buffers)
        self.copies = [
            pltpu.make_async_copy(s, b, sems.at[i])
            for i, (s, b) in enumerate(zip(sources, buffers))
        ]
        for copy in self.copies:
            copy.start()

    def __getitem__(self, i):
        if self.copies[i] is not None:
            self.copies[i].wait()
            self.copies[i] = None
        return self.buffers[i]


def start_kernel(sizes, *refs):
    loads = Loads(refs[:12], refs[20:32], refs[40])
    tables = [loads[i] for i in range(7)]
    outs, stage, sems = refs[12:20], refs[32:40], refs[41]
    field, send, slab, send_hot, codes_ref, recv_id_ref, first2, final2 = stage
    copies = [pltpu.make_async_copy(s, o, sems.at[i]) for i, (s, o) in enumerate(zip(stage, outs))]
    elements = field.shape[1]
    groups = send.shape[0]
    small, outq, inc, inq, coarse, band, plane = tables
    send_id, codes, recv_id = index_tables(
        small.shape[1] // groups,
        small[...],
        outq[...],
        inc[...],
        inq[...],
        coarse[...],
        band[0],
        plane[0],
        elements,
        sizes,
    )
    codes_ref[...] = jnp.broadcast_to(codes, codes_ref.shape)
    copies[4].start()
    recv_id_ref[...] = jnp.broadcast_to(recv_id, recv_id_ref.shape)
    copies[5].start()
    columns = lax.broadcasted_iota(jnp.int32, (FACES * elements, send_id.shape[1]), 0)
    send_hot[...] = one_hot(columns == send_id)
    copies[3].start()
    first2[0], first2[1] = split(loads[7][...])
    copies[6].start()
    final2[0], final2[1] = split(loads[8][...])
    copies[7].start()
    field[...] = solve_cells(loads[9][...], first2, final2, loads[10])
    copies[0].start()
    pack_send(field, send_hot, codes, loads[11], send, slab)
    copies[1].start()
    copies[2].start()
    for copy in copies:
        copy.wait()


def local_part(
    field_ref, mass_ref, coupling_ref, flux_ref, adjacent_ref, volume_ref, local_ref
):
    elements = field_ref.shape[1]
    traces = all_traces(field_ref)
    columns = lax.broadcasted_iota(jnp.int32, (FACES * elements, elements), 0)
    stacked = two_pieces(traces)
    parts = []
    for a in range(VARS):
        flux = []
        for d in range(3):
            total = None
            for b in range(VARS):
                row = d * 25 + a * VARS + b
                term = flux_ref[row : row + 1, :] * field_ref[b * 64 : b * 64 + 64, :]
                total = term if total is None else total + term
            flux.append(total)
        parts.append(jnp.concatenate(flux, axis=0))
    derived = mm3(volume_ref[:64], volume_ref[64:], jnp.concatenate(parts, axis=1))
    for a in range(VARS):
        rows = slice(a * 64, a * 64 + 64)
        local_ref[rows, :] = (
            mass_ref[rows, :] * field_ref[rows, :]
            + derived[:, a * elements : (a + 1) * elements]
        )
    for f in range(FACES):
        near = mm(stacked, one_hot(columns == adjacent_ref[f : f + 1, :]))
        near = near[:TILE] + near[TILE:]
        own = traces[:, f * elements : (f + 1) * elements]
        add_to_face(
            local_ref, f, coupling_ref[f * TILE : (f + 1) * TILE, :] * (own - near)
        )


def first_local_kernel(*refs):
    loads = Loads(refs[:7], refs[9:16], refs[18])
    (local_out, hot_out), (local, recv_hot), sems = refs[7:9], refs[16:18], refs[19]
    elements = local.shape[1]
    ids = jnp.transpose(loads[0][...])[:, 0:1]
    adjacent = loads[1]
    for f in range(FACES):
        recv_hot[:, f * elements : (f + 1) * elements] = one_hot(ids == adjacent[f : f + 1, :])
    hot_copy = pltpu.make_async_copy(recv_hot, hot_out, sems.at[0])
    hot_copy.start()
    local_part(loads[2], loads[3], loads[4], loads[5], adjacent, loads[6], local)
    copy = pltpu.make_async_copy(local, local_out, sems.at[1])
    copy.start()
    copy.wait()
    hot_copy.wait()


def total_of(x):
    return jnp.sum(jnp.sum(x, axis=0, keepdims=True), axis=1, keepdims=True)


def put(values):
    lane = lane_row(128)
    row = jnp.zeros((1, 128), F32)
    for position, value in values:
        row = jnp.where(lane == position, value, row)
    return row


def second_local_kernel(*refs):
    loads = Loads(refs[:7], refs[9:16], refs[18])
    (local_out, partial_out), (local, partial), sems = refs[7:9], refs[16:18], refs[19]
    adjacent = loads[0]
    local_part(loads[1], loads[2], loads[3], loads[4], adjacent, loads[5], local)
    copy = pltpu.make_async_copy(local, local_out, sems.at[0])
    copy.start()
    k0, k1 = loads[6][...], loads[1][...]
    partial[...] = put(
        [(0, total_of(k0 * k0)), (1, total_of(k0 * k1)), (2, total_of(k1 * k1))]
    )
    row_copy = pltpu.make_async_copy(partial, partial_out, sems.at[1])
    row_copy.start()
    copy.wait()
    row_copy.wait()


def finish_product(loads, work_ref):
    recv, slab = loads[0], loads[1]
    received = jnp.concatenate([unpack_received(recv), slab[...]], axis=1)
    near = mm(two_pieces(received), loads[2][...])
    near = near[:TILE] + near[TILE:]
    coupling, local = loads[3], loads[4]
    elements = local.shape[1]
    work_ref[...] = local[...]
    for f in range(FACES):
        add_to_face(
            work_ref,
            f,
            -coupling[f * TILE : (f + 1) * TILE, :] * near[:, f * elements : (f + 1) * elements],
        )
    inner = mm3(loads[5][0], loads[5][1], work_ref[...])
    return mm3(loads[7][0], loads[7][1], loads[6][...] * inner)


def middle_kernel(*refs):
    loads = Loads(refs[:11], refs[14:25], refs[29])
    outs, stage, work, sems = refs[11:14], refs[25:28], refs[28], refs[30]
    copies = [pltpu.make_async_copy(s, o, sems.at[i]) for i, (s, o) in enumerate(zip(stage, outs))]
    field, send, slab = stage
    field[...] = finish_product(loads, work)
    copies[0].start()
    pack_send(field, loads[8], loads[9][0:1, :], loads[10], send, slab)
    copies[1].start()
    copies[2].start()
    for copy in copies:
        copy.wait()


def last_kernel(*refs):
    loads = Loads(refs[:11], refs[12:23], refs[25])
    out, stage, work, sems = refs[11], refs[23], refs[24], refs[26]
    k2 = K2_SCALE * finish_product(loads, work)
    row = loads[10][...] + put(
        [
            (3, total_of(k2 * loads[8][...])),
            (4, total_of(k2 * loads[9][...])),
            (5, total_of(k2 * k2)),
        ]
    )
    stage[...] = jnp.broadcast_to(row.reshape(1, 1, 128), stage.shape)
    copy = pltpu.make_async_copy(stage, out, sems.at[0])
    copy.start()
    copy.wait()


def combine_kernel(*refs):
    loads = Loads(refs[:3], refs[4:7], refs[8])
    out, stage, sems = refs[3], refs[7], refs[9]
    rows_ref = loads[0]
    totals = jnp.sum(rows_ref[:, 0, :], axis=0, keepdims=True)
    lane = lane_row(128)
    g00, g01, g11, g02, g12, g22 = [
        jnp.sum(jnp.where(lane == i, totals, 0.0), axis=1, keepdims=True) for i in range(6)
    ]
    scale = 1.0 / K2_SCALE
    beta = jnp.sqrt(g00 + EPS)
    n00, n01, n11 = g00 / beta / beta, g01 / beta / beta, g11 / beta / beta
    h00 = n01
    w_sq = jnp.maximum(n11 - 2.0 * h00 * n01 + h00 * h00 * n00, 0.0)
    h10 = jnp.sqrt(w_sq + EPS)
    unit = beta * h10
    s = scale / unit
    t = h00 * K2_SCALE
    x0 = (g02 - t * g01) * s / beta
    x1 = ((g12 - t * g11) * s - h00 * ((g02 - t * g01) * s)) / unit
    xx = (((g22 - t * g12) - t * (g12 - t * g11)) * s) * s
    v01 = (n01 - h00 * n00) / h10
    v11 = w_sq / h10 / h10
    h01 = x0
    h11 = x1 - h01 * v01
    rest = xx - 2.0 * h01 * x0 + h01 * h01 * n00
    rest = rest - 2.0 * h11 * h11 + h11 * h11 * v11
    h21 = jnp.sqrt(jnp.maximum(rest, 0.0) + EPS)
    radius0 = jnp.sqrt(h00 * h00 + h10 * h10)
    c0, s0 = h00 / radius0, h10 / radius0
    target1 = -s0 * beta
    target0 = c0 * beta
    upper = c0 * h01 + s0 * h11
    lower = c0 * h11 - s0 * h01
    radius1 = jnp.sqrt(lower * lower + h21 * h21)
    y1 = (lower / radius1) * target1 / radius1
    y0 = (target0 - upper * y1) / radius0
    along1 = y1 / unit
    along0 = y0 / beta - along1 * h00
    stage[...] = along0 * loads[1][...] + along1 * loads[2][...]
    copy = pltpu.make_async_copy(stage, out, sems.at[0])
    copy.start()
    copy.wait()


def call(kernel, outs, args, scratch=()):
    in_place = pl.BlockSpec(memory_space=pl.ANY)
    out_list = jax.tree.leaves(outs)
    buffers = [pltpu.VMEM(a.shape, a.dtype) for a in list(args) + out_list]
    buffers += list(scratch)
    buffers += [pltpu.SemaphoreType.DMA((len(args),)), pltpu.SemaphoreType.DMA((len(out_list),))]
    return pl.pallas_call(
        kernel,
        out_shape=outs,
        in_specs=[in_place] * len(args),
        out_specs=jax.tree.map(lambda _: in_place, outs),
        scratch_shapes=buffers,
        cost_estimate=pl.CostEstimate(
            flops=10**9,
            bytes_accessed=sum(a.size * a.dtype.itemsize for a in args),
            transcendentals=0,
        ),
        compiler_params=pltpu.CompilerParams(vmem_limit_bytes=67043328),
    )(*args)


def on_device(
    source,
    mass,
    coupling,
    flux,
    first,
    final,
    mid,
    adjacent,
    plane,
    band,
    small,
    proprietor,
    outq,
    inc,
    inq,
    coarse,
):
    del proprietor
    tiles, volume = constant_matrices()
    gx_size, groups = lax.axis_size("gx"), lax.axis_size("yz")
    elements = source.shape[1]
    traces = FACES * elements
    lanes = groups * 2 * HALF
    struct = jax.ShapeDtypeStruct
    field = struct((DOFS, elements), F32)
    send = struct((groups, TILE // 2, 128), F32)
    slab = struct((TILE, 128), F32)

    k0, send0, slab0, send_hot, codes, recv_id, first2, final2 = call(
        functools.partial(start_kernel, (gx_size, groups)),
        (
            field,
            send,
            slab,
            struct((traces, lanes + 128), BF16),
            struct((8, lanes), jnp.int32),
            struct((8, lanes + 128), jnp.int32),
            struct((2, DOFS, DOFS), BF16),
            struct((2, DOFS, DOFS), BF16),
        ),
        (small, outq, inc, inq, coarse, band, plane, first, final, source, mid, tiles),
    )

    up = [(i, i + 1) for i in range(gx_size - 1)]
    down = [(j, i) for i, j in up]

    def exchange(send, slab):
        if gx_size == 2:
            slab = lax.ppermute(slab, "gx", up + down)
        else:
            halo = plane.shape[2]
            lower = lax.ppermute(slab, "gx", up)
            upper = lax.ppermute(slab, "gx", down)
            slab = jnp.where(lane_row(128) < halo, upper, lower)
        return lax.all_to_all(send, "yz", 0, 0, tiled=True), slab

    recv0, slab0 = exchange(send0, slab0)
    local0, recv_hot = call(
        first_local_kernel,
        (field, struct((lanes + 128, traces), BF16)),
        (recv_id, adjacent, k0, mass, coupling, flux, volume),
    )
    work = pltpu.VMEM((DOFS, elements), F32)
    solve_args = (coupling, local0, first2, mid, final2)
    k1, send1, slab1 = call(
        middle_kernel,
        (field, send, slab),
        (recv0, slab0, recv_hot) + solve_args + (send_hot, codes, tiles),
        scratch=[work],
    )
    recv1, slab1 = exchange(send1, slab1)
    local1, partial = call(
        second_local_kernel,
        (field, struct((1, 128), F32)),
        (adjacent, k1, mass, coupling, flux, volume, k0),
    )
    solve_args = (coupling, local1, first2, mid, final2)
    rows = call(
        last_kernel,
        struct((gx_size * groups, 1, 128), F32),
        (recv1, slab1, recv_hot) + solve_args + (k0, k1, partial),
        scratch=[work],
    )
    rows = lax.all_to_all(rows, ("gx", "yz"), 0, 0, tiled=True)
    return call(combine_kernel, field, (rows, k0, k1))


def solution(mesh):
    by_column = P(None, ("gx", "yz"))
    by_row = P(("gx", "yz"), None)
    by_plane = P(("gx", "yz"), None, None)
    return jax.shard_map(
        on_device,
        mesh=mesh,
        in_specs=(by_column,) * 4
        + (P(), P())
        + (by_column,) * 2
        + (by_plane,) * 2
        + (by_row,) * 6,
        out_specs=by_column,
        check_vma=False,
    )
```

```python
import functools

import jax
import jax.numpy as jnp
import numpy as np
from jax import lax
from jax.experimental import pallas as pl
from jax.experimental.pallas import tpu as pltpu
from jax.sharding import PartitionSpec as P

EPS = 1e-06
NODES = 4
VARS = 5
TILE = VARS * NODES * NODES
DOFS = TILE * NODES
FACES = 6
HALF = 32
K2_SCALE = 2.0**-20
VMEM_LIMIT = 40 * 2**20
F32 = jnp.float32
BF16 = jnp.bfloat16


def gll_tables():
    root = 1.0 / np.sqrt(5.0)
    points = np.array([-1.0, -root, root, 1.0])
    weights = np.array([1.0, 5.0, 5.0, 1.0]) / 6.0

    def lagrange(at):
        values = np.ones((len(at), 4))
        for j in range(4):
            for m in range(4):
                if m != j:
                    values[:, j] = values[:, j] * (at - points[m]) / (points[j] - points[m])
        return values

    derivative = np.zeros((4, 4))
    for i in range(4):
        for j in range(4):
            total = 0.0
            for m in range(4):
                if m != j:
                    term = 1.0 / (points[j] - points[m])
                    for n in range(4):
                        if n != j and n != m:
                            term = term * (points[i] - points[n]) / (points[j] - points[n])
                    total = total + term
            derivative[i, j] = total
    halves = [lagrange((points - 1.0) / 2.0), lagrange((points + 1.0) / 2.0)]
    projections = [0.5 * (1.0 / weights)[:, None] * h.T * weights[None, :] for h in halves]
    interpolate = [np.kron(halves[q // 2], halves[q % 2]) for q in range(4)]
    project = [np.kron(projections[q // 2], projections[q % 2]) for q in range(4)]
    return derivative, interpolate, project


def pieces(matrix):
    value = np.asarray(matrix, np.float32)
    high = value.astype(jnp.bfloat16)
    low = (value - high.astype(np.float32)).astype(jnp.bfloat16)
    return high, low


def constant_matrices():
    derivative, interpolate, project = gll_tables()
    eye_vars = np.eye(VARS)
    blocks = [np.kron(eye_vars, m) for m in project + interpolate] + [np.eye(TILE)]
    tiles = np.concatenate(pieces(np.concatenate(blocks, axis=1)), axis=0)
    eye = np.eye(4)
    volume = np.concatenate(
        [
            np.kron(derivative, np.kron(eye, eye)),
            np.kron(eye, np.kron(derivative, eye)),
            np.kron(eye, np.kron(eye, derivative)),
        ],
        axis=1,
    )
    volume = np.concatenate(pieces(volume), axis=0)
    return jnp.asarray(tiles), jnp.asarray(volume)


def split(x):
    high = x.astype(BF16)
    low = (x - high.astype(F32)).astype(BF16)
    return high, low


def mm(a, b):
    return jnp.dot(a, b, preferred_element_type=F32)


def mm3(a_high, a_low, b):
    columns = b.shape[1]
    b_high, b_low = split(b)
    first = mm(a_high, jnp.concatenate([b_high, b_low], axis=1))
    return first[:, :columns] + (first[:, columns:] + mm(a_low, b_high))


def solve_cells(x, first_ref, final_ref, mid_ref):
    inner = mm3(first_ref[0], first_ref[1], x)
    return mm3(final_ref[0], final_ref[1], mid_ref[...] * inner)


def face_rows(ref, face):
    end = NODES - 1 if face % 2 else 0
    if face // 2 == 0:
        return jnp.concatenate(
            [ref[pl.ds(a * 64 + end * 16, 16), :] for a in range(VARS)], axis=0
        )
    if face // 2 == 1:
        return jnp.concatenate(
            [ref[pl.ds(g * 16 + end * 4, 4), :] for g in range(VARS * 4)], axis=0
        )
    return ref[pl.ds(end, TILE, stride=4), :]


def add_to_face(ref, face, value):
    end = NODES - 1 if face % 2 else 0
    if face // 2 == 0:
        for a in range(VARS):
            ref[pl.ds(a * 64 + end * 16, 16), :] += value[a * 16 : a * 16 + 16]
    elif face // 2 == 1:
        for g in range(VARS * 4):
            ref[pl.ds(g * 16 + end * 4, 4), :] += value[g * 4 : g * 4 + 4]
    else:
        ref[pl.ds(end, TILE, stride=4), :] += value


def all_traces(ref):
    return jnp.concatenate([face_rows(ref, f) for f in range(FACES)], axis=1)


def two_pieces(x):
    high, low = split(x)
    return jnp.concatenate([high, low], axis=0)


def one_hot(condition):
    return jnp.where(condition, 1.0, 0.0).astype(BF16)


def lane_row(length):
    return lax.broadcasted_iota(jnp.int32, (1, length), 1)


def pack_send(field_ref, send_hot_ref, codes, tiles_ref, send_ref, slab_ref):
    groups = send_ref.shape[0]
    lanes = groups * 2 * HALF
    gathered = mm(two_pieces(all_traces(field_ref)), send_hot_ref[...])
    high, low = gathered[:TILE], gathered[TILE:]
    slab_ref[...] = high[:, lanes:] + low[:, lanes:]
    high, low = high[:, :lanes].astype(BF16), low[:, :lanes].astype(BF16)
    masks = [one_hot(codes == q) for q in range(9)]
    high_stack = jnp.concatenate([high * m for m in masks], axis=0)
    low_stack = jnp.concatenate([low * m for m in masks], axis=0)
    result = mm(tiles_ref[...], high_stack)
    result = result[:TILE] + (result[TILE:] + mm(tiles_ref[:TILE], low_stack))
    left = lane_row(128) < 2 * HALF
    middle = TILE // 2
    for pair in range(groups // 2):
        block = result[:, pair * 128 : pair * 128 + 128]
        top, bottom = block[:middle], block[middle:]
        send_ref[2 * pair] = jnp.where(left, top, pltpu.roll(bottom, 64, 1))
        send_ref[2 * pair + 1] = jnp.where(left, pltpu.roll(top, 64, 1), bottom)


def unpack_received(recv_ref):
    left = lane_row(128) < 2 * HALF
    blocks = []
    for pair in range(recv_ref.shape[0] // 2):
        even, odd = recv_ref[2 * pair], recv_ref[2 * pair + 1]
        top = jnp.where(left, even, pltpu.roll(odd, 64, 1))
        bottom = jnp.where(left, pltpu.roll(even, 64, 1), odd)
        blocks.append(jnp.concatenate([top, bottom], axis=0))
    return jnp.concatenate(blocks, axis=1)


def place_lanes(rows, groups, cap):
    lane = lane_row(groups * 2 * HALF)
    within = lane % HALF
    target = jnp.where(within < cap, (lane // (2 * HALF)) * cap + within, -1)
    slots = lax.broadcasted_iota(jnp.int32, (rows.shape[1], lane.shape[1]), 0)
    return mm(rows, one_hot(slots == target))


def index_tables(cap, small, outq, inc, inq, coarse, band, plane, elements, sizes):
    gx_size, groups = sizes
    gx_index, yz_index = lax.axis_index("gx"), lax.axis_index("yz")
    hang, halo = coarse.shape[1], band.shape[1]
    traces = FACES * elements
    as_f = lambda x: x.astype(F32)
    coarse_hot = one_hot(
        lax.broadcasted_iota(jnp.int32, (hang, inc.shape[1]), 0) == inc
    )
    pad = jnp.zeros((6, hang), F32)
    pick = mm(
        jnp.concatenate([as_f(coarse // 8), as_f(coarse % 8), pad], axis=0).astype(BF16),
        coarse_hot,
    )
    rows = jnp.concatenate(
        [
            as_f(small // 8),
            as_f(small % 8),
            jnp.where(inc < hang, pick[0:1], float(traces // 8)),
            jnp.where(inc < hang, pick[1:2], 0.0),
            as_f(outq),
            as_f(inq),
            as_f(inc),
            jnp.zeros_like(pick[0:1]),
        ],
        axis=0,
    ).astype(BF16)
    placed = place_lanes(rows, groups, cap).astype(jnp.int32)
    lane = lane_row(groups * 2 * HALF)
    group, within, second = lane // (2 * HALF), lane % HALF, (lane // HALF) % 2
    is_slot = within < cap
    step = halo // 2
    side = (within >= cap) & (within < cap + step)
    position = within - cap + step * second
    up = lax.rem(yz_index + 1, groups)
    down = lax.rem(yz_index + groups - 1, groups)
    slab_lane = lane_row(128)
    target = jnp.concatenate(
        [
            jnp.where(side, position, -1),
            jnp.where(slab_lane < 2 * halo, slab_lane % halo, -1),
        ],
        axis=1,
    )
    slots = lax.broadcasted_iota(jnp.int32, (halo, target.shape[1]), 0)
    halo_rows = jnp.concatenate([as_f(band), as_f(plane), jnp.zeros((4, halo), F32)], axis=0)
    edge = mm(halo_rows.astype(BF16), one_hot(slots == target)).astype(jnp.int32)
    lanes = lane.shape[1]
    side_send = jnp.where(
        group == up,
        3 * elements + edge[1:2, :lanes],
        jnp.where(group == down, 2 * elements + edge[0:1, :lanes], traces),
    )
    slot_id = jnp.where(
        second == 0, placed[0:1] * 8 + placed[1:2], placed[2:3] * 8 + placed[3:4]
    )
    send_id = jnp.where(is_slot, slot_id, jnp.where(side, side_send, traces))
    codes = jnp.where(
        is_slot, jnp.where(second == 0, placed[4:5], 4 + placed[5:6]), 8
    )
    slab_id = jnp.where(
        slab_lane < halo,
        edge[2:3, lanes:],
        jnp.where(slab_lane < 2 * halo, elements + edge[3:4, lanes:], traces),
    )
    send_id = jnp.concatenate([send_id, slab_id], axis=1)

    first_hang = traces + 4 * halo
    side_recv = jnp.where(
        group == down,
        traces + 2 * halo + position,
        jnp.where(group == up, traces + 3 * halo + position, -1),
    )
    mortar = placed[6:7]
    fine_recv = jnp.where(mortar < hang, first_hang + mortar, -1)
    reply_recv = first_hang + hang + group * cap + within
    recv_id = jnp.where(
        is_slot, jnp.where(second == 0, fine_recv, reply_recv), jnp.where(side, side_recv, -1)
    )
    from_upper = (slab_lane < halo) & (gx_index < gx_size - 1)
    from_lower = (slab_lane >= halo) & (slab_lane < 2 * halo) & (gx_index > 0)
    slab_recv = jnp.where(
        from_upper,
        traces + halo + slab_lane,
        jnp.where(from_lower, traces + slab_lane - halo, -1),
    )
    recv_id = jnp.concatenate([recv_id, slab_recv], axis=1)
    return send_id, codes, recv_id


class Refs:
    def __init__(self, plan, refs):
        arg_vmem, out_vmem = plan
        refs = list(refs)
        take = lambda n: [refs.pop(0) for _ in range(n)]
        args, outs = take(len(arg_vmem)), take(len(out_vmem))
        self.args = [a if v else refs.pop(0) for a, v in zip(args, arg_vmem)]
        self.outs = [o if v else refs.pop(0) for o, v in zip(outs, out_vmem)]
        in_sems, out_sems = take(2)
        self.work = refs
        self.pending = [
            None if v else pltpu.make_async_copy(a, b, in_sems.at[i])
            for i, (a, b, v) in enumerate(zip(args, self.args, arg_vmem))
        ]
        self.ships = [
            None if v else pltpu.make_async_copy(b, o, out_sems.at[i])
            for i, (o, b, v) in enumerate(zip(outs, self.outs, out_vmem))
        ]
        self.sent = []

    def start(self):
        for copy in self.pending:
            if copy is not None:
                copy.start()

    def get(self, i):
        if self.pending[i] is not None:
            self.pending[i].wait()
            self.pending[i] = None
        return self.args[i]

    def ship(self, i):
        if self.ships[i] is not None:
            self.ships[i].start()
            self.sent.append(self.ships[i])

    def finish(self):
        for copy in self.sent:
            copy.wait()


def start_kernel(sizes, plan, *refs):
    r = Refs(plan, refs)
    r.start()
    field, send, slab, send_hot, codes_ref, recv_id_ref, first2, final2 = r.outs
    elements = field.shape[1]
    groups = send.shape[0]
    small, outq, inc, inq, coarse, band, plane = [r.get(i) for i in range(7)]
    send_id, codes, recv_id = index_tables(
        small.shape[1] // groups,
        small[...],
        outq[...],
        inc[...],
        inq[...],
        coarse[...],
        band[0],
        plane[0],
        elements,
        sizes,
    )
    codes_ref[...] = jnp.broadcast_to(codes, codes_ref.shape)
    r.ship(4)
    recv_id_ref[...] = jnp.broadcast_to(recv_id, recv_id_ref.shape)
    r.ship(5)
    fill_send_hot(send_id, send_hot)
    r.ship(3)
    first2[0], first2[1] = split(r.get(7)[...])
    r.ship(6)
    final2[0], final2[1] = split(r.get(8)[...])
    r.ship(7)
    field[...] = solve_cells(r.get(9)[...], first2, final2, r.get(10))
    r.ship(0)
    pack_send(field, send_hot, codes, r.get(11), send, slab)
    r.ship(1)
    r.ship(2)
    r.finish()


def local_part(
    field_ref, mass_ref, coupling_ref, flux_ref, adjacent_ref, volume_ref, local_ref
):
    elements = field_ref.shape[1]
    traces = all_traces(field_ref)
    columns = lax.broadcasted_iota(jnp.int32, (FACES * elements, elements), 0)
    stacked = two_pieces(traces)
    parts = []
    for a in range(VARS):
        flux = []
        for d in range(3):
            total = None
            for b in range(VARS):
                row = d * 25 + a * VARS + b
                term = flux_ref[row : row + 1, :] * field_ref[b * 64 : b * 64 + 64, :]
                total = term if total is None else total + term
            flux.append(total)
        parts.append(jnp.concatenate(flux, axis=0))
    derived = mm3(volume_ref[:64], volume_ref[64:], jnp.concatenate(parts, axis=1))
    for a in range(VARS):
        rows = slice(a * 64, a * 64 + 64)
        local_ref[rows, :] = (
            mass_ref[rows, :] * field_ref[rows, :]
            + derived[:, a * elements : (a + 1) * elements]
        )
    for f in range(FACES):
        near = mm(stacked, one_hot(columns == adjacent_ref[f : f + 1, :]))
        near = near[:TILE] + near[TILE:]
        own = traces[:, f * elements : (f + 1) * elements]
        add_to_face(
            local_ref, f, coupling_ref[f * TILE : (f + 1) * TILE, :] * (own - near)
        )


def hold(r, outs, args):
    copies = [
        pltpu.make_async_copy(r.args[arg], r.outs[out], r.work[0].at[n])
        for n, (out, arg) in enumerate(zip(outs, args))
    ]
    for copy in copies:
        copy.start()
    return copies


def fill_received_hot(ids, adjacent, hot_ref):
    elements = adjacent.shape[1]
    column = jnp.transpose(ids)[:, 0:1]
    for f in range(FACES):
        hot_ref[:, f * elements : (f + 1) * elements] = one_hot(column == adjacent[f : f + 1, :])


def prepare(r):
    local, recv_hot, coupling, first2 = r.outs[:4]
    copies = hold(r, (2, 3), (2, 7))
    r.start()
    fill_received_hot(r.get(6)[...], r.get(4), recv_hot)
    for copy in copies:
        copy.wait()
    local_part(r.get(0), r.get(1), coupling, r.get(3), r.get(4), r.get(5), local)


def first_local_kernel(plan, *refs):
    prepare(Refs(plan, refs))


def second_local_kernel(plan, *refs):
    r = Refs(plan, refs)
    prepare(r)
    k0, k1 = r.get(8)[...], r.get(0)[...]
    r.outs[4][...] = put(
        [(0, total_of(k0 * k0)), (1, total_of(k0 * k1)), (2, total_of(k1 * k1))]
    )


def total_of(x):
    return jnp.sum(jnp.sum(x, axis=0, keepdims=True), axis=1, keepdims=True)


def put(values):
    lane = lane_row(128)
    row = jnp.zeros((1, 128), F32)
    for position, value in values:
        row = jnp.where(lane == position, value, row)
    return row


def fill_send_hot(send_id, hot_ref):
    columns = lax.broadcasted_iota(jnp.int32, hot_ref.shape, 0)
    hot_ref[...] = one_hot(columns == send_id)


def finish_product(r, work_ref):
    received = jnp.concatenate([unpack_received(r.get(0)), r.get(1)[...]], axis=1)
    near = mm(two_pieces(received), r.get(2)[...])
    near = near[:TILE] + near[TILE:]
    coupling, local = r.get(3), r.get(4)
    elements = local.shape[1]
    work_ref[...] = local[...]
    for f in range(FACES):
        add_to_face(
            work_ref,
            f,
            -coupling[f * TILE : (f + 1) * TILE, :] * near[:, f * elements : (f + 1) * elements],
        )
    first = r.get(5)
    inner = mm3(first[0], first[1], work_ref[...])
    final = r.get(7)
    return mm3(final[0], final[1], r.get(6)[...] * inner)


def middle_kernel(plan, *refs):
    r = Refs(plan, refs)
    r.start()
    field, send, slab = r.outs
    field[...] = finish_product(r, r.work[0])
    r.ship(0)
    pack_send(field, r.get(8), r.get(9)[0:1, :], r.get(10), send, slab)
    r.ship(1)
    r.ship(2)
    r.finish()


def last_kernel(plan, *refs):
    r = Refs(plan, refs)
    work = r.work[1]
    fills = hold(r, (1, 2), (8, 9))
    r.start()
    rows, k0, k1 = r.outs
    k2 = K2_SCALE * finish_product(r, work)
    for fill in fills:
        fill.wait()
    row = r.get(10)[...] + put(
        [
            (3, total_of(k2 * k0[...])),
            (4, total_of(k2 * k1[...])),
            (5, total_of(k2 * k2)),
        ]
    )
    rows[...] = jnp.broadcast_to(row.reshape(1, 1, 128), rows.shape)


def combine_kernel(plan, *refs):
    r = Refs(plan, refs)
    r.start()
    rows_ref = r.get(0)
    totals = jnp.sum(rows_ref[:, 0, :], axis=0, keepdims=True)
    lane = lane_row(128)
    g00, g01, g11, g02, g12, g22 = [
        jnp.sum(jnp.where(lane == i, totals, 0.0), axis=1, keepdims=True) for i in range(6)
    ]
    scale = 1.0 / K2_SCALE
    beta = jnp.sqrt(g00 + EPS)
    n00, n01, n11 = g00 / beta / beta, g01 / beta / beta, g11 / beta / beta
    h00 = n01
    w_sq = jnp.maximum(n11 - 2.0 * h00 * n01 + h00 * h00 * n00, 0.0)
    h10 = jnp.sqrt(w_sq + EPS)
    unit = beta * h10
    s = scale / unit
    t = h00 * K2_SCALE
    x0 = (g02 - t * g01) * s / beta
    x1 = ((g12 - t * g11) * s - h00 * ((g02 - t * g01) * s)) / unit
    xx = (((g22 - t * g12) - t * (g12 - t * g11)) * s) * s
    v01 = (n01 - h00 * n00) / h10
    v11 = w_sq / h10 / h10
    h01 = x0
    h11 = x1 - h01 * v01
    rest = xx - 2.0 * h01 * x0 + h01 * h01 * n00
    rest = rest - 2.0 * h11 * h11 + h11 * h11 * v11
    h21 = jnp.sqrt(jnp.maximum(rest, 0.0) + EPS)
    radius0 = jnp.sqrt(h00 * h00 + h10 * h10)
    c0, s0 = h00 / radius0, h10 / radius0
    target1 = -s0 * beta
    target0 = c0 * beta
    upper = c0 * h01 + s0 * h11
    lower = c0 * h11 - s0 * h01
    radius1 = jnp.sqrt(lower * lower + h21 * h21)
    y1 = (lower / radius1) * target1 / radius1
    y0 = (target0 - upper * y1) / radius0
    along1 = y1 / unit
    along0 = y0 / beta - along1 * h00
    r.outs[0][...] = along0 * r.get(1)[...] + along1 * r.get(2)[...]
    r.ship(0)
    r.finish()


def call(kernel, outs, args, arg_spaces=None, out_spaces=None, scratch=()):
    arg_spaces = arg_spaces or "h" * len(args)
    out_spaces = out_spaces or "h" * len(outs)
    space = lambda c: pltpu.VMEM if c == "v" else pltpu.HBM
    plan = (tuple(c != "h" for c in arg_spaces), tuple(c != "h" for c in out_spaces))
    buffers = [
        pltpu.VMEM(a.shape, a.dtype)
        for a, c in zip(tuple(args) + tuple(outs), arg_spaces + out_spaces)
        if c == "h"
    ]
    buffers += [pltpu.SemaphoreType.DMA((len(args),)), pltpu.SemaphoreType.DMA((len(outs),))]
    return pl.pallas_call(
        functools.partial(kernel, plan),
        out_shape=tuple(space(c)(o.shape, o.dtype) for o, c in zip(outs, out_spaces)),
        in_specs=[pl.BlockSpec(memory_space=space(c)) for c in arg_spaces],
        out_specs=tuple(pl.BlockSpec(memory_space=space(c)) for c in out_spaces),
        scratch_shapes=buffers + list(scratch),
        cost_estimate=pl.CostEstimate(
            flops=10**9,
            bytes_accessed=sum(a.size * a.dtype.itemsize for a in args),
            transcendentals=0,
        ),
        compiler_params=pltpu.CompilerParams(vmem_limit_bytes=VMEM_LIMIT),
    )(*[pltpu.with_memory_space_constraint(a, space(c)) for a, c in zip(args, arg_spaces)])


def on_device(
    source,
    mass,
    coupling,
    flux,
    first,
    final,
    mid,
    adjacent,
    plane,
    band,
    small,
    proprietor,
    outq,
    inc,
    inq,
    coarse,
):
    del proprietor
    tiles, volume = constant_matrices()
    gx_size, groups = lax.axis_size("gx"), lax.axis_size("yz")
    elements = source.shape[1]
    traces = FACES * elements
    lanes = groups * 2 * HALF
    struct = jax.ShapeDtypeStruct
    field = struct((DOFS, elements), F32)
    send = struct((groups, TILE // 2, 128), F32)
    slab = struct((TILE, 128), F32)

    k0, send0, slab0, send_hot, codes, recv_id, first2, final2 = call(
        functools.partial(start_kernel, (gx_size, groups)),
        (
            field,
            send,
            slab,
            struct((traces, lanes + 128), BF16),
            struct((8, lanes), jnp.int32),
            struct((8, lanes + 128), jnp.int32),
            struct((2, DOFS, DOFS), BF16),
            struct((2, DOFS, DOFS), BF16),
        ),
        (small, outq, inc, inq, coarse, band, plane, first, final, source, mid, tiles),
    )

    up = [(i, i + 1) for i in range(gx_size - 1)]
    down = [(j, i) for i, j in up]

    def exchange(send, slab):
        if gx_size == 2:
            slab = lax.ppermute(slab, "gx", up + down)
        else:
            halo = plane.shape[2]
            lower = lax.ppermute(slab, "gx", up)
            upper = lax.ppermute(slab, "gx", down)
            slab = jnp.where(lane_row(128) < halo, upper, lower)
        return lax.all_to_all(send, "yz", 0, 0, tiled=True), slab

    recv0, slab0 = exchange(send0, slab0)
    copy_sems = pltpu.SemaphoreType.DMA((2,))
    work = pltpu.VMEM((DOFS, elements), F32)
    held = (
        field,
        struct((lanes + 128, traces), BF16),
        struct(coupling.shape, F32),
        struct(first2.shape, BF16),
    )
    local_args = lambda u: (u, mass, coupling, flux, adjacent, volume, recv_id, first2)
    local, recv_hot, near_coupling, near_first = call(
        first_local_kernel, held, local_args(k0), "hhrhhhhr", "vvvv", scratch=[copy_sems]
    )
    k1, send1, slab1 = call(
        middle_kernel,
        (field, send, slab),
        (recv0, slab0, recv_hot, near_coupling, local, near_first)
        + (mid, final2, send_hot, codes, tiles),
        "vvvvvvhhhhh",
        scratch=[work],
    )
    recv1, slab1 = exchange(send1, slab1)
    local, recv_hot, near_coupling, near_first, partial = call(
        second_local_kernel,
        held + (struct((1, 128), F32),),
        local_args(k1) + (k0,),
        "hhrhhhhrh",
        "vvvvv",
        scratch=[copy_sems],
    )
    rows, k0, k1 = call(
        last_kernel,
        (struct((gx_size * groups, 1, 128), F32), field, field),
        (recv1, slab1, recv_hot, near_coupling, local, near_first)
        + (mid, final2, k0, k1, partial),
        "vvvvvvhhrrv",
        "vvv",
        scratch=[copy_sems, work],
    )
    rows = lax.all_to_all(rows, ("gx", "yz"), 0, 0, tiled=True)
    (update,) = call(combine_kernel, (field,), (rows, k0, k1), "vvv")
    return update


def solution(mesh):
    by_column = P(None, ("gx", "yz"))
    by_row = P(("gx", "yz"), None)
    by_plane = P(("gx", "yz"), None, None)
    return jax.shard_map(
        on_device,
        mesh=mesh,
        in_specs=(by_column,) * 4
        + (P(), P())
        + (by_column,) * 2
        + (by_plane,) * 2
        + (by_row,) * 6,
        out_specs=by_column,
        check_vma=False,
    )
```

```python
import functools

import jax
import jax.numpy as jnp
import numpy as np
from jax import lax
from jax.experimental import pallas as pl
from jax.experimental.pallas import tpu as pltpu
from jax.sharding import PartitionSpec as P

EPS = 1e-06
NODES = 4
VARS = 5
TILE = VARS * NODES * NODES
DOFS = TILE * NODES
FACES = 6
STRIDE = 64
K2_SCALE = 2.0**-20
VMEM_LIMIT = 40 * 2**20
F32 = jnp.float32
BF16 = jnp.bfloat16


def gll_tables():
    root = 1.0 / np.sqrt(5.0)
    points = np.array([-1.0, -root, root, 1.0])
    weights = np.array([1.0, 5.0, 5.0, 1.0]) / 6.0

    def lagrange(at):
        values = np.ones((len(at), 4))
        for j in range(4):
            for m in range(4):
                if m != j:
                    values[:, j] = values[:, j] * (at - points[m]) / (points[j] - points[m])
        return values

    derivative = np.zeros((4, 4))
    for i in range(4):
        for j in range(4):
            total = 0.0
            for m in range(4):
                if m != j:
                    term = 1.0 / (points[j] - points[m])
                    for n in range(4):
                        if n != j and n != m:
                            term = term * (points[i] - points[n]) / (points[j] - points[n])
                    total = total + term
            derivative[i, j] = total
    halves = [lagrange((points - 1.0) / 2.0), lagrange((points + 1.0) / 2.0)]
    projections = [0.5 * (1.0 / weights)[:, None] * h.T * weights[None, :] for h in halves]
    interpolate = [np.kron(halves[q // 2], halves[q % 2]) for q in range(4)]
    project = [np.kron(projections[q // 2], projections[q % 2]) for q in range(4)]
    return derivative, interpolate, project


def pieces(matrix):
    value = np.asarray(matrix, np.float32)
    high = value.astype(jnp.bfloat16)
    low = (value - high.astype(np.float32)).astype(jnp.bfloat16)
    return high, low


def constant_matrices():
    derivative, interpolate, project = gll_tables()
    eye_vars = np.eye(VARS)
    blocks = [np.kron(eye_vars, m) for m in project + interpolate]
    tiles = np.concatenate(pieces(np.concatenate(blocks, axis=1)), axis=0)
    eye = np.eye(4)
    volume = np.concatenate(
        [
            np.kron(derivative, np.kron(eye, eye)),
            np.kron(eye, np.kron(derivative, eye)),
            np.kron(eye, np.kron(eye, derivative)),
        ],
        axis=1,
    )
    volume = np.concatenate(pieces(volume), axis=0)
    return jnp.asarray(tiles), jnp.asarray(volume)


def split(x):
    high = x.astype(BF16)
    low = (x - high.astype(F32)).astype(BF16)
    return high, low


def mm(a, b):
    return jnp.dot(a, b, preferred_element_type=F32)


def mm3(a_high, a_low, b):
    columns = b.shape[1]
    b_high, b_low = split(b)
    first = mm(a_high, jnp.concatenate([b_high, b_low], axis=1))
    return first[:, :columns] + (first[:, columns:] + mm(a_low, b_high))


def solve_cells(x, first_ref, final_ref, mid_ref):
    inner = mm3(first_ref[0], first_ref[1], x)
    return mm3(final_ref[0], final_ref[1], mid_ref[...] * inner)


def face_rows(ref, face):
    end = NODES - 1 if face % 2 else 0
    if face // 2 == 0:
        return jnp.concatenate(
            [ref[pl.ds(a * 64 + end * 16, 16), :] for a in range(VARS)], axis=0
        )
    if face // 2 == 1:
        return jnp.concatenate(
            [ref[pl.ds(g * 16 + end * 4, 4), :] for g in range(VARS * 4)], axis=0
        )
    return ref[pl.ds(end, TILE, stride=4), :]


def add_to_face(ref, face, value):
    end = NODES - 1 if face % 2 else 0
    if face // 2 == 0:
        for a in range(VARS):
            ref[pl.ds(a * 64 + end * 16, 16), :] += value[a * 16 : a * 16 + 16]
    elif face // 2 == 1:
        for g in range(VARS * 4):
            ref[pl.ds(g * 16 + end * 4, 4), :] += value[g * 4 : g * 4 + 4]
    else:
        ref[pl.ds(end, TILE, stride=4), :] += value


def all_traces(ref):
    return jnp.concatenate([face_rows(ref, f) for f in range(FACES)], axis=1)


def two_pieces(x):
    high, low = split(x)
    return jnp.concatenate([high, low], axis=0)


def one_hot(condition):
    return jnp.where(condition, 1.0, 0.0).astype(BF16)


def lane_row(length):
    return lax.broadcasted_iota(jnp.int32, (1, length), 1)


def fold_plan(columns):
    for rows in range(8, TILE + 1, 8):
        full, rest = TILE // rows, TILE % rows
        parts = rows // rest if rest else 1
        width = -(-columns // parts) if rest else 0
        if full * columns + width <= 128:
            break
    plan = [(g * rows, rows, 0, columns, 0, g * columns) for g in range(full)]
    if rest:
        for part in range(parts):
            count = min(width, columns - part * width)
            if count > 0:
                plan.append(
                    (full * rows, rest, part * width, count, part * rest, full * columns)
                )
    return rows, plan


def roll_lanes(x, shift):
    return pltpu.roll(x, shift % 128, 1) if shift % 128 else x


def in_lanes(start, count):
    lane = lane_row(128)
    return (lane >= start) & (lane < start + count)


def fold_halves(block):
    middle = TILE // 2
    return jnp.where(
        lane_row(128) < STRIDE, block[:middle], roll_lanes(block[middle:], STRIDE)
    )


def unfold_halves(block):
    return jnp.concatenate([block, roll_lanes(block, STRIDE)], axis=0)


def pack_send(field_ref, send_hot_ref, codes, tiles_ref, send_ref, halo_ref, cap):
    groups = send_ref.shape[0]
    lanes = groups * STRIDE
    gathered = mm(two_pieces(all_traces(field_ref)), send_hot_ref[...])
    high, low = gathered[:TILE], gathered[TILE:]
    halo_ref[...] = fold_halves(high[:, lanes:] + low[:, lanes:])
    high, low = high[:, :lanes].astype(BF16), low[:, :lanes].astype(BF16)
    masks = [one_hot(codes == q) for q in range(8)]
    high_stack = jnp.concatenate([high * m for m in masks], axis=0)
    low_stack = jnp.concatenate([low * m for m in masks], axis=0)
    result = mm(tiles_ref[...], high_stack)
    result = result[:TILE] + (result[TILE:] + mm(tiles_ref[:TILE], low_stack))
    rows, plan = fold_plan(2 * cap)
    for group in range(groups):
        block = result[:, group // 2 * 128 : group // 2 * 128 + 128]
        base = group % 2 * STRIDE
        folded = [None] * (rows // 8)
        for row, count, column, width, to_row, to_lane in plan:
            for k in range(count // 8):
                part = roll_lanes(block[row + 8 * k : row + 8 * k + 8], to_lane - base - column)
                at = to_row // 8 + k
                if folded[at] is not None:
                    part = jnp.where(in_lanes(to_lane, width), part, folded[at])
                folded[at] = part
        send_ref[group] = jnp.concatenate(folded, axis=0)


def unpack_received(recv_ref, cap):
    rows, plan = fold_plan(2 * cap)
    blocks = []
    for pair in range(recv_ref.shape[0] // 2):
        wide = [None] * (TILE // 8)
        for side in range(2):
            block = recv_ref[2 * pair + side]
            base = side * STRIDE
            for row, count, column, width, to_row, to_lane in plan:
                for k in range(count // 8):
                    part = roll_lanes(
                        block[to_row + 8 * k : to_row + 8 * k + 8], base + column - to_lane
                    )
                    at = row // 8 + k
                    if wide[at] is not None:
                        part = jnp.where(in_lanes(base + column, width), part, wide[at])
                    wide[at] = part
        blocks.append(jnp.concatenate(wide, axis=0))
    return jnp.concatenate(blocks, axis=1)


def index_tables(cap, small, outq, inc, inq, coarse, band, plane, elements, sizes):
    gx_size, groups = sizes
    gx_index = lax.axis_index("gx")
    hang, halo = coarse.shape[1], band.shape[1]
    traces = FACES * elements
    as_f = lambda x: x.astype(F32)
    coarse_hot = one_hot(
        lax.broadcasted_iota(jnp.int32, (hang, inc.shape[1]), 0) == inc
    )
    pad = jnp.zeros((6, hang), F32)
    pick = mm(
        jnp.concatenate([as_f(coarse // 8), as_f(coarse % 8), pad], axis=0).astype(BF16),
        coarse_hot,
    )
    rows = jnp.concatenate(
        [
            as_f(small // 8),
            as_f(small % 8),
            jnp.where(inc < hang, pick[0:1], float(traces // 8)),
            jnp.where(inc < hang, pick[1:2], 0.0),
            as_f(outq),
            as_f(inq),
            as_f(inc),
            jnp.zeros_like(pick[0:1]),
        ],
        axis=0,
    ).astype(BF16)
    lane = lane_row(groups * STRIDE)
    group, within = lane // STRIDE, lane % STRIDE
    is_fine, is_used = within < cap, within < 2 * cap
    slot = group * cap + jnp.where(is_fine, within, within - cap)
    slots = lax.broadcasted_iota(jnp.int32, (rows.shape[1], lane.shape[1]), 0)
    placed = mm(rows, one_hot(slots == jnp.where(is_used, slot, -1))).astype(jnp.int32)
    send_id = jnp.where(
        is_fine, placed[0:1] * 8 + placed[1:2], placed[2:3] * 8 + placed[3:4]
    )
    send_id = jnp.where(is_used, send_id, traces)
    codes = jnp.where(is_fine, placed[4:5], 4 + placed[5:6])
    first_hang = traces + 4 * halo
    mortar = placed[6:7]
    recv_id = jnp.where(
        is_fine, jnp.where(mortar < hang, first_hang + mortar, -1), first_hang + hang + slot
    )
    recv_id = jnp.where(is_used, recv_id, -1)

    edge_lane = lane_row(128)
    target = jnp.where(edge_lane < 4 * halo, edge_lane % halo, -1)
    slots = lax.broadcasted_iota(jnp.int32, (halo, 128), 0)
    halo_rows = jnp.concatenate([as_f(plane), as_f(band), jnp.zeros((4, halo), F32)], axis=0)
    edge = mm(halo_rows.astype(BF16), one_hot(slots == target)).astype(jnp.int32)
    halo_id = jnp.zeros_like(edge_lane) + traces
    halo_recv = jnp.zeros_like(edge_lane) - 1
    present = (gx_index < gx_size - 1, gx_index > 0, True, True)
    starts = (traces + halo, traces, traces + 3 * halo, traces + 2 * halo)
    for face in range(4):
        here = edge_lane // halo == face
        halo_id = jnp.where(here, face * elements + edge[face : face + 1], halo_id)
        halo_recv = jnp.where(
            here & present[face], starts[face] + edge_lane - face * halo, halo_recv
        )
    send_id = jnp.concatenate([send_id, halo_id], axis=1)
    recv_id = jnp.concatenate([recv_id, halo_recv], axis=1)
    return send_id, codes, recv_id


class Refs:
    def __init__(self, plan, refs):
        arg_vmem, out_vmem = plan
        refs = list(refs)
        take = lambda n: [refs.pop(0) for _ in range(n)]
        args, outs = take(len(arg_vmem)), take(len(out_vmem))
        self.args = [a if v else refs.pop(0) for a, v in zip(args, arg_vmem)]
        self.outs = [o if v else refs.pop(0) for o, v in zip(outs, out_vmem)]
        in_sems, out_sems = take(2)
        self.work = refs
        self.pending = [
            None if v else pltpu.make_async_copy(a, b, in_sems.at[i])
            for i, (a, b, v) in enumerate(zip(args, self.args, arg_vmem))
        ]
        self.ships = [
            None if v else pltpu.make_async_copy(b, o, out_sems.at[i])
            for i, (o, b, v) in enumerate(zip(outs, self.outs, out_vmem))
        ]
        self.sent = []

    def start(self):
        for copy in self.pending:
            if copy is not None:
                copy.start()

    def get(self, i):
        if self.pending[i] is not None:
            self.pending[i].wait()
            self.pending[i] = None
        return self.args[i]

    def ship(self, i):
        if self.ships[i] is not None:
            self.ships[i].start()
            self.sent.append(self.ships[i])

    def finish(self):
        for copy in self.sent:
            copy.wait()


def start_kernel(sizes, plan, *refs):
    r = Refs(plan, refs)
    r.start()
    field, send, edge, send_hot, codes_ref, recv_id_ref, first2, final2 = r.outs
    elements = field.shape[1]
    groups = send.shape[0]
    small, outq, inc, inq, coarse, band, plane = [r.get(i) for i in range(7)]
    send_id, codes, recv_id = index_tables(
        small.shape[1] // groups,
        small[...],
        outq[...],
        inc[...],
        inq[...],
        coarse[...],
        band[0],
        plane[0],
        elements,
        sizes,
    )
    codes_ref[...] = jnp.broadcast_to(codes, codes_ref.shape)
    r.ship(4)
    recv_id_ref[...] = jnp.broadcast_to(recv_id, recv_id_ref.shape)
    r.ship(5)
    fill_send_hot(send_id, send_hot)
    r.ship(3)
    first2[0], first2[1] = split(r.get(7)[...])
    r.ship(6)
    final2[0], final2[1] = split(r.get(8)[...])
    r.ship(7)
    field[...] = solve_cells(r.get(9)[...], first2, final2, r.get(10))
    r.ship(0)
    pack_send(field, send_hot, codes, r.get(11), send, edge, small.shape[1] // groups)
    r.ship(1)
    r.ship(2)
    r.finish()


def local_part(
    field_ref, mass_ref, coupling_ref, flux_ref, adjacent_ref, volume_ref, local_ref
):
    elements = field_ref.shape[1]
    traces = all_traces(field_ref)
    columns = lax.broadcasted_iota(jnp.int32, (FACES * elements, elements), 0)
    stacked = two_pieces(traces)
    parts = []
    for a in range(VARS):
        flux = []
        for d in range(3):
            total = None
            for b in range(VARS):
                row = d * 25 + a * VARS + b
                term = flux_ref[row : row + 1, :] * field_ref[b * 64 : b * 64 + 64, :]
                total = term if total is None else total + term
            flux.append(total)
        parts.append(jnp.concatenate(flux, axis=0))
    derived = mm3(volume_ref[:64], volume_ref[64:], jnp.concatenate(parts, axis=1))
    for a in range(VARS):
        rows = slice(a * 64, a * 64 + 64)
        local_ref[rows, :] = (
            mass_ref[rows, :] * field_ref[rows, :]
            + derived[:, a * elements : (a + 1) * elements]
        )
    for f in range(FACES):
        near = mm(stacked, one_hot(columns == adjacent_ref[f : f + 1, :]))
        near = near[:TILE] + near[TILE:]
        own = traces[:, f * elements : (f + 1) * elements]
        add_to_face(
            local_ref, f, coupling_ref[f * TILE : (f + 1) * TILE, :] * (own - near)
        )


def hold(r, outs, args):
    copies = [
        pltpu.make_async_copy(r.args[arg], r.outs[out], r.work[0].at[n])
        for n, (out, arg) in enumerate(zip(outs, args))
    ]
    for copy in copies:
        copy.start()
    return copies


def fill_received_hot(ids, adjacent, hot_ref):
    elements = adjacent.shape[1]
    column = jnp.transpose(ids)[:, 0:1]
    for f in range(FACES):
        hot_ref[:, f * elements : (f + 1) * elements] = one_hot(column == adjacent[f : f + 1, :])


def prepare(r):
    local, recv_hot, coupling, first2 = r.outs[:4]
    copies = hold(r, (2, 3), (2, 7))
    r.start()
    fill_received_hot(r.get(6)[...], r.get(4), recv_hot)
    for copy in copies:
        copy.wait()
    local_part(r.get(0), r.get(1), coupling, r.get(3), r.get(4), r.get(5), local)


def first_local_kernel(plan, *refs):
    prepare(Refs(plan, refs))


def second_local_kernel(plan, *refs):
    r = Refs(plan, refs)
    prepare(r)
    k0, k1 = r.get(8)[...], r.get(0)[...]
    r.outs[4][...] = put(
        [(0, total_of(k0 * k0)), (1, total_of(k0 * k1)), (2, total_of(k1 * k1))]
    )


def total_of(x):
    return jnp.sum(jnp.sum(x, axis=0, keepdims=True), axis=1, keepdims=True)


def put(values):
    lane = lane_row(128)
    row = jnp.zeros((1, 128), F32)
    for position, value in values:
        row = jnp.where(lane == position, value, row)
    return row


def fill_send_hot(send_id, hot_ref):
    columns = lax.broadcasted_iota(jnp.int32, hot_ref.shape, 0)
    hot_ref[...] = one_hot(columns == send_id)


def finish_product(sizes, r, work_ref):
    cap, halo = sizes
    upper, lower, after, before = [r.get(i)[...] for i in range(1, 5)]
    face = lane_row(128) % STRIDE // halo
    edge = jnp.where(
        face < 2, jnp.where(face < 1, upper, lower), jnp.where(face < 3, after, before)
    )
    received = jnp.concatenate([unpack_received(r.get(0), cap), unfold_halves(edge)], axis=1)
    near = mm(two_pieces(received), r.get(5)[...])
    near = near[:TILE] + near[TILE:]
    coupling, local = r.get(6), r.get(7)
    elements = local.shape[1]
    work_ref[...] = local[...]
    for f in range(FACES):
        add_to_face(
            work_ref,
            f,
            -coupling[f * TILE : (f + 1) * TILE, :] * near[:, f * elements : (f + 1) * elements],
        )
    first = r.get(8)
    inner = mm3(first[0], first[1], work_ref[...])
    final = r.get(10)
    return mm3(final[0], final[1], r.get(9)[...] * inner)


def middle_kernel(sizes, plan, *refs):
    r = Refs(plan, refs)
    r.start()
    field, send, edge = r.outs
    field[...] = finish_product(sizes, r, r.work[0])
    r.ship(0)
    pack_send(field, r.get(11), r.get(12)[0:1, :], r.get(13), send, edge, sizes[0])
    r.ship(1)
    r.ship(2)
    r.finish()


def last_kernel(sizes, plan, *refs):
    r = Refs(plan, refs)
    work = r.work[1]
    fills = hold(r, (1, 2), (11, 12))
    r.start()
    rows, k0, k1 = r.outs
    k2 = K2_SCALE * finish_product(sizes, r, work)
    for fill in fills:
        fill.wait()
    row = r.get(13)[...] + put(
        [
            (3, total_of(k2 * k0[...])),
            (4, total_of(k2 * k1[...])),
            (5, total_of(k2 * k2)),
        ]
    )
    rows[...] = jnp.broadcast_to(row.reshape(1, 1, 128), rows.shape)


def combine_kernel(plan, *refs):
    r = Refs(plan, refs)
    r.start()
    rows_ref = r.get(0)
    totals = jnp.sum(rows_ref[:, 0, :], axis=0, keepdims=True)
    lane = lane_row(128)
    g00, g01, g11, g02, g12, g22 = [
        jnp.sum(jnp.where(lane == i, totals, 0.0), axis=1, keepdims=True) for i in range(6)
    ]
    scale = 1.0 / K2_SCALE
    beta = jnp.sqrt(g00 + EPS)
    n00, n01, n11 = g00 / beta / beta, g01 / beta / beta, g11 / beta / beta
    h00 = n01
    w_sq = jnp.maximum(n11 - 2.0 * h00 * n01 + h00 * h00 * n00, 0.0)
    h10 = jnp.sqrt(w_sq + EPS)
    unit = beta * h10
    s = scale / unit
    t = h00 * K2_SCALE
    x0 = (g02 - t * g01) * s / beta
    x1 = ((g12 - t * g11) * s - h00 * ((g02 - t * g01) * s)) / unit
    xx = (((g22 - t * g12) - t * (g12 - t * g11)) * s) * s
    v01 = (n01 - h00 * n00) / h10
    v11 = w_sq / h10 / h10
    h01 = x0
    h11 = x1 - h01 * v01
    rest = xx - 2.0 * h01 * x0 + h01 * h01 * n00
    rest = rest - 2.0 * h11 * h11 + h11 * h11 * v11
    h21 = jnp.sqrt(jnp.maximum(rest, 0.0) + EPS)
    radius0 = jnp.sqrt(h00 * h00 + h10 * h10)
    c0, s0 = h00 / radius0, h10 / radius0
    target1 = -s0 * beta
    target0 = c0 * beta
    upper = c0 * h01 + s0 * h11
    lower = c0 * h11 - s0 * h01
    radius1 = jnp.sqrt(lower * lower + h21 * h21)
    y1 = (lower / radius1) * target1 / radius1
    y0 = (target0 - upper * y1) / radius0
    along1 = y1 / unit
    along0 = y0 / beta - along1 * h00
    r.outs[0][...] = along0 * r.get(1)[...] + along1 * r.get(2)[...]
    r.ship(0)
    r.finish()


def call(kernel, outs, args, arg_spaces=None, out_spaces=None, scratch=()):
    arg_spaces = arg_spaces or "h" * len(args)
    out_spaces = out_spaces or "h" * len(outs)
    space = lambda c: pltpu.VMEM if c == "v" else pltpu.HBM
    plan = (tuple(c != "h" for c in arg_spaces), tuple(c != "h" for c in out_spaces))
    buffers = [
        pltpu.VMEM(a.shape, a.dtype)
        for a, c in zip(tuple(args) + tuple(outs), arg_spaces + out_spaces)
        if c == "h"
    ]
    buffers += [pltpu.SemaphoreType.DMA((len(args),)), pltpu.SemaphoreType.DMA((len(outs),))]
    return pl.pallas_call(
        functools.partial(kernel, plan),
        out_shape=tuple(space(c)(o.shape, o.dtype) for o, c in zip(outs, out_spaces)),
        in_specs=[pl.BlockSpec(memory_space=space(c)) for c in arg_spaces],
        out_specs=tuple(pl.BlockSpec(memory_space=space(c)) for c in out_spaces),
        scratch_shapes=buffers + list(scratch),
        cost_estimate=pl.CostEstimate(
            flops=10**9,
            bytes_accessed=sum(a.size * a.dtype.itemsize for a in args),
            transcendentals=0,
        ),
        compiler_params=pltpu.CompilerParams(vmem_limit_bytes=VMEM_LIMIT),
    )(*[pltpu.with_memory_space_constraint(a, space(c)) for a, c in zip(args, arg_spaces)])


def on_device(
    source,
    mass,
    coupling,
    flux,
    first,
    final,
    mid,
    adjacent,
    plane,
    band,
    small,
    proprietor,
    outq,
    inc,
    inq,
    coarse,
):
    del proprietor
    tiles, volume = constant_matrices()
    gx_size, groups = lax.axis_size("gx"), lax.axis_size("yz")
    elements = source.shape[1]
    traces = FACES * elements
    lanes = groups * STRIDE
    cap, halo = small.shape[1] // groups, plane.shape[2]
    struct = jax.ShapeDtypeStruct
    field = struct((DOFS, elements), F32)
    send = struct((groups, fold_plan(2 * cap)[0], 128), F32)
    edge = struct((TILE // 2, 128), F32)

    k0, send0, edge0, send_hot, codes, recv_id, first2, final2 = call(
        functools.partial(start_kernel, (gx_size, groups)),
        (
            field,
            send,
            edge,
            struct((traces, lanes + 128), BF16),
            struct((8, lanes), jnp.int32),
            struct((8, lanes + 128), jnp.int32),
            struct((2, DOFS, DOFS), BF16),
            struct((2, DOFS, DOFS), BF16),
        ),
        (small, outq, inc, inq, coarse, band, plane, first, final, source, mid, tiles),
        out_spaces="hhvhhhhh",
    )

    up = [(i, i + 1) for i in range(gx_size - 1)]
    down = [(j, i) for i, j in up]
    ring = [(i, (i + 1) % groups) for i in range(groups)]
    back = [(j, i) for i, j in ring]

    def exchange(send, edge):
        if gx_size == 2:
            upper = lower = lax.ppermute(edge, "gx", up + down)
        else:
            upper, lower = lax.ppermute(edge, "gx", down), lax.ppermute(edge, "gx", up)
        before, after = lax.ppermute(edge, "yz", ring), lax.ppermute(edge, "yz", back)
        return lax.all_to_all(send, "yz", 0, 0, tiled=True), upper, lower, after, before

    came = exchange(send0, edge0)
    copy_sems = pltpu.SemaphoreType.DMA((2,))
    work = pltpu.VMEM((DOFS, elements), F32)
    held = (
        field,
        struct((lanes + 128, traces), BF16),
        struct(coupling.shape, F32),
        struct(first2.shape, BF16),
    )
    local_args = lambda u: (u, mass, coupling, flux, adjacent, volume, recv_id, first2)
    local, recv_hot, near_coupling, near_first = call(
        first_local_kernel, held, local_args(k0), "hhrhhhhr", "vvvv", scratch=[copy_sems]
    )
    k1, send1, edge1 = call(
        functools.partial(middle_kernel, (cap, halo)),
        (field, send, edge),
        came
        + (recv_hot, near_coupling, local, near_first)
        + (mid, final2, send_hot, codes, tiles),
        "vvvvvvvvvhhhhh",
        "hhv",
        scratch=[work],
    )
    came = exchange(send1, edge1)
    local, recv_hot, near_coupling, near_first, partial = call(
        second_local_kernel,
        held + (struct((1, 128), F32),),
        local_args(k1) + (k0,),
        "hhrhhhhrh",
        "vvvvv",
        scratch=[copy_sems],
    )
    rows, k0, k1 = call(
        functools.partial(last_kernel, (cap, halo)),
        (struct((gx_size * groups, 1, 128), F32), field, field),
        came
        + (recv_hot, near_coupling, local, near_first)
        + (mid, final2, k0, k1, partial),
        "vvvvvvvvvhhrrv",
        "vvv",
        scratch=[copy_sems, work],
    )
    rows = lax.all_to_all(rows, ("gx", "yz"), 0, 0, tiled=True)
    (update,) = call(combine_kernel, (field,), (rows, k0, k1), "vvv")
    return update


def solution(mesh):
    by_column = P(None, ("gx", "yz"))
    by_row = P(("gx", "yz"), None)
    by_plane = P(("gx", "yz"), None, None)
    return jax.shard_map(
        on_device,
        mesh=mesh,
        in_specs=(by_column,) * 4
        + (P(), P())
        + (by_column,) * 2
        + (by_plane,) * 2
        + (by_row,) * 6,
        out_specs=by_column,
        check_vma=False,
    )
```

```python
import functools

import jax
import jax.numpy as jnp
import numpy as np
from jax import lax
from jax.experimental import pallas as pl
from jax.experimental.pallas import tpu as pltpu
from jax.sharding import PartitionSpec as P

EPS = 1e-06
NODES = 4
VARS = 5
TILE = VARS * NODES * NODES
DOFS = TILE * NODES
FACES = 6
FOLD = 64
K2_SCALE = 2.0**-20
VMEM_LIMIT = 40 * 2**20
F32 = jnp.float32
BF16 = jnp.bfloat16


def gll_tables():
    root = 1.0 / np.sqrt(5.0)
    points = np.array([-1.0, -root, root, 1.0])
    weights = np.array([1.0, 5.0, 5.0, 1.0]) / 6.0

    def lagrange(at):
        values = np.ones((len(at), 4))
        for j in range(4):
            for m in range(4):
                if m != j:
                    values[:, j] = values[:, j] * (at - points[m]) / (points[j] - points[m])
        return values

    derivative = np.zeros((4, 4))
    for i in range(4):
        for j in range(4):
            total = 0.0
            for m in range(4):
                if m != j:
                    term = 1.0 / (points[j] - points[m])
                    for n in range(4):
                        if n != j and n != m:
                            term = term * (points[i] - points[n]) / (points[j] - points[n])
                    total = total + term
            derivative[i, j] = total
    halves = [lagrange((points - 1.0) / 2.0), lagrange((points + 1.0) / 2.0)]
    projections = [0.5 * (1.0 / weights)[:, None] * h.T * weights[None, :] for h in halves]
    interpolate = [np.kron(halves[q // 2], halves[q % 2]) for q in range(4)]
    project = [np.kron(projections[q // 2], projections[q % 2]) for q in range(4)]
    return derivative, interpolate, project


def pieces(matrix):
    value = np.asarray(matrix, np.float32)
    high = value.astype(jnp.bfloat16)
    low = (value - high.astype(np.float32)).astype(jnp.bfloat16)
    return high, low


def constant_matrices():
    derivative, interpolate, project = gll_tables()
    eye_vars = np.eye(VARS)
    blocks = [np.kron(eye_vars, m) for m in project + interpolate]
    tiles = np.concatenate(pieces(np.concatenate(blocks, axis=1)), axis=0)
    eye = np.eye(4)
    volume = np.concatenate(
        [
            np.kron(derivative, np.kron(eye, eye)),
            np.kron(eye, np.kron(derivative, eye)),
            np.kron(eye, np.kron(eye, derivative)),
        ],
        axis=1,
    )
    volume = np.concatenate(pieces(volume), axis=0)
    return jnp.asarray(tiles), jnp.asarray(volume)


def split(x):
    high = x.astype(BF16)
    low = (x - high.astype(F32)).astype(BF16)
    return high, low


def mm(a, b):
    return jnp.dot(a, b, preferred_element_type=F32)


def mm3(a_high, a_low, b):
    columns = b.shape[1]
    b_high, b_low = split(b)
    first = mm(a_high, jnp.concatenate([b_high, b_low], axis=1))
    return first[:, :columns] + (first[:, columns:] + mm(a_low, b_high))


def solve_cells(x, first_ref, final_ref, mid_ref):
    inner = mm3(first_ref[0], first_ref[1], x)
    return mm3(final_ref[0], final_ref[1], mid_ref[...] * inner)


def face_rows(ref, face):
    end = NODES - 1 if face % 2 else 0
    if face // 2 == 0:
        return jnp.concatenate(
            [ref[pl.ds(a * 64 + end * 16, 16), :] for a in range(VARS)], axis=0
        )
    if face // 2 == 1:
        return jnp.concatenate(
            [ref[pl.ds(g * 16 + end * 4, 4), :] for g in range(VARS * 4)], axis=0
        )
    return ref[pl.ds(end, TILE, stride=4), :]


def add_to_face(ref, face, value):
    end = NODES - 1 if face % 2 else 0
    if face // 2 == 0:
        for a in range(VARS):
            ref[pl.ds(a * 64 + end * 16, 16), :] += value[a * 16 : a * 16 + 16]
    elif face // 2 == 1:
        for g in range(VARS * 4):
            ref[pl.ds(g * 16 + end * 4, 4), :] += value[g * 4 : g * 4 + 4]
    else:
        ref[pl.ds(end, TILE, stride=4), :] += value


def all_traces(ref):
    return jnp.concatenate([face_rows(ref, f) for f in range(FACES)], axis=1)


def two_pieces(x):
    high, low = split(x)
    return jnp.concatenate([high, low], axis=0)


def one_hot(condition):
    return jnp.where(condition, 1.0, 0.0).astype(BF16)


def lane_row(length):
    return lax.broadcasted_iota(jnp.int32, (1, length), 1)


def fold_plan(columns):
    for rows in range(8, TILE + 1, 8):
        full, rest = TILE // rows, TILE % rows
        parts = rows // rest if rest else 1
        width = -(-columns // parts) if rest else 0
        if full * columns + width <= 128:
            break
    plan = [(g * rows, rows, 0, columns, 0, g * columns) for g in range(full)]
    if rest:
        for part in range(parts):
            count = min(width, columns - part * width)
            if count > 0:
                plan.append(
                    (full * rows, rest, part * width, count, part * rest, full * columns)
                )
    return rows, plan


def table_lanes(groups, cap, halo):
    return -(-(groups * 2 * cap + 4 * halo) // 128) * 128


def roll_lanes(x, shift):
    return pltpu.roll(x, shift % 128, 1) if shift % 128 else x


def in_lanes(start, count):
    lane = lane_row(128)
    return (lane >= start) & (lane < start + count)


def window(x, start, width, to):
    block, offset = start // 128, start % 128
    value = roll_lanes(x[:, block * 128 : block * 128 + 128], to - offset)
    if offset + width > 128:
        after = roll_lanes(x[:, block * 128 + 128 : block * 128 + 256], to - offset)
        value = jnp.where(lane_row(128) < to + 128 - offset, value, after)
    return value


def fold_halves(block):
    middle = TILE // 2
    return jnp.where(
        lane_row(128) < FOLD, block[:middle], roll_lanes(block[middle:], FOLD)
    )


def unfold_halves(block):
    return jnp.concatenate([block, roll_lanes(block, FOLD)], axis=0)


def pack_send(field_ref, send_hot_ref, codes, tiles_ref, send_ref, edge_ref, sizes):
    cap, halo = sizes
    groups = send_ref.shape[0]
    gathered = mm(two_pieces(all_traces(field_ref)), send_hot_ref[...])
    high, low = gathered[:TILE], gathered[TILE:]
    first_edge = groups * 2 * cap
    from_block = first_edge // 128 * 128
    edges = high[:, from_block:] + low[:, from_block:]
    edge_ref[...] = fold_halves(window(edges, first_edge - from_block, 4 * halo, 0))
    high, low = high.astype(BF16), low.astype(BF16)
    masks = [one_hot(codes == q) for q in range(8)]
    high_stack = jnp.concatenate([high * m for m in masks], axis=0)
    low_stack = jnp.concatenate([low * m for m in masks], axis=0)
    result = mm(tiles_ref[...], high_stack)
    result = result[:TILE] + (result[TILE:] + mm(tiles_ref[:TILE], low_stack))
    rows, plan = fold_plan(2 * cap)
    for group in range(groups):
        folded = [None] * (rows // 8)
        for row, count, column, width, to_row, to_lane in plan:
            part = window(
                result[row : row + count], group * 2 * cap + column, width, to_lane
            )
            for k in range(count // 8):
                at, value = to_row // 8 + k, part[8 * k : 8 * k + 8]
                if folded[at] is not None:
                    value = jnp.where(in_lanes(to_lane, width), value, folded[at])
                folded[at] = value
        send_ref[group] = jnp.concatenate(folded, axis=0)


def unpack_received(recv_ref, edge, sizes):
    cap, halo = sizes
    groups = recv_ref.shape[0]
    plan = fold_plan(2 * cap)[1]
    wide = [[None] * (TILE // 8) for _ in range(table_lanes(groups, cap, halo) // 128)]

    def lay(value, row, count, start, width, from_lane):
        offset = start % 128
        value = roll_lanes(value, offset - from_lane)
        for block, low, high in (
            (start // 128, offset, min(128, offset + width)),
            (start // 128 + 1, 0, offset + width - 128),
        ):
            for k in range(count // 8 if high > low else 0):
                part, held = value[8 * k : 8 * k + 8], wide[block][row // 8 + k]
                if held is not None:
                    part = jnp.where(in_lanes(low, high - low), part, held)
                wide[block][row // 8 + k] = part

    for group in range(groups):
        block = recv_ref[group]
        for row, count, column, width, to_row, to_lane in plan:
            start = group * 2 * cap + column
            lay(block[to_row : to_row + count], row, count, start, width, to_lane)
    lay(unfold_halves(edge), 0, TILE, groups * 2 * cap, 4 * halo, 0)
    return jnp.concatenate([jnp.concatenate(w, axis=0) for w in wide], axis=1)


def index_tables(cap, small, outq, inc, inq, coarse, band, plane, elements, sizes):
    gx_size, groups = sizes
    gx_index = lax.axis_index("gx")
    hang, halo = coarse.shape[1], band.shape[1]
    traces = FACES * elements
    as_f = lambda x: x.astype(F32)
    coarse_hot = one_hot(
        lax.broadcasted_iota(jnp.int32, (hang, inc.shape[1]), 0) == inc
    )
    pad = jnp.zeros((6, hang), F32)
    pick = mm(
        jnp.concatenate([as_f(coarse // 8), as_f(coarse % 8), pad], axis=0).astype(BF16),
        coarse_hot,
    )
    rows = jnp.concatenate(
        [
            as_f(small // 8),
            as_f(small % 8),
            jnp.where(inc < hang, pick[0:1], float(traces // 8)),
            jnp.where(inc < hang, pick[1:2], 0.0),
            as_f(outq),
            as_f(inq),
            as_f(inc),
            jnp.zeros_like(pick[0:1]),
        ],
        axis=0,
    ).astype(BF16)
    lane = lane_row(table_lanes(groups, cap, halo))
    group, within = lane // (2 * cap), lane % (2 * cap)
    is_tile, is_fine = lane < groups * 2 * cap, within < cap
    slot = group * cap + jnp.where(is_fine, within, within - cap)
    slots = lax.broadcasted_iota(jnp.int32, (rows.shape[1], lane.shape[1]), 0)
    placed = mm(rows, one_hot(slots == jnp.where(is_tile, slot, -1))).astype(jnp.int32)
    edge_lane = lane - groups * 2 * cap
    is_edge = (edge_lane >= 0) & (edge_lane < 4 * halo)
    face = edge_lane // halo
    slots = lax.broadcasted_iota(jnp.int32, (halo, lane.shape[1]), 0)
    edge_rows = jnp.concatenate([as_f(plane), as_f(band), jnp.zeros((4, halo), F32)], axis=0)
    edge = mm(
        edge_rows.astype(BF16), one_hot(slots == jnp.where(is_edge, edge_lane % halo, -1))
    ).astype(jnp.int32)
    tile_id = jnp.where(
        is_fine, placed[0:1] * 8 + placed[1:2], placed[2:3] * 8 + placed[3:4]
    )
    send_id = jnp.where(is_tile, tile_id, traces)
    codes = jnp.where(is_tile, jnp.where(is_fine, placed[4:5], 4 + placed[5:6]), 8)
    first_hang = traces + 4 * halo
    mortar = placed[6:7]
    tile_recv = jnp.where(
        is_fine, jnp.where(mortar < hang, first_hang + mortar, -1), first_hang + hang + slot
    )
    recv_id = jnp.where(is_tile, tile_recv, -1)
    present = (gx_index < gx_size - 1, gx_index > 0, True, True)
    starts = (traces + halo, traces, traces + 3 * halo, traces + 2 * halo)
    for f in range(4):
        here = is_edge & (face == f)
        send_id = jnp.where(here, f * elements + edge[f : f + 1], send_id)
        recv_id = jnp.where(here & present[f], starts[f] + edge_lane - f * halo, recv_id)
    return send_id, codes, recv_id


class Refs:
    def __init__(self, plan, refs):
        arg_vmem, out_vmem = plan
        refs = list(refs)
        take = lambda n: [refs.pop(0) for _ in range(n)]
        args, outs = take(len(arg_vmem)), take(len(out_vmem))
        self.args = [a if v else refs.pop(0) for a, v in zip(args, arg_vmem)]
        self.outs = [o if v else refs.pop(0) for o, v in zip(outs, out_vmem)]
        in_sems, out_sems = take(2)
        self.work = refs
        self.pending = [
            None if v else pltpu.make_async_copy(a, b, in_sems.at[i])
            for i, (a, b, v) in enumerate(zip(args, self.args, arg_vmem))
        ]
        self.ships = [
            None if v else pltpu.make_async_copy(b, o, out_sems.at[i])
            for i, (o, b, v) in enumerate(zip(outs, self.outs, out_vmem))
        ]
        self.sent = []

    def start(self):
        for copy in self.pending:
            if copy is not None:
                copy.start()

    def get(self, i):
        if self.pending[i] is not None:
            self.pending[i].wait()
            self.pending[i] = None
        return self.args[i]

    def ship(self, i):
        if self.ships[i] is not None:
            self.ships[i].start()
            self.sent.append(self.ships[i])

    def finish(self):
        for copy in self.sent:
            copy.wait()


def start_kernel(sizes, plan, *refs):
    r = Refs(plan, refs)
    r.start()
    field, send, edge, send_hot, codes_ref, recv_id_ref, first2, final2 = r.outs
    elements = field.shape[1]
    groups = send.shape[0]
    small, outq, inc, inq, coarse, band, plane = [r.get(i) for i in range(7)]
    send_id, codes, recv_id = index_tables(
        small.shape[1] // groups,
        small[...],
        outq[...],
        inc[...],
        inq[...],
        coarse[...],
        band[0],
        plane[0],
        elements,
        sizes,
    )
    codes_ref[...] = jnp.broadcast_to(codes, codes_ref.shape)
    r.ship(4)
    recv_id_ref[...] = jnp.broadcast_to(recv_id, recv_id_ref.shape)
    r.ship(5)
    fill_send_hot(send_id, send_hot)
    r.ship(3)
    first2[0], first2[1] = split(r.get(7)[...])
    r.ship(6)
    final2[0], final2[1] = split(r.get(8)[...])
    r.ship(7)
    field[...] = solve_cells(r.get(9)[...], first2, final2, r.get(10))
    r.ship(0)
    tile_sizes = (small.shape[1] // groups, plane.shape[2])
    pack_send(field, send_hot, codes, r.get(11), send, edge, tile_sizes)
    r.ship(1)
    r.ship(2)
    r.finish()


def local_part(
    field_ref, mass_ref, coupling_ref, flux_ref, adjacent_ref, volume_ref, local_ref
):
    elements = field_ref.shape[1]
    traces = all_traces(field_ref)
    columns = lax.broadcasted_iota(jnp.int32, (FACES * elements, elements), 0)
    stacked = two_pieces(traces)
    parts = []
    for a in range(VARS):
        flux = []
        for d in range(3):
            total = None
            for b in range(VARS):
                row = d * 25 + a * VARS + b
                term = flux_ref[row : row + 1, :] * field_ref[b * 64 : b * 64 + 64, :]
                total = term if total is None else total + term
            flux.append(total)
        parts.append(jnp.concatenate(flux, axis=0))
    derived = mm3(volume_ref[:64], volume_ref[64:], jnp.concatenate(parts, axis=1))
    for a in range(VARS):
        rows = slice(a * 64, a * 64 + 64)
        local_ref[rows, :] = (
            mass_ref[rows, :] * field_ref[rows, :]
            + derived[:, a * elements : (a + 1) * elements]
        )
    for f in range(FACES):
        near = mm(stacked, one_hot(columns == adjacent_ref[f : f + 1, :]))
        near = near[:TILE] + near[TILE:]
        own = traces[:, f * elements : (f + 1) * elements]
        add_to_face(
            local_ref, f, coupling_ref[f * TILE : (f + 1) * TILE, :] * (own - near)
        )


def hold(r, outs, args):
    copies = [
        pltpu.make_async_copy(r.args[arg], r.outs[out], r.work[0].at[n])
        for n, (out, arg) in enumerate(zip(outs, args))
    ]
    for copy in copies:
        copy.start()
    return copies


def fill_received_hot(ids, adjacent, hot_ref):
    elements = adjacent.shape[1]
    column = jnp.transpose(ids)[:, 0:1]
    for f in range(FACES):
        hot_ref[:, f * elements : (f + 1) * elements] = one_hot(column == adjacent[f : f + 1, :])


def prepare(r):
    local, recv_hot, coupling, first2 = r.outs[:4]
    copies = hold(r, (2, 3), (2, 7))
    r.start()
    fill_received_hot(r.get(6)[...], r.get(4), recv_hot)
    for copy in copies:
        copy.wait()
    local_part(r.get(0), r.get(1), coupling, r.get(3), r.get(4), r.get(5), local)


def first_local_kernel(plan, *refs):
    prepare(Refs(plan, refs))


def second_local_kernel(plan, *refs):
    r = Refs(plan, refs)
    prepare(r)
    k0, k1 = r.get(8)[...], r.get(0)[...]
    r.outs[4][...] = put(
        [(0, total_of(k0 * k0)), (1, total_of(k0 * k1)), (2, total_of(k1 * k1))]
    )


def total_of(x):
    return jnp.sum(jnp.sum(x, axis=0, keepdims=True), axis=1, keepdims=True)


def put(values):
    lane = lane_row(128)
    row = jnp.zeros((1, 128), F32)
    for position, value in values:
        row = jnp.where(lane == position, value, row)
    return row


def fill_send_hot(send_id, hot_ref):
    columns = lax.broadcasted_iota(jnp.int32, hot_ref.shape, 0)
    hot_ref[...] = one_hot(columns == send_id)


def finish_product(sizes, r, work_ref):
    halo = sizes[1]
    upper, lower, after, before = [r.get(i)[...] for i in range(1, 5)]
    face = lane_row(128) % FOLD // halo
    edge = jnp.where(
        face < 2, jnp.where(face < 1, upper, lower), jnp.where(face < 3, after, before)
    )
    received = unpack_received(r.get(0), edge, sizes)
    near = mm(two_pieces(received), r.get(5)[...])
    near = near[:TILE] + near[TILE:]
    coupling, local = r.get(6), r.get(7)
    elements = local.shape[1]
    work_ref[...] = local[...]
    for f in range(FACES):
        add_to_face(
            work_ref,
            f,
            -coupling[f * TILE : (f + 1) * TILE, :] * near[:, f * elements : (f + 1) * elements],
        )
    first = r.get(8)
    inner = mm3(first[0], first[1], work_ref[...])
    final = r.get(10)
    return mm3(final[0], final[1], r.get(9)[...] * inner)


def middle_kernel(sizes, plan, *refs):
    r = Refs(plan, refs)
    r.start()
    field, send, edge = r.outs
    field[...] = finish_product(sizes, r, r.work[0])
    r.ship(0)
    pack_send(field, r.get(11), r.get(12)[0:1, :], r.get(13), send, edge, sizes)
    r.ship(1)
    r.ship(2)
    r.finish()


def last_kernel(sizes, plan, *refs):
    r = Refs(plan, refs)
    work = r.work[1]
    fills = hold(r, (1, 2), (11, 12))
    r.start()
    rows, k0, k1 = r.outs
    k2 = K2_SCALE * finish_product(sizes, r, work)
    for fill in fills:
        fill.wait()
    row = r.get(13)[...] + put(
        [
            (3, total_of(k2 * k0[...])),
            (4, total_of(k2 * k1[...])),
            (5, total_of(k2 * k2)),
        ]
    )
    rows[...] = jnp.broadcast_to(row.reshape(1, 1, 128), rows.shape)


def combine_kernel(plan, *refs):
    r = Refs(plan, refs)
    r.start()
    rows_ref = r.get(0)
    totals = jnp.sum(rows_ref[:, 0, :], axis=0, keepdims=True)
    lane = lane_row(128)
    g00, g01, g11, g02, g12, g22 = [
        jnp.sum(jnp.where(lane == i, totals, 0.0), axis=1, keepdims=True) for i in range(6)
    ]
    scale = 1.0 / K2_SCALE
    beta = jnp.sqrt(g00 + EPS)
    n00, n01, n11 = g00 / beta / beta, g01 / beta / beta, g11 / beta / beta
    h00 = n01
    w_sq = jnp.maximum(n11 - 2.0 * h00 * n01 + h00 * h00 * n00, 0.0)
    h10 = jnp.sqrt(w_sq + EPS)
    unit = beta * h10
    s = scale / unit
    t = h00 * K2_SCALE
    x0 = (g02 - t * g01) * s / beta
    x1 = ((g12 - t * g11) * s - h00 * ((g02 - t * g01) * s)) / unit
    xx = (((g22 - t * g12) - t * (g12 - t * g11)) * s) * s
    v01 = (n01 - h00 * n00) / h10
    v11 = w_sq / h10 / h10
    h01 = x0
    h11 = x1 - h01 * v01
    rest = xx - 2.0 * h01 * x0 + h01 * h01 * n00
    rest = rest - 2.0 * h11 * h11 + h11 * h11 * v11
    h21 = jnp.sqrt(jnp.maximum(rest, 0.0) + EPS)
    radius0 = jnp.sqrt(h00 * h00 + h10 * h10)
    c0, s0 = h00 / radius0, h10 / radius0
    target1 = -s0 * beta
    target0 = c0 * beta
    upper = c0 * h01 + s0 * h11
    lower = c0 * h11 - s0 * h01
    radius1 = jnp.sqrt(lower * lower + h21 * h21)
    y1 = (lower / radius1) * target1 / radius1
    y0 = (target0 - upper * y1) / radius0
    along1 = y1 / unit
    along0 = y0 / beta - along1 * h00
    r.outs[0][...] = along0 * r.get(1)[...] + along1 * r.get(2)[...]
    r.ship(0)
    r.finish()


def call(kernel, outs, args, arg_spaces=None, out_spaces=None, scratch=()):
    arg_spaces = arg_spaces or "h" * len(args)
    out_spaces = out_spaces or "h" * len(outs)
    space = lambda c: pltpu.VMEM if c == "v" else pltpu.HBM
    plan = (tuple(c != "h" for c in arg_spaces), tuple(c != "h" for c in out_spaces))
    buffers = [
        pltpu.VMEM(a.shape, a.dtype)
        for a, c in zip(tuple(args) + tuple(outs), arg_spaces + out_spaces)
        if c == "h"
    ]
    buffers += [pltpu.SemaphoreType.DMA((len(args),)), pltpu.SemaphoreType.DMA((len(outs),))]
    return pl.pallas_call(
        functools.partial(kernel, plan),
        out_shape=tuple(space(c)(o.shape, o.dtype) for o, c in zip(outs, out_spaces)),
        in_specs=[pl.BlockSpec(memory_space=space(c)) for c in arg_spaces],
        out_specs=tuple(pl.BlockSpec(memory_space=space(c)) for c in out_spaces),
        scratch_shapes=buffers + list(scratch),
        cost_estimate=pl.CostEstimate(
            flops=10**9,
            bytes_accessed=sum(a.size * a.dtype.itemsize for a in args),
            transcendentals=0,
        ),
        compiler_params=pltpu.CompilerParams(vmem_limit_bytes=VMEM_LIMIT),
    )(*[pltpu.with_memory_space_constraint(a, space(c)) for a, c in zip(args, arg_spaces)])


def on_device(
    source,
    mass,
    coupling,
    flux,
    first,
    final,
    mid,
    adjacent,
    plane,
    band,
    small,
    proprietor,
    outq,
    inc,
    inq,
    coarse,
):
    del proprietor
    tiles, volume = constant_matrices()
    gx_size, groups = lax.axis_size("gx"), lax.axis_size("yz")
    elements = source.shape[1]
    traces = FACES * elements
    cap, halo = small.shape[1] // groups, plane.shape[2]
    lanes = table_lanes(groups, cap, halo)
    struct = jax.ShapeDtypeStruct
    field = struct((DOFS, elements), F32)
    send = struct((groups, fold_plan(2 * cap)[0], 128), F32)
    edge = struct((TILE // 2, 128), F32)

    k0, send0, edge0, send_hot, codes, recv_id, first2, final2 = call(
        functools.partial(start_kernel, (gx_size, groups)),
        (
            field,
            send,
            edge,
            struct((traces, lanes), BF16),
            struct((8, lanes), jnp.int32),
            struct((8, lanes), jnp.int32),
            struct((2, DOFS, DOFS), BF16),
            struct((2, DOFS, DOFS), BF16),
        ),
        (small, outq, inc, inq, coarse, band, plane, first, final, source, mid, tiles),
        out_spaces="hhvhhhhh",
    )

    up = [(i, i + 1) for i in range(gx_size - 1)]
    down = [(j, i) for i, j in up]
    ring = [(i, (i + 1) % groups) for i in range(groups)]
    back = [(j, i) for i, j in ring]

    def exchange(send, edge):
        if gx_size == 2:
            upper = lower = lax.ppermute(edge, "gx", up + down)
        else:
            upper, lower = lax.ppermute(edge, "gx", down), lax.ppermute(edge, "gx", up)
        before, after = lax.ppermute(edge, "yz", ring), lax.ppermute(edge, "yz", back)
        return lax.all_to_all(send, "yz", 0, 0, tiled=True), upper, lower, after, before

    came = exchange(send0, edge0)
    copy_sems = pltpu.SemaphoreType.DMA((2,))
    work = pltpu.VMEM((DOFS, elements), F32)
    held = (
        field,
        struct((lanes, traces), BF16),
        struct(coupling.shape, F32),
        struct(first2.shape, BF16),
    )
    local_args = lambda u: (u, mass, coupling, flux, adjacent, volume, recv_id, first2)
    local, recv_hot, near_coupling, near_first = call(
        first_local_kernel, held, local_args(k0), "hhrhhhhr", "vvvv", scratch=[copy_sems]
    )
    k1, send1, edge1 = call(
        functools.partial(middle_kernel, (cap, halo)),
        (field, send, edge),
        came
        + (recv_hot, near_coupling, local, near_first)
        + (mid, final2, send_hot, codes, tiles),
        "vvvvvvvvvhhhhh",
        "hhv",
        scratch=[work],
    )
    came = exchange(send1, edge1)
    local, recv_hot, near_coupling, near_first, partial = call(
        second_local_kernel,
        held + (struct((1, 128), F32),),
        local_args(k1) + (k0,),
        "hhrhhhhrh",
        "vvvvv",
        scratch=[copy_sems],
    )
    rows, k0, k1 = call(
        functools.partial(last_kernel, (cap, halo)),
        (struct((gx_size * groups, 1, 128), F32), field, field),
        came
        + (recv_hot, near_coupling, local, near_first)
        + (mid, final2, k0, k1, partial),
        "vvvvvvvvvhhrrv",
        "vvv",
        scratch=[copy_sems, work],
    )
    rows = lax.all_to_all(rows, ("gx", "yz"), 0, 0, tiled=True)
    (update,) = call(combine_kernel, (field,), (rows, k0, k1), "vvv")
    return update


def solution(mesh):
    by_column = P(None, ("gx", "yz"))
    by_row = P(("gx", "yz"), None)
    by_plane = P(("gx", "yz"), None, None)
    return jax.shard_map(
        on_device,
        mesh=mesh,
        in_specs=(by_column,) * 4
        + (P(), P())
        + (by_column,) * 2
        + (by_plane,) * 2
        + (by_row,) * 6,
        out_specs=by_column,
        check_vma=False,
    )
```

```python
import functools

import jax
import jax.numpy as jnp
import numpy as np
from jax import lax
from jax.experimental import pallas as pl
from jax.experimental.pallas import tpu as pltpu
from jax.sharding import PartitionSpec as P

EPS = 1e-06
NODES = 4
VARS = 5
TILE = VARS * NODES * NODES
DOFS = TILE * NODES
FACES = 6
FOLD = 64
CHUNK = 1
K2_SCALE = 2.0**-20
VMEM_LIMIT = 40 * 2**20
F32 = jnp.float32
BF16 = jnp.bfloat16


def gll_tables():
    root = 1.0 / np.sqrt(5.0)
    points = np.array([-1.0, -root, root, 1.0])
    weights = np.array([1.0, 5.0, 5.0, 1.0]) / 6.0

    def lagrange(at):
        values = np.ones((len(at), 4))
        for j in range(4):
            for m in range(4):
                if m != j:
                    values[:, j] = values[:, j] * (at - points[m]) / (points[j] - points[m])
        return values

    derivative = np.zeros((4, 4))
    for i in range(4):
        for j in range(4):
            total = 0.0
            for m in range(4):
                if m != j:
                    term = 1.0 / (points[j] - points[m])
                    for n in range(4):
                        if n != j and n != m:
                            term = term * (points[i] - points[n]) / (points[j] - points[n])
                    total = total + term
            derivative[i, j] = total
    halves = [lagrange((points - 1.0) / 2.0), lagrange((points + 1.0) / 2.0)]
    projections = [0.5 * (1.0 / weights)[:, None] * h.T * weights[None, :] for h in halves]
    interpolate = [np.kron(halves[q // 2], halves[q % 2]) for q in range(4)]
    project = [np.kron(projections[q // 2], projections[q % 2]) for q in range(4)]
    return derivative, interpolate, project


def pieces(matrix):
    value = np.asarray(matrix, np.float32)
    high = value.astype(jnp.bfloat16)
    low = (value - high.astype(np.float32)).astype(jnp.bfloat16)
    return high, low


def constant_matrices():
    derivative, interpolate, project = gll_tables()
    eye_vars = np.eye(VARS)
    blocks = [np.kron(eye_vars, m) for m in project + interpolate]
    tiles = np.concatenate(pieces(np.concatenate(blocks, axis=1)), axis=0)
    eye = np.eye(4)
    volume = np.concatenate(
        [
            np.kron(derivative, np.kron(eye, eye)),
            np.kron(eye, np.kron(derivative, eye)),
            np.kron(eye, np.kron(eye, derivative)),
        ],
        axis=1,
    )
    volume = np.concatenate(pieces(volume), axis=0)
    return jnp.asarray(tiles), jnp.asarray(volume)


def split(x):
    high = x.astype(BF16)
    low = (x - high.astype(F32)).astype(BF16)
    return high, low


def mm(a, b):
    return jnp.dot(a, b, preferred_element_type=F32)


def mm3(a_high, a_low, b):
    columns = b.shape[1]
    b_high, b_low = split(b)
    first = mm(a_high, jnp.concatenate([b_high, b_low], axis=1))
    return first[:, :columns] + (first[:, columns:] + mm(a_low, b_high))


def solve_cells(x, first_ref, final_ref, mid_ref):
    inner = mm3(first_ref[0], first_ref[1], x)
    return mm3(final_ref[0], final_ref[1], mid_ref[...] * inner)


def face_rows(ref, face):
    end = NODES - 1 if face % 2 else 0
    if face // 2 == 0:
        return jnp.concatenate(
            [ref[pl.ds(a * 64 + end * 16, 16), :] for a in range(VARS)], axis=0
        )
    if face // 2 == 1:
        return jnp.concatenate(
            [ref[pl.ds(g * 16 + end * 4, 4), :] for g in range(VARS * 4)], axis=0
        )
    return ref[pl.ds(end, TILE, stride=4), :]


def add_to_face(ref, face, value):
    end = NODES - 1 if face % 2 else 0
    if face // 2 == 0:
        for a in range(VARS):
            ref[pl.ds(a * 64 + end * 16, 16), :] += value[a * 16 : a * 16 + 16]
    elif face // 2 == 1:
        for g in range(VARS * 4):
            ref[pl.ds(g * 16 + end * 4, 4), :] += value[g * 4 : g * 4 + 4]
    else:
        ref[pl.ds(end, TILE, stride=4), :] += value


def all_traces(ref):
    return jnp.concatenate([face_rows(ref, f) for f in range(FACES)], axis=1)


def two_pieces(x):
    high, low = split(x)
    return jnp.concatenate([high, low], axis=0)


def one_hot(condition):
    return jnp.where(condition, 1.0, 0.0).astype(BF16)


def lane_row(length):
    return lax.broadcasted_iota(jnp.int32, (1, length), 1)


def fold_plan(columns):
    for rows in range(8, TILE + 1, 8):
        full, rest = TILE // rows, TILE % rows
        parts = rows // rest if rest else 1
        width = -(-columns // parts) if rest else 0
        if full * columns + width <= 128:
            break
    plan = [(g * rows, rows, 0, columns, 0, g * columns) for g in range(full)]
    if rest:
        for part in range(parts):
            count = min(width, columns - part * width)
            if count > 0:
                plan.append(
                    (full * rows, rest, part * width, count, part * rest, full * columns)
                )
    return rows, plan


def table_lanes(groups, cap, halo):
    return -(-(groups * 2 * cap + 4 * halo) // 128) * 128


def roll_lanes(x, shift):
    return pltpu.roll(x, shift % 128, 1) if shift % 128 else x


def in_lanes(start, count):
    lane = lane_row(128)
    return (lane >= start) & (lane < start + count)


def window(blocks, rows, start, width, to):
    block, offset = start // 128, start % 128
    value = roll_lanes(blocks[block][rows], to - offset)
    if offset + width > 128:
        after = roll_lanes(blocks[block + 1][rows], to - offset)
        value = jnp.where(lane_row(128) < to + 128 - offset, value, after)
    return value


def fold_halves(block):
    middle = TILE // 2
    return jnp.where(
        lane_row(128) < FOLD, block[:middle], roll_lanes(block[middle:], FOLD)
    )


def unfold_halves(block):
    return jnp.concatenate([block, roll_lanes(block, FOLD)], axis=0)


def pick_columns(table, ids):
    lane = jnp.broadcast_to(ids % 128, (TILE, 128))
    block = ids // 128
    value = jnp.zeros((TILE, 128), F32)
    for b, part in enumerate(table):
        part = jnp.take_along_axis(part, lane, axis=1, mode="promise_in_bounds")
        value = jnp.where(block == b, part, value)
    return value


def pack_send(field_ref, send_id, codes, tiles_ref, send_ref, edge_ref, sizes, ship):
    cap, halo = sizes
    groups = send_ref.shape[0]
    traces = all_traces(field_ref)
    table = [traces[:, b : b + 128] for b in range(0, traces.shape[1], 128)]
    rows, plan = fold_plan(2 * cap)
    picked, done, sent = [], [], 0
    count = send_id.shape[1] // 128
    for part, start in enumerate(range(0, count, CHUNK)):
        lanes = slice(start * 128, min(start + CHUNK, count) * 128)
        for b in range(lanes.start, lanes.stop, 128):
            picked.append(pick_columns(table, send_id[:, b : b + 128]))
        high, low = split(jnp.concatenate(picked[start:], axis=1))
        masks = [one_hot(codes[:, lanes] == q) for q in range(8)]
        high_stack = jnp.concatenate([high * m for m in masks], axis=0)
        low_stack = jnp.concatenate([low * m for m in masks], axis=0)
        result = mm(tiles_ref[...], high_stack)
        result = result[:TILE] + (result[TILE:] + mm(tiles_ref[:TILE], low_stack))
        done += [result[:, b : b + 128] for b in range(0, result.shape[1], 128)]
        ready = min(groups, lanes.stop // (2 * cap))
        for group in range(sent, ready):
            folded = [None] * (rows // 8)
            for row, height, column, width, to_row, to_lane in plan:
                piece = window(
                    done, slice(row, row + height), group * 2 * cap + column, width, to_lane
                )
                for k in range(height // 8):
                    at, value = to_row // 8 + k, piece[8 * k : 8 * k + 8]
                    if folded[at] is not None:
                        value = jnp.where(in_lanes(to_lane, width), value, folded[at])
                    folded[at] = value
            send_ref[group] = jnp.concatenate(folded, axis=0)
        if ready > sent:
            ship(part, sent, ready)
        sent = ready
    edges = window(picked, slice(None), groups * 2 * cap, 4 * halo, 0)
    edge_ref[...] = fold_halves(edges)


def unpack_received(recv_ref, edge, sizes):
    cap, halo = sizes
    groups = recv_ref.shape[0]
    plan = fold_plan(2 * cap)[1]
    wide = [[None] * (TILE // 8) for _ in range(table_lanes(groups, cap, halo) // 128)]

    def lay(value, row, count, start, width, from_lane):
        offset = start % 128
        value = roll_lanes(value, offset - from_lane)
        for block, low, high in (
            (start // 128, offset, min(128, offset + width)),
            (start // 128 + 1, 0, offset + width - 128),
        ):
            for k in range(count // 8 if high > low else 0):
                part, held = value[8 * k : 8 * k + 8], wide[block][row // 8 + k]
                if held is not None:
                    part = jnp.where(in_lanes(low, high - low), part, held)
                wide[block][row // 8 + k] = part

    for group in range(groups):
        block = recv_ref[group]
        for row, count, column, width, to_row, to_lane in plan:
            start = group * 2 * cap + column
            lay(block[to_row : to_row + count], row, count, start, width, to_lane)
    lay(unfold_halves(edge), 0, TILE, groups * 2 * cap, 4 * halo, 0)
    return jnp.concatenate([jnp.concatenate(w, axis=0) for w in wide], axis=1)


def pick_lanes(rows, ids):
    length = rows[0].shape[1]
    table = jnp.concatenate(rows + [jnp.zeros((8 - len(rows), length), jnp.int32)], axis=0)
    wide = -(-length // 128) * 128
    if wide > length:
        table = jnp.concatenate([table, jnp.zeros((8, wide - length), jnp.int32)], axis=1)
    count = ids.shape[1]
    full = -(-count // 128) * 128
    if full > count:
        ids = jnp.concatenate([ids, jnp.zeros((1, full - count), jnp.int32)], axis=1)
    picked = []
    for start in range(0, full, 128):
        wanted = ids[:, start : start + 128]
        lane = jnp.broadcast_to(wanted % 128, (8, 128))
        value = jnp.zeros((8, 128), jnp.int32)
        for b in range(wide // 128):
            part = jnp.take_along_axis(
                table[:, b * 128 : b * 128 + 128], lane, axis=1, mode="promise_in_bounds"
            )
            value = jnp.where(wanted // 128 == b, part, value)
        picked.append(value)
    return jnp.concatenate(picked, axis=1)[:, :count]


def index_tables(cap, small, outq, inc, inq, coarse, band, plane, elements, sizes):
    gx_size, groups = sizes
    gx_index = lax.axis_index("gx")
    hang, halo = coarse.shape[1], band.shape[1]
    traces = FACES * elements
    lane = lane_row(table_lanes(groups, cap, halo))
    group, within = lane // (2 * cap), lane % (2 * cap)
    is_tile, is_fine = lane < groups * 2 * cap, within < cap
    slot = group * cap + jnp.where(is_fine, within, within - cap)
    edge_lane = lane - groups * 2 * cap
    is_edge = (edge_lane >= 0) & (edge_lane < 4 * halo)
    face = edge_lane // halo
    owned = pick_lanes([coarse], jnp.minimum(inc, hang - 1))[0:1]
    owned = jnp.where(inc < hang, owned, traces)
    placed = pick_lanes([small, owned, outq, inq, inc], jnp.where(is_tile, slot, 0))
    edge = pick_lanes(
        [plane[0:1], plane[1:2], band[0:1], band[1:2]], jnp.where(is_edge, edge_lane % halo, 0)
    )
    tile_id = jnp.where(is_fine, placed[0:1], placed[1:2])
    send_id = jnp.where(is_tile, tile_id, traces)
    codes = jnp.where(is_tile, jnp.where(is_fine, placed[2:3], 4 + placed[3:4]), 8)
    first_hang = traces + 4 * halo
    mortar = placed[4:5]
    tile_recv = jnp.where(
        is_fine, jnp.where(mortar < hang, first_hang + mortar, -1), first_hang + hang + slot
    )
    recv_id = jnp.where(is_tile, tile_recv, -1)
    present = (gx_index < gx_size - 1, gx_index > 0, True, True)
    starts = (traces + halo, traces, traces + 3 * halo, traces + 2 * halo)
    for f in range(4):
        here = is_edge & (face == f)
        send_id = jnp.where(here, f * elements + edge[f : f + 1], send_id)
        recv_id = jnp.where(here & present[f], starts[f] + edge_lane - f * halo, recv_id)
    return send_id, codes, recv_id


class Refs:
    def __init__(self, plan, refs):
        arg_vmem, out_vmem = plan
        refs = list(refs)
        take = lambda n: [refs.pop(0) for _ in range(n)]
        args, outs = take(len(arg_vmem)), take(len(out_vmem))
        self.args = [a if v else refs.pop(0) for a, v in zip(args, arg_vmem)]
        self.outs = [o if v else refs.pop(0) for o, v in zip(outs, out_vmem)]
        in_sems, out_sems = take(2)
        self.work = refs
        self.pending = [
            None if v else pltpu.make_async_copy(a, b, in_sems.at[i])
            for i, (a, b, v) in enumerate(zip(args, self.args, arg_vmem))
        ]
        self.ships = [
            None if v else pltpu.make_async_copy(b, o, out_sems.at[i])
            for i, (o, b, v) in enumerate(zip(outs, self.outs, out_vmem))
        ]
        self.places = outs
        self.sent = []

    def start(self):
        for copy in self.pending:
            if copy is not None:
                copy.start()

    def get(self, i):
        if self.pending[i] is not None:
            self.pending[i].wait()
            self.pending[i] = None
        return self.args[i]

    def ship(self, i):
        if self.ships[i] is not None:
            self.ships[i].start()
            self.sent.append(self.ships[i])

    def ship_rows(self, i, sems):
        def ship(part, start, stop):
            rows = pl.ds(start, stop - start)
            copy = pltpu.make_async_copy(
                self.outs[i].at[rows], self.places[i].at[rows], sems.at[part]
            )
            copy.start()
            self.sent.append(copy)

        return ship

    def finish(self):
        for copy in self.sent:
            copy.wait()


def start_kernel(sizes, plan, *refs):
    r = Refs(plan, refs)
    r.start()
    field, send, edge, ids = r.outs
    first2, final2, part_sems = r.work
    elements = field.shape[1]
    groups = send.shape[0]
    small, outq, inc, inq, coarse, band, plane = [r.get(i) for i in range(7)]
    send_id, codes, recv_id = index_tables(
        small.shape[1] // groups,
        small[...],
        outq[...],
        inc[...],
        inq[...],
        coarse[...],
        band[0],
        plane[0],
        elements,
        sizes,
    )
    ids[...] = jnp.concatenate(
        [send_id, codes, recv_id, jnp.zeros((5, ids.shape[1]), jnp.int32)], axis=0
    )
    r.ship(3)
    first2[0], first2[1] = split(r.get(7)[...])
    final2[0], final2[1] = split(r.get(8)[...])
    field[...] = solve_cells(r.get(9)[...], first2, final2, r.get(10))
    r.ship(0)
    tile_sizes = (small.shape[1] // groups, plane.shape[2])
    ship = r.ship_rows(1, part_sems)
    pack_send(field, send_id, codes, r.get(11), send, edge, tile_sizes, ship)
    r.finish()


def local_part(
    field_ref, mass_ref, coupling_ref, flux_ref, adjacent_ref, volume_ref, local_ref
):
    elements = field_ref.shape[1]
    traces = all_traces(field_ref)
    columns = lax.broadcasted_iota(jnp.int32, (FACES * elements, elements), 0)
    stacked = two_pieces(traces)
    parts = []
    for a in range(VARS):
        flux = []
        for d in range(3):
            total = None
            for b in range(VARS):
                row = d * 25 + a * VARS + b
                term = flux_ref[row : row + 1, :] * field_ref[b * 64 : b * 64 + 64, :]
                total = term if total is None else total + term
            flux.append(total)
        parts.append(jnp.concatenate(flux, axis=0))
    derived = mm3(volume_ref[:64], volume_ref[64:], jnp.concatenate(parts, axis=1))
    for a in range(VARS):
        rows = slice(a * 64, a * 64 + 64)
        local_ref[rows, :] = (
            mass_ref[rows, :] * field_ref[rows, :]
            + derived[:, a * elements : (a + 1) * elements]
        )
    for f in range(FACES):
        near = mm(stacked, one_hot(columns == adjacent_ref[f : f + 1, :]))
        near = near[:TILE] + near[TILE:]
        own = traces[:, f * elements : (f + 1) * elements]
        add_to_face(
            local_ref, f, coupling_ref[f * TILE : (f + 1) * TILE, :] * (own - near)
        )


def hold(r, outs, args):
    copies = [
        pltpu.make_async_copy(r.args[arg], r.outs[out], r.work[0].at[n])
        for n, (out, arg) in enumerate(zip(outs, args))
    ]
    for copy in copies:
        copy.start()
    return copies


def fill_received_hot(ids, adjacent, hot_ref):
    elements = adjacent.shape[1]
    column = jnp.transpose(ids)[:, 2:3]
    for f in range(FACES):
        hot_ref[:, f * elements : (f + 1) * elements] = one_hot(column == adjacent[f : f + 1, :])


def local_kernel(plan, *refs):
    r = Refs(plan, refs)
    local, recv_hot, coupling, mid, first2, final2, ids = r.outs[:7]
    copies = hold(r, (2, 3), (8, 9))
    r.start()
    ids[...] = r.get(5)[...]
    fill_received_hot(ids[...], r.get(3), recv_hot)
    copies[0].wait()
    local_part(r.get(0), r.get(1), coupling, r.get(2), r.get(3), r.get(4), local)
    first2[0], first2[1] = split(r.get(6)[...])
    final2[0], final2[1] = split(r.get(7)[...])
    if len(r.outs) > 7:
        k0, k1 = r.get(10)[...], r.get(0)[...]
        r.outs[7][...] = put(
            [(0, total_of(k0 * k0)), (1, total_of(k0 * k1)), (2, total_of(k1 * k1))]
        )
    copies[1].wait()


def total_of(x):
    return jnp.sum(jnp.sum(x, axis=0, keepdims=True), axis=1, keepdims=True)


def put(values):
    lane = lane_row(128)
    row = jnp.zeros((1, 128), F32)
    for position, value in values:
        row = jnp.where(lane == position, value, row)
    return row


def finish_product(sizes, r, work_ref):
    halo = sizes[1]
    upper, lower, after, before = [r.get(i)[...] for i in range(1, 5)]
    face = lane_row(128) % FOLD // halo
    edge = jnp.where(
        face < 2, jnp.where(face < 1, upper, lower), jnp.where(face < 3, after, before)
    )
    received = unpack_received(r.get(0), edge, sizes)
    near = mm(two_pieces(received), r.get(5)[...])
    near = near[:TILE] + near[TILE:]
    coupling, local = r.get(6), r.get(7)
    elements = local.shape[1]
    work_ref[...] = local[...]
    for f in range(FACES):
        add_to_face(
            work_ref,
            f,
            -coupling[f * TILE : (f + 1) * TILE, :] * near[:, f * elements : (f + 1) * elements],
        )
    mid, first, final = r.get(8), r.get(9), r.get(10)
    inner = mm3(first[0], first[1], work_ref[...])
    return mm3(final[0], final[1], mid[...] * inner)


def middle_kernel(sizes, plan, *refs):
    r = Refs(plan, refs)
    r.start()
    field, send, edge = r.outs
    work, ids = r.work[0], r.get(11)
    ship = r.ship_rows(1, r.work[1])
    field[...] = finish_product(sizes, r, work)
    r.ship(0)
    pack_send(field, ids[0:1, :], ids[1:2, :], r.get(12), send, edge, sizes, ship)
    r.finish()


def last_kernel(sizes, plan, *refs):
    r = Refs(plan, refs)
    work = r.work[1]
    fills = hold(r, (1, 2), (11, 12))
    r.start()
    rows, k0, k1 = r.outs
    k2 = K2_SCALE * finish_product(sizes, r, work)
    for fill in fills:
        fill.wait()
    row = r.get(13)[...] + put(
        [
            (3, total_of(k2 * k0[...])),
            (4, total_of(k2 * k1[...])),
            (5, total_of(k2 * k2)),
        ]
    )
    rows[...] = jnp.broadcast_to(row.reshape(1, 1, 128), rows.shape)


def combine_kernel(plan, *refs):
    r = Refs(plan, refs)
    r.start()
    rows_ref = r.get(0)
    totals = jnp.sum(rows_ref[:, 0, :], axis=0, keepdims=True)
    lane = lane_row(128)
    g00, g01, g11, g02, g12, g22 = [
        jnp.sum(jnp.where(lane == i, totals, 0.0), axis=1, keepdims=True) for i in range(6)
    ]
    scale = 1.0 / K2_SCALE
    beta = jnp.sqrt(g00 + EPS)
    n00, n01, n11 = g00 / beta / beta, g01 / beta / beta, g11 / beta / beta
    h00 = n01
    w_sq = jnp.maximum(n11 - 2.0 * h00 * n01 + h00 * h00 * n00, 0.0)
    h10 = jnp.sqrt(w_sq + EPS)
    unit = beta * h10
    s = scale / unit
    t = h00 * K2_SCALE
    x0 = (g02 - t * g01) * s / beta
    x1 = ((g12 - t * g11) * s - h00 * ((g02 - t * g01) * s)) / unit
    xx = (((g22 - t * g12) - t * (g12 - t * g11)) * s) * s
    v01 = (n01 - h00 * n00) / h10
    v11 = w_sq / h10 / h10
    h01 = x0
    h11 = x1 - h01 * v01
    rest = xx - 2.0 * h01 * x0 + h01 * h01 * n00
    rest = rest - 2.0 * h11 * h11 + h11 * h11 * v11
    h21 = jnp.sqrt(jnp.maximum(rest, 0.0) + EPS)
    radius0 = jnp.sqrt(h00 * h00 + h10 * h10)
    c0, s0 = h00 / radius0, h10 / radius0
    target1 = -s0 * beta
    target0 = c0 * beta
    upper = c0 * h01 + s0 * h11
    lower = c0 * h11 - s0 * h01
    radius1 = jnp.sqrt(lower * lower + h21 * h21)
    y1 = (lower / radius1) * target1 / radius1
    y0 = (target0 - upper * y1) / radius0
    along1 = y1 / unit
    along0 = y0 / beta - along1 * h00
    r.outs[0][...] = along0 * r.get(1)[...] + along1 * r.get(2)[...]
    r.ship(0)
    r.finish()


def call(kernel, outs, args, arg_spaces=None, out_spaces=None, scratch=()):
    arg_spaces = arg_spaces or "h" * len(args)
    out_spaces = out_spaces or "h" * len(outs)
    space = lambda c: pltpu.VMEM if c == "v" else pltpu.HBM
    plan = (tuple(c != "h" for c in arg_spaces), tuple(c != "h" for c in out_spaces))
    buffers = [
        pltpu.VMEM(a.shape, a.dtype)
        for a, c in zip(tuple(args) + tuple(outs), arg_spaces + out_spaces)
        if c == "h"
    ]
    buffers += [pltpu.SemaphoreType.DMA((len(args),)), pltpu.SemaphoreType.DMA((len(outs),))]
    return pl.pallas_call(
        functools.partial(kernel, plan),
        out_shape=tuple(space(c)(o.shape, o.dtype) for o, c in zip(outs, out_spaces)),
        in_specs=[pl.BlockSpec(memory_space=space(c)) for c in arg_spaces],
        out_specs=tuple(pl.BlockSpec(memory_space=space(c)) for c in out_spaces),
        scratch_shapes=buffers + list(scratch),
        cost_estimate=pl.CostEstimate(
            flops=10**9,
            bytes_accessed=sum(a.size * a.dtype.itemsize for a in args),
            transcendentals=0,
        ),
        compiler_params=pltpu.CompilerParams(vmem_limit_bytes=VMEM_LIMIT),
    )(*[pltpu.with_memory_space_constraint(a, space(c)) for a, c in zip(args, arg_spaces)])


def on_device(
    source,
    mass,
    coupling,
    flux,
    first,
    final,
    mid,
    adjacent,
    plane,
    band,
    small,
    proprietor,
    outq,
    inc,
    inq,
    coarse,
):
    del proprietor
    tiles, volume = constant_matrices()
    gx_size, groups = lax.axis_size("gx"), lax.axis_size("yz")
    elements = source.shape[1]
    traces = FACES * elements
    cap, halo = small.shape[1] // groups, plane.shape[2]
    lanes = table_lanes(groups, cap, halo)
    struct = jax.ShapeDtypeStruct
    field = struct((DOFS, elements), F32)
    send = struct((groups, fold_plan(2 * cap)[0], 128), F32)
    edge = struct((TILE // 2, 128), F32)

    part_sems = pltpu.SemaphoreType.DMA((-(-lanes // (128 * CHUNK)),))
    pieces2 = pltpu.VMEM((2, DOFS, DOFS), BF16)
    k0, send0, edge0, ids = call(
        functools.partial(start_kernel, (gx_size, groups)),
        (
            field,
            send,
            edge,
            struct((8, lanes), jnp.int32),
        ),
        (small, outq, inc, inq, coarse, band, plane, first, final, source, mid, tiles),
        out_spaces="hhvh",
        scratch=[pieces2, pieces2, part_sems],
    )

    up = [(i, i + 1) for i in range(gx_size - 1)]
    down = [(j, i) for i, j in up]
    ring = [(i, (i + 1) % groups) for i in range(groups)]
    back = [(j, i) for i, j in ring]

    def exchange(send, edge):
        if gx_size == 2:
            upper = lower = lax.ppermute(edge, "gx", up + down)
        else:
            upper, lower = lax.ppermute(edge, "gx", down), lax.ppermute(edge, "gx", up)
        before, after = lax.ppermute(edge, "yz", ring), lax.ppermute(edge, "yz", back)
        return lax.all_to_all(send, "yz", 0, 0, tiled=True), upper, lower, after, before

    came = exchange(send0, edge0)
    copy_sems = pltpu.SemaphoreType.DMA((2,))
    work = pltpu.VMEM((DOFS, elements), F32)

    def local_step(u, start=()):
        factor = struct((2, DOFS, DOFS), BF16)
        outs = (field, struct((lanes, traces), BF16), struct(coupling.shape, F32), field)
        outs += (factor, factor, struct(ids.shape, jnp.int32))
        outs += (struct((1, 128), F32),) * len(start)
        return call(
            local_kernel,
            outs,
            (u, mass, flux, adjacent, volume, ids, first, final, coupling, mid) + start,
            "hhhhhhhhrr" + "h" * len(start),
            "v" * len(outs),
            scratch=[copy_sems],
        )

    local, recv_hot, near, *factors, near_ids = local_step(k0)
    k1, send1, edge1 = call(
        functools.partial(middle_kernel, (cap, halo)),
        (field, send, edge),
        came + (recv_hot, near, local, *factors, near_ids, tiles),
        "v" * 12 + "h",
        "hhv",
        scratch=[work, part_sems],
    )
    came = exchange(send1, edge1)
    local, recv_hot, near, *factors, near_ids, partial = local_step(k1, (k0,))
    rows, k0, k1 = call(
        functools.partial(last_kernel, (cap, halo)),
        (struct((gx_size * groups, 1, 128), F32), field, field),
        came + (recv_hot, near, local, *factors, k0, k1, partial),
        "v" * 11 + "rrv",
        "vvv",
        scratch=[copy_sems, work],
    )
    rows = lax.all_to_all(rows, ("gx", "yz"), 0, 0, tiled=True)
    (update,) = call(combine_kernel, (field,), (rows, k0, k1), "vvv")
    return update


def solution(mesh):
    by_column = P(None, ("gx", "yz"))
    by_row = P(("gx", "yz"), None)
    by_plane = P(("gx", "yz"), None, None)
    return jax.shard_map(
        on_device,
        mesh=mesh,
        in_specs=(by_column,) * 4
        + (P(), P())
        + (by_column,) * 2
        + (by_plane,) * 2
        + (by_row,) * 6,
        out_specs=by_column,
        check_vma=False,
    )
```

```python
import functools

import jax
import jax.numpy as jnp
import numpy as np
from jax import lax
from jax.experimental import pallas as pl
from jax.experimental.pallas import tpu as pltpu
from jax.sharding import PartitionSpec as P

EPS = 1e-06
NODES = 4
VARS = 5
TILE = VARS * NODES * NODES
DOFS = TILE * NODES
FACES = 6
FOLD = 64
CHUNK = 1
K2_SCALE = 2.0**-20
VMEM_LIMIT = 40 * 2**20
F32 = jnp.float32
BF16 = jnp.bfloat16


def gll_tables():
    root = 1.0 / np.sqrt(5.0)
    points = np.array([-1.0, -root, root, 1.0])
    weights = np.array([1.0, 5.0, 5.0, 1.0]) / 6.0

    def lagrange(at):
        values = np.ones((len(at), 4))
        for j in range(4):
            for m in range(4):
                if m != j:
                    values[:, j] = values[:, j] * (at - points[m]) / (points[j] - points[m])
        return values

    derivative = np.zeros((4, 4))
    for i in range(4):
        for j in range(4):
            total = 0.0
            for m in range(4):
                if m != j:
                    term = 1.0 / (points[j] - points[m])
                    for n in range(4):
                        if n != j and n != m:
                            term = term * (points[i] - points[n]) / (points[j] - points[n])
                    total = total + term
            derivative[i, j] = total
    halves = [lagrange((points - 1.0) / 2.0), lagrange((points + 1.0) / 2.0)]
    projections = [0.5 * (1.0 / weights)[:, None] * h.T * weights[None, :] for h in halves]
    interpolate = [np.kron(halves[q // 2], halves[q % 2]) for q in range(4)]
    project = [np.kron(projections[q // 2], projections[q % 2]) for q in range(4)]
    return derivative, interpolate, project


def pieces(matrix):
    value = np.asarray(matrix, np.float32)
    high = value.astype(jnp.bfloat16)
    low = (value - high.astype(np.float32)).astype(jnp.bfloat16)
    return high, low


def constant_matrices():
    derivative, interpolate, project = gll_tables()
    eye_vars = np.eye(VARS)
    blocks = [np.kron(eye_vars, m) for m in project + interpolate]
    tiles = np.concatenate(pieces(np.concatenate(blocks, axis=1)), axis=0)
    eye = np.eye(4)
    volume = np.concatenate(
        [
            np.kron(derivative, np.kron(eye, eye)),
            np.kron(eye, np.kron(derivative, eye)),
            np.kron(eye, np.kron(eye, derivative)),
        ],
        axis=1,
    )
    volume = np.concatenate(pieces(volume), axis=0)
    return jnp.asarray(tiles), jnp.asarray(volume)


def split(x):
    high = x.astype(BF16)
    low = (x - high.astype(F32)).astype(BF16)
    return high, low


def mm(a, b):
    return jnp.dot(a, b, preferred_element_type=F32)


def mm3(a_high, a_low, b):
    columns = b.shape[1]
    b_high, b_low = split(b)
    first = mm(a_high, jnp.concatenate([b_high, b_low], axis=1))
    return first[:, :columns] + (first[:, columns:] + mm(a_low, b_high))


def face_rows(ref, face):
    end = NODES - 1 if face % 2 else 0
    if face // 2 == 0:
        return jnp.concatenate(
            [ref[pl.ds(a * 64 + end * 16, 16), :] for a in range(VARS)], axis=0
        )
    if face // 2 == 1:
        return jnp.concatenate(
            [ref[pl.ds(g * 16 + end * 4, 4), :] for g in range(VARS * 4)], axis=0
        )
    return ref[pl.ds(end, TILE, stride=4), :]


def add_to_face(ref, face, value):
    end = NODES - 1 if face % 2 else 0
    if face // 2 == 0:
        for a in range(VARS):
            ref[pl.ds(a * 64 + end * 16, 16), :] += value[a * 16 : a * 16 + 16]
    elif face // 2 == 1:
        for g in range(VARS * 4):
            ref[pl.ds(g * 16 + end * 4, 4), :] += value[g * 4 : g * 4 + 4]
    else:
        ref[pl.ds(end, TILE, stride=4), :] += value


def all_traces(ref):
    return jnp.concatenate([face_rows(ref, f) for f in range(FACES)], axis=1)


def two_pieces(x):
    high, low = split(x)
    return jnp.concatenate([high, low], axis=0)


def one_hot(condition):
    return jnp.where(condition, 1.0, 0.0).astype(BF16)


def lane_row(length):
    return lax.broadcasted_iota(jnp.int32, (1, length), 1)


def fold_plan(columns):
    for rows in range(8, TILE + 1, 8):
        full, rest = TILE // rows, TILE % rows
        parts = rows // rest if rest else 1
        width = -(-columns // parts) if rest else 0
        if full * columns + width <= 128:
            break
    plan = [(g * rows, rows, 0, columns, 0, g * columns) for g in range(full)]
    if rest:
        for part in range(parts):
            count = min(width, columns - part * width)
            if count > 0:
                plan.append(
                    (full * rows, rest, part * width, count, part * rest, full * columns)
                )
    return rows, plan


def table_lanes(groups, cap, halo):
    return -(-(groups * 2 * cap + 4 * halo) // 128) * 128


def roll_lanes(x, shift):
    return pltpu.roll(x, shift % 128, 1) if shift % 128 else x


def in_lanes(start, count):
    lane = lane_row(128)
    return (lane >= start) & (lane < start + count)


def window(blocks, rows, start, width, to):
    block, offset = start // 128, start % 128
    value = blocks[block][rows]
    if offset + width > 128:
        value = jnp.where(lane_row(128) >= offset, value, blocks[block + 1][rows])
    return roll_lanes(value, to - offset)


def fold_halves(block):
    middle = TILE // 2
    return jnp.where(
        lane_row(128) < FOLD, block[:middle], roll_lanes(block[middle:], FOLD)
    )


def unfold_halves(block):
    return jnp.concatenate([block, roll_lanes(block, FOLD)], axis=0)


def pick_columns(table, ids):
    lane = jnp.broadcast_to(ids % 128, (TILE, 128))
    block = ids // 128
    value = jnp.zeros((TILE, 128), F32)
    for b, part in enumerate(table):
        part = jnp.take_along_axis(part, lane, axis=1, mode="promise_in_bounds")
        value = jnp.where(block == b, part, value)
    return value


def pack_send(field_ref, send_id, codes, tiles_ref, send_ref, edge_ref, sizes, ship):
    cap, halo = sizes
    groups = send_ref.shape[0]
    traces = all_traces(field_ref)
    table = [traces[:, b : b + 128] for b in range(0, traces.shape[1], 128)]
    rows, plan = fold_plan(2 * cap)
    picked, done, sent = [], [], 0
    count = send_id.shape[1] // 128
    for part, start in enumerate(range(0, count, CHUNK)):
        lanes = slice(start * 128, min(start + CHUNK, count) * 128)
        for b in range(lanes.start, lanes.stop, 128):
            picked.append(pick_columns(table, send_id[:, b : b + 128]))
        high, low = split(jnp.concatenate(picked[start:], axis=1))
        masks = [one_hot(codes[:, lanes] == q) for q in range(8)]
        high_stack = jnp.concatenate([high * m for m in masks], axis=0)
        low_stack = jnp.concatenate([low * m for m in masks], axis=0)
        width = high.shape[1]
        result = mm(tiles_ref[:TILE], jnp.concatenate([high_stack, low_stack], axis=1))
        result = result[:, :width] + (result[:, width:] + mm(tiles_ref[TILE:], high_stack))
        done += [result[:, b : b + 128] for b in range(0, result.shape[1], 128)]
        ready = min(groups, lanes.stop // (2 * cap))
        for group in range(sent, ready):
            folded = [None] * (rows // 8)
            for row, height, column, width, to_row, to_lane in plan:
                piece = window(
                    done, slice(row, row + height), group * 2 * cap + column, width, to_lane
                )
                for k in range(height // 8):
                    at, value = to_row // 8 + k, piece[8 * k : 8 * k + 8]
                    if folded[at] is not None:
                        value = jnp.where(in_lanes(to_lane, width), value, folded[at])
                    folded[at] = value
            send_ref[group] = jnp.concatenate(folded, axis=0)
        if ready > sent:
            ship(part, sent, ready)
        sent = ready
    edges = window(picked, slice(None), groups * 2 * cap, 4 * halo, 0)
    edge_ref[...] = fold_halves(edges)


def unpack_received(recv_ref, edge, sizes):
    cap, halo = sizes
    groups = recv_ref.shape[0]
    plan = fold_plan(2 * cap)[1]
    wide = [[None] * (TILE // 8) for _ in range(table_lanes(groups, cap, halo) // 128)]

    def lay(value, row, count, start, width, from_lane):
        offset = start % 128
        value = roll_lanes(value, offset - from_lane)
        for block, low, high in (
            (start // 128, offset, min(128, offset + width)),
            (start // 128 + 1, 0, offset + width - 128),
        ):
            for k in range(count // 8 if high > low else 0):
                part, held = value[8 * k : 8 * k + 8], wide[block][row // 8 + k]
                if held is not None:
                    part = jnp.where(in_lanes(low, high - low), part, held)
                wide[block][row // 8 + k] = part

    for group in range(groups):
        block = recv_ref[group]
        for row, count, column, width, to_row, to_lane in plan:
            start = group * 2 * cap + column
            lay(block[to_row : to_row + count], row, count, start, width, to_lane)
    lay(unfold_halves(edge), 0, TILE, groups * 2 * cap, 4 * halo, 0)
    return jnp.concatenate([jnp.concatenate(w, axis=0) for w in wide], axis=1)


def pick_lanes(rows, ids):
    length = rows[0].shape[1]
    table = jnp.concatenate(rows + [jnp.zeros((8 - len(rows), length), jnp.int32)], axis=0)
    wide = -(-length // 128) * 128
    if wide > length:
        table = jnp.concatenate([table, jnp.zeros((8, wide - length), jnp.int32)], axis=1)
    count = ids.shape[1]
    full = -(-count // 128) * 128
    if full > count:
        ids = jnp.concatenate([ids, jnp.zeros((1, full - count), jnp.int32)], axis=1)
    picked = []
    for start in range(0, full, 128):
        wanted = ids[:, start : start + 128]
        lane = jnp.broadcast_to(wanted % 128, (8, 128))
        value = jnp.zeros((8, 128), jnp.int32)
        for b in range(wide // 128):
            part = jnp.take_along_axis(
                table[:, b * 128 : b * 128 + 128], lane, axis=1, mode="promise_in_bounds"
            )
            value = jnp.where(wanted // 128 == b, part, value)
        picked.append(value)
    return jnp.concatenate(picked, axis=1)[:, :count]


def index_tables(cap, small, outq, inc, inq, coarse, band, plane, elements, sizes):
    gx_size, groups = sizes
    gx_index = lax.axis_index("gx")
    hang, halo = coarse.shape[1], band.shape[1]
    traces = FACES * elements
    lane = lane_row(table_lanes(groups, cap, halo))
    group, within = lane // (2 * cap), lane % (2 * cap)
    is_tile, is_fine = lane < groups * 2 * cap, within < cap
    slot = group * cap + jnp.where(is_fine, within, within - cap)
    edge_lane = lane - groups * 2 * cap
    is_edge = (edge_lane >= 0) & (edge_lane < 4 * halo)
    face = edge_lane // halo
    owned = pick_lanes([coarse], jnp.minimum(inc, hang - 1))[0:1]
    owned = jnp.where(inc < hang, owned, traces)
    placed = pick_lanes([small, owned, outq, inq, inc], jnp.where(is_tile, slot, 0))
    edge = pick_lanes(
        [plane[0:1], plane[1:2], band[0:1], band[1:2]], jnp.where(is_edge, edge_lane % halo, 0)
    )
    tile_id = jnp.where(is_fine, placed[0:1], placed[1:2])
    send_id = jnp.where(is_tile, tile_id, traces)
    codes = jnp.where(is_tile, jnp.where(is_fine, placed[2:3], 4 + placed[3:4]), 8)
    first_hang = traces + 4 * halo
    mortar = placed[4:5]
    tile_recv = jnp.where(
        is_fine, jnp.where(mortar < hang, first_hang + mortar, -1), first_hang + hang + slot
    )
    recv_id = jnp.where(is_tile, tile_recv, -1)
    present = (gx_index < gx_size - 1, gx_index > 0, True, True)
    starts = (traces + halo, traces, traces + 3 * halo, traces + 2 * halo)
    for f in range(4):
        here = is_edge & (face == f)
        send_id = jnp.where(here, f * elements + edge[f : f + 1], send_id)
        recv_id = jnp.where(here & present[f], starts[f] + edge_lane - f * halo, recv_id)
    return send_id, codes, recv_id


class Refs:
    def __init__(self, plan, refs):
        arg_vmem, out_vmem = plan
        refs = list(refs)
        take = lambda n: [refs.pop(0) for _ in range(n)]
        args, outs = take(len(arg_vmem)), take(len(out_vmem))
        self.args = [a if v else refs.pop(0) for a, v in zip(args, arg_vmem)]
        self.outs = [o if v else refs.pop(0) for o, v in zip(outs, out_vmem)]
        in_sems, out_sems = take(2)
        self.work = refs
        self.pending = [
            None if v else pltpu.make_async_copy(a, b, in_sems.at[i])
            for i, (a, b, v) in enumerate(zip(args, self.args, arg_vmem))
        ]
        self.ships = [
            None if v else pltpu.make_async_copy(b, o, out_sems.at[i])
            for i, (o, b, v) in enumerate(zip(outs, self.outs, out_vmem))
        ]
        self.places = outs
        self.sent = []

    def start(self):
        for copy in self.pending:
            if copy is not None:
                copy.start()

    def get(self, i):
        if self.pending[i] is not None:
            self.pending[i].wait()
            self.pending[i] = None
        return self.args[i]

    def ship(self, i):
        if self.ships[i] is not None:
            self.ships[i].start()
            self.sent.append(self.ships[i])

    def ship_rows(self, i, sems):
        def ship(part, start, stop):
            rows = pl.ds(start, stop - start)
            copy = pltpu.make_async_copy(
                self.outs[i].at[rows], self.places[i].at[rows], sems.at[part]
            )
            copy.start()
            self.sent.append(copy)

        return ship

    def finish(self):
        for copy in self.sent:
            copy.wait()


def start_kernel(sizes, plan, *refs):
    r = Refs(plan, refs)
    r.start()
    field, send, edge, ids = r.outs
    first2, final2, part_sems = r.work
    elements = field.shape[1]
    groups = send.shape[0]
    small, outq, inc, inq, coarse, band, plane = [r.get(i) for i in range(7)]
    send_id, codes, recv_id = index_tables(
        small.shape[1] // groups,
        small[...],
        outq[...],
        inc[...],
        inq[...],
        coarse[...],
        band[0],
        plane[0],
        elements,
        sizes,
    )
    ids[...] = jnp.concatenate(
        [send_id, codes, recv_id, jnp.zeros((5, ids.shape[1]), jnp.int32)], axis=0
    )
    r.ship(3)
    first, final, source, mid = [r.get(i) for i in range(7, 11)]
    first2[0], first2[1] = split(first[...])
    inner = mm3(first2[0], first2[1], source[...])
    final2[0], final2[1] = split(final[...])
    field[...] = mm3(final2[0], final2[1], mid[...] * inner)
    r.ship(0)
    tile_sizes = (small.shape[1] // groups, plane.shape[2])
    ship = r.ship_rows(1, part_sems)
    pack_send(field, send_id, codes, r.get(11), send, edge, tile_sizes, ship)
    r.finish()


def local_part(
    field_ref, mass_ref, coupling_ref, flux_ref, adjacent_ref, volume_ref, local_ref
):
    elements = field_ref.shape[1]
    traces = all_traces(field_ref)
    columns = lax.broadcasted_iota(jnp.int32, (FACES * elements, elements), 0)
    stacked = two_pieces(traces)
    parts = []
    for a in range(VARS):
        flux = []
        for d in range(3):
            total = None
            for b in range(VARS):
                row = d * 25 + a * VARS + b
                term = flux_ref[row : row + 1, :] * field_ref[b * 64 : b * 64 + 64, :]
                total = term if total is None else total + term
            flux.append(total)
        parts.append(jnp.concatenate(flux, axis=0))
    derived = mm3(volume_ref[:64], volume_ref[64:], jnp.concatenate(parts, axis=1))
    for a in range(VARS):
        rows = slice(a * 64, a * 64 + 64)
        local_ref[rows, :] = (
            mass_ref[rows, :] * field_ref[rows, :]
            + derived[:, a * elements : (a + 1) * elements]
        )
    for f in range(FACES):
        near = mm(stacked, one_hot(columns == adjacent_ref[f : f + 1, :]))
        near = near[:TILE] + near[TILE:]
        own = traces[:, f * elements : (f + 1) * elements]
        add_to_face(
            local_ref, f, coupling_ref[f * TILE : (f + 1) * TILE, :] * (own - near)
        )


def hold(r, outs, args):
    copies = [
        pltpu.make_async_copy(r.args[arg], r.outs[out], r.work[0].at[n])
        for n, (out, arg) in enumerate(zip(outs, args))
    ]
    for copy in copies:
        copy.start()
    return copies


def fill_received_hot(ids, adjacent, hot_ref):
    elements = adjacent.shape[1]
    column = jnp.transpose(ids)[:, 2:3]
    for f in range(FACES):
        hot_ref[:, f * elements : (f + 1) * elements] = one_hot(column == adjacent[f : f + 1, :])


def local_kernel(plan, *refs):
    r = Refs(plan, refs)
    local, recv_hot, coupling, mid, first2, final2, ids = r.outs[:7]
    copies = hold(r, (2, 3), (8, 9))
    r.start()
    ids[...] = r.get(5)[...]
    fill_received_hot(ids[...], r.get(3), recv_hot)
    copies[0].wait()
    local_part(r.get(0), r.get(1), coupling, r.get(2), r.get(3), r.get(4), local)
    first2[0], first2[1] = split(r.get(6)[...])
    final2[0], final2[1] = split(r.get(7)[...])
    if len(r.outs) > 7:
        k0, k1 = r.get(10)[...], r.get(0)[...]
        r.outs[7][...] = put(
            [(0, total_of(k0 * k0)), (1, total_of(k0 * k1)), (2, total_of(k1 * k1))]
        )
    copies[1].wait()


def total_of(x):
    return jnp.sum(jnp.sum(x, axis=0, keepdims=True), axis=1, keepdims=True)


def put(values):
    lane = lane_row(128)
    row = jnp.zeros((1, 128), F32)
    for position, value in values:
        row = jnp.where(lane == position, value, row)
    return row


def finish_product(sizes, r, work_ref):
    halo = sizes[1]
    upper, lower, after, before = [r.get(i)[...] for i in range(1, 5)]
    face = lane_row(128) % FOLD // halo
    edge = jnp.where(
        face < 2, jnp.where(face < 1, upper, lower), jnp.where(face < 3, after, before)
    )
    received = unpack_received(r.get(0), edge, sizes)
    near = mm(two_pieces(received), r.get(5)[...])
    near = near[:TILE] + near[TILE:]
    coupling, local = r.get(6), r.get(7)
    elements = local.shape[1]
    work_ref[...] = local[...]
    for f in range(FACES):
        add_to_face(
            work_ref,
            f,
            -coupling[f * TILE : (f + 1) * TILE, :] * near[:, f * elements : (f + 1) * elements],
        )
    mid, first, final = r.get(8), r.get(9), r.get(10)
    inner = mm3(first[0], first[1], work_ref[...])
    return mm3(final[0], final[1], mid[...] * inner)


def middle_kernel(sizes, plan, *refs):
    r = Refs(plan, refs)
    r.start()
    field, send, edge = r.outs
    work, ids = r.work[0], r.get(11)
    ship = r.ship_rows(1, r.work[1])
    field[...] = finish_product(sizes, r, work)
    r.ship(0)
    pack_send(field, ids[0:1, :], ids[1:2, :], r.get(12), send, edge, sizes, ship)
    r.finish()


def last_kernel(sizes, plan, *refs):
    r = Refs(plan, refs)
    work = r.work[1]
    fills = hold(r, (1, 2), (11, 12))
    r.start()
    rows, k0, k1 = r.outs
    k2 = K2_SCALE * finish_product(sizes, r, work)
    for fill in fills:
        fill.wait()
    row = r.get(13)[...] + put(
        [
            (3, total_of(k2 * k0[...])),
            (4, total_of(k2 * k1[...])),
            (5, total_of(k2 * k2)),
        ]
    )
    rows[...] = jnp.broadcast_to(row.reshape(1, 1, 128), rows.shape)


def combine_kernel(plan, *refs):
    r = Refs(plan, refs)
    r.start()
    rows_ref = r.get(0)
    totals = jnp.sum(rows_ref[:, 0, :], axis=0, keepdims=True)
    lane = lane_row(128)
    g00, g01, g11, g02, g12, g22 = [
        jnp.sum(jnp.where(lane == i, totals, 0.0), axis=1, keepdims=True) for i in range(6)
    ]
    scale = 1.0 / K2_SCALE
    beta = jnp.sqrt(g00 + EPS)
    n00, n01, n11 = g00 / beta / beta, g01 / beta / beta, g11 / beta / beta
    h00 = n01
    w_sq = jnp.maximum(n11 - 2.0 * h00 * n01 + h00 * h00 * n00, 0.0)
    h10 = jnp.sqrt(w_sq + EPS)
    unit = beta * h10
    s = scale / unit
    t = h00 * K2_SCALE
    x0 = (g02 - t * g01) * s / beta
    x1 = ((g12 - t * g11) * s - h00 * ((g02 - t * g01) * s)) / unit
    xx = (((g22 - t * g12) - t * (g12 - t * g11)) * s) * s
    v01 = (n01 - h00 * n00) / h10
    v11 = w_sq / h10 / h10
    h01 = x0
    h11 = x1 - h01 * v01
    rest = xx - 2.0 * h01 * x0 + h01 * h01 * n00
    rest = rest - 2.0 * h11 * h11 + h11 * h11 * v11
    h21 = jnp.sqrt(jnp.maximum(rest, 0.0) + EPS)
    radius0 = jnp.sqrt(h00 * h00 + h10 * h10)
    c0, s0 = h00 / radius0, h10 / radius0
    target1 = -s0 * beta
    target0 = c0 * beta
    upper = c0 * h01 + s0 * h11
    lower = c0 * h11 - s0 * h01
    radius1 = jnp.sqrt(lower * lower + h21 * h21)
    y1 = (lower / radius1) * target1 / radius1
    y0 = (target0 - upper * y1) / radius0
    along1 = y1 / unit
    along0 = y0 / beta - along1 * h00
    r.outs[0][...] = along0 * r.get(1)[...] + along1 * r.get(2)[...]
    r.ship(0)
    r.finish()


def call(kernel, outs, args, arg_spaces=None, out_spaces=None, scratch=()):
    arg_spaces = arg_spaces or "h" * len(args)
    out_spaces = out_spaces or "h" * len(outs)
    space = lambda c: pltpu.VMEM if c == "v" else pltpu.HBM
    plan = (tuple(c != "h" for c in arg_spaces), tuple(c != "h" for c in out_spaces))
    buffers = [
        pltpu.VMEM(a.shape, a.dtype)
        for a, c in zip(tuple(args) + tuple(outs), arg_spaces + out_spaces)
        if c == "h"
    ]
    buffers += [pltpu.SemaphoreType.DMA((len(args),)), pltpu.SemaphoreType.DMA((len(outs),))]
    return pl.pallas_call(
        functools.partial(kernel, plan),
        out_shape=tuple(space(c)(o.shape, o.dtype) for o, c in zip(outs, out_spaces)),
        in_specs=[pl.BlockSpec(memory_space=space(c)) for c in arg_spaces],
        out_specs=tuple(pl.BlockSpec(memory_space=space(c)) for c in out_spaces),
        scratch_shapes=buffers + list(scratch),
        cost_estimate=pl.CostEstimate(
            flops=10**9,
            bytes_accessed=sum(a.size * a.dtype.itemsize for a in args),
            transcendentals=0,
        ),
        compiler_params=pltpu.CompilerParams(vmem_limit_bytes=VMEM_LIMIT),
    )(*[pltpu.with_memory_space_constraint(a, space(c)) for a, c in zip(args, arg_spaces)])


def on_device(
    source,
    mass,
    coupling,
    flux,
    first,
    final,
    mid,
    adjacent,
    plane,
    band,
    small,
    proprietor,
    outq,
    inc,
    inq,
    coarse,
):
    del proprietor
    tiles, volume = constant_matrices()
    gx_size, groups = lax.axis_size("gx"), lax.axis_size("yz")
    elements = source.shape[1]
    traces = FACES * elements
    cap, halo = small.shape[1] // groups, plane.shape[2]
    lanes = table_lanes(groups, cap, halo)
    struct = jax.ShapeDtypeStruct
    field = struct((DOFS, elements), F32)
    send = struct((groups, fold_plan(2 * cap)[0], 128), F32)
    edge = struct((TILE // 2, 128), F32)

    part_sems = pltpu.SemaphoreType.DMA((-(-lanes // (128 * CHUNK)),))
    pieces2 = pltpu.VMEM((2, DOFS, DOFS), BF16)
    k0, send0, edge0, ids = call(
        functools.partial(start_kernel, (gx_size, groups)),
        (
            field,
            send,
            edge,
            struct((8, lanes), jnp.int32),
        ),
        (small, outq, inc, inq, coarse, band, plane, first, final, source, mid, tiles),
        out_spaces="hhvh",
        scratch=[pieces2, pieces2, part_sems],
    )

    up = [(i, i + 1) for i in range(gx_size - 1)]
    down = [(j, i) for i, j in up]
    ring = [(i, (i + 1) % groups) for i in range(groups)]
    back = [(j, i) for i, j in ring]

    def exchange(send, edge):
        if gx_size == 2:
            upper = lower = lax.ppermute(edge, "gx", up + down)
        else:
            upper, lower = lax.ppermute(edge, "gx", down), lax.ppermute(edge, "gx", up)
        before, after = lax.ppermute(edge, "yz", ring), lax.ppermute(edge, "yz", back)
        return lax.all_to_all(send, "yz", 0, 0, tiled=True), upper, lower, after, before

    came = exchange(send0, edge0)
    copy_sems = pltpu.SemaphoreType.DMA((2,))
    work = pltpu.VMEM((DOFS, elements), F32)

    def local_step(u, start=()):
        factor = struct((2, DOFS, DOFS), BF16)
        outs = (field, struct((lanes, traces), BF16), struct(coupling.shape, F32), field)
        outs += (factor, factor, struct(ids.shape, jnp.int32))
        outs += (struct((1, 128), F32),) * len(start)
        return call(
            local_kernel,
            outs,
            (u, mass, flux, adjacent, volume, ids, first, final, coupling, mid) + start,
            "hhhhhhhhrr" + "h" * len(start),
            "v" * len(outs),
            scratch=[copy_sems],
        )

    local, recv_hot, near, *factors, near_ids = local_step(k0)
    k1, send1, edge1 = call(
        functools.partial(middle_kernel, (cap, halo)),
        (field, send, edge),
        came + (recv_hot, near, local, *factors, near_ids, tiles),
        "v" * 12 + "h",
        "hhv",
        scratch=[work, part_sems],
    )
    came = exchange(send1, edge1)
    local, recv_hot, near, *factors, near_ids, partial = local_step(k1, (k0,))
    rows, k0, k1 = call(
        functools.partial(last_kernel, (cap, halo)),
        (struct((gx_size * groups, 1, 128), F32), field, field),
        came + (recv_hot, near, local, *factors, k0, k1, partial),
        "v" * 11 + "rrv",
        "vvv",
        scratch=[copy_sems, work],
    )
    rows = lax.all_to_all(rows, ("gx", "yz"), 0, 0, tiled=True)
    (update,) = call(combine_kernel, (field,), (rows, k0, k1), "vvv")
    return update


def solution(mesh):
    by_column = P(None, ("gx", "yz"))
    by_row = P(("gx", "yz"), None)
    by_plane = P(("gx", "yz"), None, None)
    return jax.shard_map(
        on_device,
        mesh=mesh,
        in_specs=(by_column,) * 4
        + (P(), P())
        + (by_column,) * 2
        + (by_plane,) * 2
        + (by_row,) * 6,
        out_specs=by_column,
        check_vma=False,
    )
```

```python
import functools

import jax
import jax.numpy as jnp
import numpy as np
from jax import lax
from jax.experimental import pallas as pl
from jax.experimental.pallas import tpu as pltpu
from jax.sharding import PartitionSpec as P

EPS = 1e-06
NODES = 4
VARS = 5
TILE = VARS * NODES * NODES
DOFS = TILE * NODES
FACES = 6
FOLD = 64
CHUNK = 1
K2_SCALE = 2.0**-20
VMEM_LIMIT = 40 * 2**20
F32 = jnp.float32
BF16 = jnp.bfloat16


def gll_tables():
    root = 1.0 / np.sqrt(5.0)
    points = np.array([-1.0, -root, root, 1.0])
    weights = np.array([1.0, 5.0, 5.0, 1.0]) / 6.0

    def lagrange(at):
        values = np.ones((len(at), 4))
        for j in range(4):
            for m in range(4):
                if m != j:
                    values[:, j] = values[:, j] * (at - points[m]) / (points[j] - points[m])
        return values

    derivative = np.zeros((4, 4))
    for i in range(4):
        for j in range(4):
            total = 0.0
            for m in range(4):
                if m != j:
                    term = 1.0 / (points[j] - points[m])
                    for n in range(4):
                        if n != j and n != m:
                            term = term * (points[i] - points[n]) / (points[j] - points[n])
                    total = total + term
            derivative[i, j] = total
    halves = [lagrange((points - 1.0) / 2.0), lagrange((points + 1.0) / 2.0)]
    projections = [0.5 * (1.0 / weights)[:, None] * h.T * weights[None, :] for h in halves]
    interpolate = [np.kron(halves[q // 2], halves[q % 2]) for q in range(4)]
    project = [np.kron(projections[q // 2], projections[q % 2]) for q in range(4)]
    return derivative, interpolate, project


def pieces(matrix):
    value = np.asarray(matrix, np.float32)
    high = value.astype(jnp.bfloat16)
    low = (value - high.astype(np.float32)).astype(jnp.bfloat16)
    return high, low


def constant_matrices():
    derivative, interpolate, project = gll_tables()
    eye_vars = np.eye(VARS)
    blocks = [np.kron(eye_vars, m) for m in project + interpolate]
    tiles = np.concatenate(pieces(np.concatenate(blocks, axis=1)), axis=0)
    eye = np.eye(4)
    volume = np.concatenate(
        [
            np.kron(derivative, np.kron(eye, eye)),
            np.kron(eye, np.kron(derivative, eye)),
            np.kron(eye, np.kron(eye, derivative)),
        ],
        axis=1,
    )
    volume = np.concatenate(pieces(volume), axis=0)
    return jnp.asarray(tiles), jnp.asarray(volume)


def split(x):
    high = x.astype(BF16)
    low = (x - high.astype(F32)).astype(BF16)
    return high, low


def mm(a, b):
    return jnp.dot(a, b, preferred_element_type=F32)


def mm3(a_high, a_low, b):
    columns = b.shape[1]
    b_high, b_low = split(b)
    first = mm(a_high, jnp.concatenate([b_high, b_low], axis=1))
    return first[:, :columns] + (first[:, columns:] + mm(a_low, b_high))


def face_rows(ref, face):
    end = NODES - 1 if face % 2 else 0
    if face // 2 == 0:
        return jnp.concatenate(
            [ref[pl.ds(a * 64 + end * 16, 16), :] for a in range(VARS)], axis=0
        )
    if face // 2 == 1:
        return jnp.concatenate(
            [ref[pl.ds(g * 16 + end * 4, 4), :] for g in range(VARS * 4)], axis=0
        )
    return ref[pl.ds(end, TILE, stride=4), :]


def add_to_face(ref, face, value):
    end = NODES - 1 if face % 2 else 0
    if face // 2 == 0:
        for a in range(VARS):
            ref[pl.ds(a * 64 + end * 16, 16), :] += value[a * 16 : a * 16 + 16]
    elif face // 2 == 1:
        for g in range(VARS * 4):
            ref[pl.ds(g * 16 + end * 4, 4), :] += value[g * 4 : g * 4 + 4]
    else:
        ref[pl.ds(end, TILE, stride=4), :] += value


def all_traces(ref):
    return jnp.concatenate([face_rows(ref, f) for f in range(FACES)], axis=1)


def two_pieces(x):
    high, low = split(x)
    return jnp.concatenate([high, low], axis=0)


def one_hot(condition):
    return jnp.where(condition, 1.0, 0.0).astype(BF16)


def lane_row(length):
    return lax.broadcasted_iota(jnp.int32, (1, length), 1)


def fold_plan(columns):
    for rows in range(8, TILE + 1, 8):
        full, rest = TILE // rows, TILE % rows
        parts = rows // rest if rest else 1
        width = -(-columns // parts) if rest else 0
        if full * columns + width <= 128:
            break
    plan = [(g * rows, rows, 0, columns, 0, g * columns) for g in range(full)]
    if rest:
        for part in range(parts):
            count = min(width, columns - part * width)
            if count > 0:
                plan.append(
                    (full * rows, rest, part * width, count, part * rest, full * columns)
                )
    return rows, plan


def table_lanes(groups, cap, halo):
    return -(-(groups * 2 * cap + 4 * halo) // 128) * 128


def roll_lanes(x, shift):
    return pltpu.roll(x, shift % 128, 1) if shift % 128 else x


def in_lanes(start, count):
    lane = lane_row(128)
    return (lane >= start) & (lane < start + count)


def window(blocks, rows, start, width, to):
    block, offset = start // 128, start % 128
    value = blocks[block][rows]
    if offset + width > 128:
        value = jnp.where(lane_row(128) >= offset, value, blocks[block + 1][rows])
    return roll_lanes(value, to - offset)


def fold_halves(block):
    middle = TILE // 2
    return jnp.where(
        lane_row(128) < FOLD, block[:middle], roll_lanes(block[middle:], FOLD)
    )


def unfold_halves(block):
    return jnp.concatenate([block, roll_lanes(block, FOLD)], axis=0)


def pick_columns(table, ids):
    lane = jnp.broadcast_to(ids % 128, (TILE, 128))
    block = ids // 128
    value = jnp.zeros((TILE, 128), F32)
    for b, part in enumerate(table):
        part = jnp.take_along_axis(part, lane, axis=1, mode="promise_in_bounds")
        value = jnp.where(block == b, part, value)
    return value


def pack_send(field_ref, send_id, codes, tiles_ref, send_ref, edge_ref, sizes, ship):
    cap, halo = sizes
    groups = send_ref.shape[0]
    traces = all_traces(field_ref)
    table = [traces[:, b : b + 128] for b in range(0, traces.shape[1], 128)]
    rows, plan = fold_plan(2 * cap)
    picked, done, sent = [], [], 0
    count = send_id.shape[1] // 128
    for part, start in enumerate(range(0, count, CHUNK)):
        lanes = slice(start * 128, min(start + CHUNK, count) * 128)
        for b in range(lanes.start, lanes.stop, 128):
            picked.append(pick_columns(table, send_id[:, b : b + 128]))
        high, low = split(jnp.concatenate(picked[start:], axis=1))
        masks = [one_hot(codes[:, lanes] == q) for q in range(8)]
        high_stack = jnp.concatenate([high * m for m in masks], axis=0)
        low_stack = jnp.concatenate([low * m for m in masks], axis=0)
        width = high.shape[1]
        result = mm(tiles_ref[:TILE], jnp.concatenate([high_stack, low_stack], axis=1))
        result = result[:, :width] + (result[:, width:] + mm(tiles_ref[TILE:], high_stack))
        done += [result[:, b : b + 128] for b in range(0, result.shape[1], 128)]
        ready = min(groups, lanes.stop // (2 * cap))
        for group in range(sent, ready):
            folded = [None] * (rows // 8)
            for row, height, column, width, to_row, to_lane in plan:
                piece = window(
                    done, slice(row, row + height), group * 2 * cap + column, width, to_lane
                )
                for k in range(height // 8):
                    at, value = to_row // 8 + k, piece[8 * k : 8 * k + 8]
                    if folded[at] is not None:
                        value = jnp.where(in_lanes(to_lane, width), value, folded[at])
                    folded[at] = value
            send_ref[group] = jnp.concatenate(folded, axis=0)
        if ready > sent:
            ship(part, sent, ready)
        sent = ready
    edges = window(picked, slice(None), groups * 2 * cap, 4 * halo, 0)
    edge_ref[...] = fold_halves(edges)


def unpack_received(recv_ref, edge, sizes):
    cap, halo = sizes
    groups = recv_ref.shape[0]
    plan = fold_plan(2 * cap)[1]
    wide = [[None] * (TILE // 8) for _ in range(table_lanes(groups, cap, halo) // 128)]

    def lay(value, row, count, start, width, from_lane):
        offset = start % 128
        value = roll_lanes(value, offset - from_lane)
        for block, low, high in (
            (start // 128, offset, min(128, offset + width)),
            (start // 128 + 1, 0, offset + width - 128),
        ):
            for k in range(count // 8 if high > low else 0):
                part, held = value[8 * k : 8 * k + 8], wide[block][row // 8 + k]
                if held is not None:
                    part = jnp.where(in_lanes(low, high - low), part, held)
                wide[block][row // 8 + k] = part

    for group in range(groups):
        block = recv_ref[group]
        for row, count, column, width, to_row, to_lane in plan:
            start = group * 2 * cap + column
            lay(block[to_row : to_row + count], row, count, start, width, to_lane)
    lay(unfold_halves(edge), 0, TILE, groups * 2 * cap, 4 * halo, 0)
    return jnp.concatenate([jnp.concatenate(w, axis=0) for w in wide], axis=1)


def pick_lanes(rows, ids):
    length = rows[0].shape[1]
    table = jnp.concatenate(rows + [jnp.zeros((8 - len(rows), length), jnp.int32)], axis=0)
    wide = -(-length // 128) * 128
    if wide > length:
        table = jnp.concatenate([table, jnp.zeros((8, wide - length), jnp.int32)], axis=1)
    count = ids.shape[1]
    full = -(-count // 128) * 128
    if full > count:
        ids = jnp.concatenate([ids, jnp.zeros((1, full - count), jnp.int32)], axis=1)
    picked = []
    for start in range(0, full, 128):
        wanted = ids[:, start : start + 128]
        lane = jnp.broadcast_to(wanted % 128, (8, 128))
        value = jnp.zeros((8, 128), jnp.int32)
        for b in range(wide // 128):
            part = jnp.take_along_axis(
                table[:, b * 128 : b * 128 + 128], lane, axis=1, mode="promise_in_bounds"
            )
            value = jnp.where(wanted // 128 == b, part, value)
        picked.append(value)
    return jnp.concatenate(picked, axis=1)[:, :count]


def index_tables(cap, small, outq, inc, inq, coarse, band, plane, elements, sizes):
    gx_size, groups = sizes
    gx_index = lax.axis_index("gx")
    hang, halo = coarse.shape[1], band.shape[1]
    traces = FACES * elements
    lane = lane_row(table_lanes(groups, cap, halo))
    group, within = lane // (2 * cap), lane % (2 * cap)
    is_tile, is_fine = lane < groups * 2 * cap, within < cap
    slot = group * cap + jnp.where(is_fine, within, within - cap)
    edge_lane = lane - groups * 2 * cap
    is_edge = (edge_lane >= 0) & (edge_lane < 4 * halo)
    face = edge_lane // halo
    owned = pick_lanes([coarse], jnp.minimum(inc, hang - 1))[0:1]
    owned = jnp.where(inc < hang, owned, traces)
    placed = pick_lanes([small, owned, outq, inq, inc], jnp.where(is_tile, slot, 0))
    edge = pick_lanes(
        [plane[0:1], plane[1:2], band[0:1], band[1:2]], jnp.where(is_edge, edge_lane % halo, 0)
    )
    tile_id = jnp.where(is_fine, placed[0:1], placed[1:2])
    send_id = jnp.where(is_tile, tile_id, traces)
    codes = jnp.where(is_tile, jnp.where(is_fine, placed[2:3], 4 + placed[3:4]), 8)
    first_hang = traces + 4 * halo
    mortar = placed[4:5]
    tile_recv = jnp.where(
        is_fine, jnp.where(mortar < hang, first_hang + mortar, -1), first_hang + hang + slot
    )
    recv_id = jnp.where(is_tile, tile_recv, -1)
    present = (gx_index < gx_size - 1, gx_index > 0, True, True)
    starts = (traces + halo, traces, traces + 3 * halo, traces + 2 * halo)
    for f in range(4):
        here = is_edge & (face == f)
        send_id = jnp.where(here, f * elements + edge[f : f + 1], send_id)
        recv_id = jnp.where(here & present[f], starts[f] + edge_lane - f * halo, recv_id)
    return send_id, codes, recv_id


class Refs:
    def __init__(self, plan, refs):
        arg_vmem, out_vmem = plan
        refs = list(refs)
        take = lambda n: [refs.pop(0) for _ in range(n)]
        args, outs = take(len(arg_vmem)), take(len(out_vmem))
        self.args = [a if v else refs.pop(0) for a, v in zip(args, arg_vmem)]
        self.outs = [o if v else refs.pop(0) for o, v in zip(outs, out_vmem)]
        in_sems, out_sems = take(2)
        self.work = refs
        self.pending = [
            None if v else pltpu.make_async_copy(a, b, in_sems.at[i])
            for i, (a, b, v) in enumerate(zip(args, self.args, arg_vmem))
        ]
        self.ships = [
            None if v else pltpu.make_async_copy(b, o, out_sems.at[i])
            for i, (o, b, v) in enumerate(zip(outs, self.outs, out_vmem))
        ]
        self.places = outs
        self.sent = []

    def start(self):
        for copy in self.pending:
            if copy is not None:
                copy.start()

    def get(self, i):
        if self.pending[i] is not None:
            self.pending[i].wait()
            self.pending[i] = None
        return self.args[i]

    def ship(self, i):
        if self.ships[i] is not None:
            self.ships[i].start()
            self.sent.append(self.ships[i])

    def ship_rows(self, i, sems):
        def ship(part, start, stop):
            rows = pl.ds(start, stop - start)
            copy = pltpu.make_async_copy(
                self.outs[i].at[rows], self.places[i].at[rows], sems.at[part]
            )
            copy.start()
            self.sent.append(copy)

        return ship

    def finish(self):
        for copy in self.sent:
            copy.wait()


def start_kernel(sizes, plan, *refs):
    r = Refs(plan, refs)
    r.start()
    field, send, edge, ids = r.outs
    first2, final2, part_sems = r.work
    elements = field.shape[1]
    groups = send.shape[0]
    small, outq, inc, inq, coarse, band, plane = [r.get(i) for i in range(7)]
    send_id, codes, recv_id = index_tables(
        small.shape[1] // groups,
        small[...],
        outq[...],
        inc[...],
        inq[...],
        coarse[...],
        band[0],
        plane[0],
        elements,
        sizes,
    )
    ids[...] = jnp.concatenate(
        [send_id, codes, recv_id, jnp.zeros((5, ids.shape[1]), jnp.int32)], axis=0
    )
    r.ship(3)
    first, source = r.get(7), r.get(8)
    first2[0], first2[1] = split(first[...])
    inner = mm3(first2[0], first2[1], source[...])
    final, mid = r.get(9), r.get(10)
    final2[0], final2[1] = split(final[...])
    field[...] = mm3(final2[0], final2[1], mid[...] * inner)
    r.ship(0)
    tile_sizes = (small.shape[1] // groups, plane.shape[2])
    ship = r.ship_rows(1, part_sems)
    pack_send(field, send_id, codes, r.get(11), send, edge, tile_sizes, ship)
    r.finish()


def local_part(
    field_ref, mass_ref, coupling_ref, flux_ref, adjacent_ref, volume_ref, local_ref
):
    elements = field_ref.shape[1]
    traces = all_traces(field_ref)
    columns = lax.broadcasted_iota(jnp.int32, (FACES * elements, elements), 0)
    stacked = two_pieces(traces)
    parts = []
    for a in range(VARS):
        flux = []
        for d in range(3):
            total = None
            for b in range(VARS):
                row = d * 25 + a * VARS + b
                term = flux_ref[row : row + 1, :] * field_ref[b * 64 : b * 64 + 64, :]
                total = term if total is None else total + term
            flux.append(total)
        parts.append(jnp.concatenate(flux, axis=0))
    derived = mm3(volume_ref[:64], volume_ref[64:], jnp.concatenate(parts, axis=1))
    for a in range(VARS):
        rows = slice(a * 64, a * 64 + 64)
        local_ref[rows, :] = (
            mass_ref[rows, :] * field_ref[rows, :]
            + derived[:, a * elements : (a + 1) * elements]
        )
    for f in range(FACES):
        near = mm(stacked, one_hot(columns == adjacent_ref[f : f + 1, :]))
        near = near[:TILE] + near[TILE:]
        own = traces[:, f * elements : (f + 1) * elements]
        add_to_face(
            local_ref, f, coupling_ref[f * TILE : (f + 1) * TILE, :] * (own - near)
        )


def hold(r, outs, args):
    copies = [
        pltpu.make_async_copy(r.args[arg], r.outs[out], r.work[0].at[n])
        for n, (out, arg) in enumerate(zip(outs, args))
    ]
    for copy in copies:
        copy.start()
    return copies


def fill_received_hot(ids, adjacent, hot_ref):
    elements = adjacent.shape[1]
    column = jnp.transpose(ids)[:, 2:3]
    for f in range(FACES):
        hot_ref[:, f * elements : (f + 1) * elements] = one_hot(column == adjacent[f : f + 1, :])


def local_kernel(plan, *refs):
    r = Refs(plan, refs)
    local, recv_hot, coupling, mid, first2, final2, ids = r.outs[:7]
    copies = hold(r, (2, 3), (8, 9))
    r.start()
    ids[...] = r.get(5)[...]
    fill_received_hot(ids[...], r.get(3), recv_hot)
    copies[0].wait()
    local_part(r.get(0), r.get(1), coupling, r.get(2), r.get(3), r.get(4), local)
    first2[0], first2[1] = split(r.get(6)[...])
    final2[0], final2[1] = split(r.get(7)[...])
    if len(r.outs) > 7:
        k0, k1 = r.get(10)[...], r.get(0)[...]
        r.outs[7][...] = put(
            [(0, total_of(k0 * k0)), (1, total_of(k0 * k1)), (2, total_of(k1 * k1))]
        )
    copies[1].wait()


def total_of(x):
    return jnp.sum(jnp.sum(x, axis=0, keepdims=True), axis=1, keepdims=True)


def put(values):
    lane = lane_row(128)
    row = jnp.zeros((1, 128), F32)
    for position, value in values:
        row = jnp.where(lane == position, value, row)
    return row


def finish_product(sizes, r, work_ref):
    halo = sizes[1]
    upper, lower, after, before = [r.get(i)[...] for i in range(1, 5)]
    face = lane_row(128) % FOLD // halo
    edge = jnp.where(
        face < 2, jnp.where(face < 1, upper, lower), jnp.where(face < 3, after, before)
    )
    received = unpack_received(r.get(0), edge, sizes)
    near = mm(two_pieces(received), r.get(5)[...])
    near = near[:TILE] + near[TILE:]
    coupling, local = r.get(6), r.get(7)
    elements = local.shape[1]
    work_ref[...] = local[...]
    for f in range(FACES):
        add_to_face(
            work_ref,
            f,
            -coupling[f * TILE : (f + 1) * TILE, :] * near[:, f * elements : (f + 1) * elements],
        )
    mid, first, final = r.get(8), r.get(9), r.get(10)
    inner = mm3(first[0], first[1], work_ref[...])
    return mm3(final[0], final[1], mid[...] * inner)


def middle_kernel(sizes, plan, *refs):
    r = Refs(plan, refs)
    r.start()
    field, send, edge = r.outs
    work, ids = r.work[0], r.get(11)
    ship = r.ship_rows(1, r.work[1])
    field[...] = finish_product(sizes, r, work)
    r.ship(0)
    pack_send(field, ids[0:1, :], ids[1:2, :], r.get(12), send, edge, sizes, ship)
    r.finish()


def last_kernel(sizes, plan, *refs):
    r = Refs(plan, refs)
    work = r.work[1]
    fills = hold(r, (1, 2), (11, 12))
    r.start()
    rows, k0, k1 = r.outs
    k2 = K2_SCALE * finish_product(sizes, r, work)
    for fill in fills:
        fill.wait()
    row = r.get(13)[...] + put(
        [
            (3, total_of(k2 * k0[...])),
            (4, total_of(k2 * k1[...])),
            (5, total_of(k2 * k2)),
        ]
    )
    rows[...] = jnp.broadcast_to(row.reshape(1, 1, 128), rows.shape)


def combine_kernel(plan, *refs):
    r = Refs(plan, refs)
    r.start()
    rows_ref = r.get(0)
    totals = jnp.sum(rows_ref[:, 0, :], axis=0, keepdims=True)
    lane = lane_row(128)
    g00, g01, g11, g02, g12, g22 = [
        jnp.sum(jnp.where(lane == i, totals, 0.0), axis=1, keepdims=True) for i in range(6)
    ]
    scale = 1.0 / K2_SCALE
    beta = jnp.sqrt(g00 + EPS)
    n00, n01, n11 = g00 / beta / beta, g01 / beta / beta, g11 / beta / beta
    h00 = n01
    w_sq = jnp.maximum(n11 - 2.0 * h00 * n01 + h00 * h00 * n00, 0.0)
    h10 = jnp.sqrt(w_sq + EPS)
    unit = beta * h10
    s = scale / unit
    t = h00 * K2_SCALE
    x0 = (g02 - t * g01) * s / beta
    x1 = ((g12 - t * g11) * s - h00 * ((g02 - t * g01) * s)) / unit
    xx = (((g22 - t * g12) - t * (g12 - t * g11)) * s) * s
    v01 = (n01 - h00 * n00) / h10
    v11 = w_sq / h10 / h10
    h01 = x0
    h11 = x1 - h01 * v01
    rest = xx - 2.0 * h01 * x0 + h01 * h01 * n00
    rest = rest - 2.0 * h11 * h11 + h11 * h11 * v11
    h21 = jnp.sqrt(jnp.maximum(rest, 0.0) + EPS)
    radius0 = jnp.sqrt(h00 * h00 + h10 * h10)
    c0, s0 = h00 / radius0, h10 / radius0
    target1 = -s0 * beta
    target0 = c0 * beta
    upper = c0 * h01 + s0 * h11
    lower = c0 * h11 - s0 * h01
    radius1 = jnp.sqrt(lower * lower + h21 * h21)
    y1 = (lower / radius1) * target1 / radius1
    y0 = (target0 - upper * y1) / radius0
    along1 = y1 / unit
    along0 = y0 / beta - along1 * h00
    r.outs[0][...] = along0 * r.get(1)[...] + along1 * r.get(2)[...]
    r.ship(0)
    r.finish()


def call(kernel, outs, args, arg_spaces=None, out_spaces=None, scratch=()):
    arg_spaces = arg_spaces or "h" * len(args)
    out_spaces = out_spaces or "h" * len(outs)
    space = lambda c: pltpu.VMEM if c == "v" else pltpu.HBM
    plan = (tuple(c != "h" for c in arg_spaces), tuple(c != "h" for c in out_spaces))
    buffers = [
        pltpu.VMEM(a.shape, a.dtype)
        for a, c in zip(tuple(args) + tuple(outs), arg_spaces + out_spaces)
        if c == "h"
    ]
    buffers += [pltpu.SemaphoreType.DMA((len(args),)), pltpu.SemaphoreType.DMA((len(outs),))]
    return pl.pallas_call(
        functools.partial(kernel, plan),
        out_shape=tuple(space(c)(o.shape, o.dtype) for o, c in zip(outs, out_spaces)),
        in_specs=[pl.BlockSpec(memory_space=space(c)) for c in arg_spaces],
        out_specs=tuple(pl.BlockSpec(memory_space=space(c)) for c in out_spaces),
        scratch_shapes=buffers + list(scratch),
        cost_estimate=pl.CostEstimate(
            flops=10**9,
            bytes_accessed=sum(a.size * a.dtype.itemsize for a in args),
            transcendentals=0,
        ),
        compiler_params=pltpu.CompilerParams(vmem_limit_bytes=VMEM_LIMIT),
    )(*[pltpu.with_memory_space_constraint(a, space(c)) for a, c in zip(args, arg_spaces)])


def on_device(
    source,
    mass,
    coupling,
    flux,
    first,
    final,
    mid,
    adjacent,
    plane,
    band,
    small,
    proprietor,
    outq,
    inc,
    inq,
    coarse,
):
    del proprietor
    tiles, volume = constant_matrices()
    gx_size, groups = lax.axis_size("gx"), lax.axis_size("yz")
    elements = source.shape[1]
    traces = FACES * elements
    cap, halo = small.shape[1] // groups, plane.shape[2]
    lanes = table_lanes(groups, cap, halo)
    struct = jax.ShapeDtypeStruct
    field = struct((DOFS, elements), F32)
    send = struct((groups, fold_plan(2 * cap)[0], 128), F32)
    edge = struct((TILE // 2, 128), F32)

    part_sems = pltpu.SemaphoreType.DMA((-(-lanes // (128 * CHUNK)),))
    pieces2 = pltpu.VMEM((2, DOFS, DOFS), BF16)
    k0, send0, edge0, ids = call(
        functools.partial(start_kernel, (gx_size, groups)),
        (
            field,
            send,
            edge,
            struct((8, lanes), jnp.int32),
        ),
        (small, outq, inc, inq, coarse, band, plane, first, source, final, mid, tiles),
        out_spaces="hhvh",
        scratch=[pieces2, pieces2, part_sems],
    )

    up = [(i, i + 1) for i in range(gx_size - 1)]
    down = [(j, i) for i, j in up]
    ring = [(i, (i + 1) % groups) for i in range(groups)]
    back = [(j, i) for i, j in ring]

    def exchange(send, edge):
        if gx_size == 2:
            upper = lower = lax.ppermute(edge, "gx", up + down)
        else:
            upper, lower = lax.ppermute(edge, "gx", down), lax.ppermute(edge, "gx", up)
        before, after = lax.ppermute(edge, "yz", ring), lax.ppermute(edge, "yz", back)
        return lax.all_to_all(send, "yz", 0, 0, tiled=True), upper, lower, after, before

    came = exchange(send0, edge0)
    copy_sems = pltpu.SemaphoreType.DMA((2,))
    work = pltpu.VMEM((DOFS, elements), F32)

    def local_step(u, start=()):
        factor = struct((2, DOFS, DOFS), BF16)
        outs = (field, struct((lanes, traces), BF16), struct(coupling.shape, F32), field)
        outs += (factor, factor, struct(ids.shape, jnp.int32))
        outs += (struct((1, 128), F32),) * len(start)
        return call(
            local_kernel,
            outs,
            (u, mass, flux, adjacent, volume, ids, first, final, coupling, mid) + start,
            "hhhhhhhhrr" + "h" * len(start),
            "v" * len(outs),
            scratch=[copy_sems],
        )

    local, recv_hot, near, *factors, near_ids = local_step(k0)
    k1, send1, edge1 = call(
        functools.partial(middle_kernel, (cap, halo)),
        (field, send, edge),
        came + (recv_hot, near, local, *factors, near_ids, tiles),
        "v" * 12 + "h",
        "hhv",
        scratch=[work, part_sems],
    )
    came = exchange(send1, edge1)
    local, recv_hot, near, *factors, near_ids, partial = local_step(k1, (k0,))
    rows, k0, k1 = call(
        functools.partial(last_kernel, (cap, halo)),
        (struct((gx_size * groups, 1, 128), F32), field, field),
        came + (recv_hot, near, local, *factors, k0, k1, partial),
        "v" * 11 + "rrv",
        "vvv",
        scratch=[copy_sems, work],
    )
    rows = lax.all_to_all(rows, ("gx", "yz"), 0, 0, tiled=True)
    (update,) = call(combine_kernel, (field,), (rows, k0, k1), "vvv")
    return update


def solution(mesh):
    by_column = P(None, ("gx", "yz"))
    by_row = P(("gx", "yz"), None)
    by_plane = P(("gx", "yz"), None, None)
    return jax.shard_map(
        on_device,
        mesh=mesh,
        in_specs=(by_column,) * 4
        + (P(), P())
        + (by_column,) * 2
        + (by_plane,) * 2
        + (by_row,) * 6,
        out_specs=by_column,
        check_vma=False,
    )
```

```python
import functools

import jax
import jax.numpy as jnp
import numpy as np
from jax import lax
from jax.experimental import pallas as pl
from jax.experimental.pallas import tpu as pltpu
from jax.sharding import PartitionSpec as P

EPS = 1e-06
NODES = 4
VARS = 5
TILE = VARS * NODES * NODES
DOFS = TILE * NODES
FACES = 6
FOLD = 64
CHUNK = 1
K2_SCALE = 2.0**-20
VMEM_LIMIT = 40 * 2**20
F32 = jnp.float32
BF16 = jnp.bfloat16


def gll_tables():
    root = 1.0 / np.sqrt(5.0)
    points = np.array([-1.0, -root, root, 1.0])
    weights = np.array([1.0, 5.0, 5.0, 1.0]) / 6.0

    def lagrange(at):
        values = np.ones((len(at), 4))
        for j in range(4):
            for m in range(4):
                if m != j:
                    values[:, j] = values[:, j] * (at - points[m]) / (points[j] - points[m])
        return values

    derivative = np.zeros((4, 4))
    for i in range(4):
        for j in range(4):
            total = 0.0
            for m in range(4):
                if m != j:
                    term = 1.0 / (points[j] - points[m])
                    for n in range(4):
                        if n != j and n != m:
                            term = term * (points[i] - points[n]) / (points[j] - points[n])
                    total = total + term
            derivative[i, j] = total
    halves = [lagrange((points - 1.0) / 2.0), lagrange((points + 1.0) / 2.0)]
    projections = [0.5 * (1.0 / weights)[:, None] * h.T * weights[None, :] for h in halves]
    interpolate = [np.kron(halves[q // 2], halves[q % 2]) for q in range(4)]
    project = [np.kron(projections[q // 2], projections[q % 2]) for q in range(4)]
    return derivative, interpolate, project


def pieces(matrix):
    value = np.asarray(matrix, np.float32)
    high = value.astype(jnp.bfloat16)
    low = (value - high.astype(np.float32)).astype(jnp.bfloat16)
    return high, low


def constant_matrices():
    derivative, interpolate, project = gll_tables()
    eye_vars = np.eye(VARS)
    blocks = [np.kron(eye_vars, m) for m in project + interpolate]
    tiles = np.concatenate(pieces(np.concatenate(blocks, axis=1)), axis=0)
    eye = np.eye(4)
    volume = np.concatenate(
        [
            np.kron(derivative, np.kron(eye, eye)),
            np.kron(eye, np.kron(derivative, eye)),
            np.kron(eye, np.kron(eye, derivative)),
        ],
        axis=1,
    )
    volume = np.concatenate(pieces(volume), axis=0)
    return jnp.asarray(tiles), jnp.asarray(volume)


def split(x):
    high = x.astype(BF16)
    low = (x - high.astype(F32)).astype(BF16)
    return high, low


def mm(a, b):
    return jnp.dot(a, b, preferred_element_type=F32)


def mm3(a_high, a_low, b):
    columns = b.shape[1]
    b_high, b_low = split(b)
    first = mm(a_high, jnp.concatenate([b_high, b_low], axis=1))
    return first[:, :columns] + (first[:, columns:] + mm(a_low, b_high))


def face_rows(ref, face):
    end = NODES - 1 if face % 2 else 0
    if face // 2 == 0:
        return jnp.concatenate(
            [ref[pl.ds(a * 64 + end * 16, 16), :] for a in range(VARS)], axis=0
        )
    if face // 2 == 1:
        return jnp.concatenate(
            [ref[pl.ds(g * 16 + end * 4, 4), :] for g in range(VARS * 4)], axis=0
        )
    return ref[pl.ds(end, TILE, stride=4), :]


def add_to_face(ref, face, value):
    end = NODES - 1 if face % 2 else 0
    if face // 2 == 0:
        for a in range(VARS):
            ref[pl.ds(a * 64 + end * 16, 16), :] += value[a * 16 : a * 16 + 16]
    elif face // 2 == 1:
        for g in range(VARS * 4):
            ref[pl.ds(g * 16 + end * 4, 4), :] += value[g * 4 : g * 4 + 4]
    else:
        ref[pl.ds(end, TILE, stride=4), :] += value


def all_traces(ref):
    return jnp.concatenate([face_rows(ref, f) for f in range(FACES)], axis=1)


def two_pieces(x):
    high, low = split(x)
    return jnp.concatenate([high, low], axis=0)


def one_hot(condition):
    return jnp.where(condition, 1.0, 0.0).astype(BF16)


def lane_row(length):
    return lax.broadcasted_iota(jnp.int32, (1, length), 1)


def fold_plan(columns):
    for rows in range(8, TILE + 1, 8):
        full, rest = TILE // rows, TILE % rows
        parts = rows // rest if rest else 1
        width = -(-columns // parts) if rest else 0
        if full * columns + width <= 128:
            break
    plan = [(g * rows, rows, 0, columns, 0, g * columns) for g in range(full)]
    if rest:
        for part in range(parts):
            count = min(width, columns - part * width)
            if count > 0:
                plan.append(
                    (full * rows, rest, part * width, count, part * rest, full * columns)
                )
    return rows, plan


def table_lanes(groups, cap, halo):
    return -(-(groups * 2 * cap + 4 * halo) // 128) * 128


def roll_lanes(x, shift):
    return pltpu.roll(x, shift % 128, 1) if shift % 128 else x


def in_lanes(start, count):
    lane = lane_row(128)
    return (lane >= start) & (lane < start + count)


def window(blocks, rows, start, width, to):
    block, offset = start // 128, start % 128
    value = blocks[block][rows]
    if offset + width > 128:
        value = jnp.where(lane_row(128) >= offset, value, blocks[block + 1][rows])
    return roll_lanes(value, to - offset)


def fold_halves(block):
    middle = TILE // 2
    return jnp.where(
        lane_row(128) < FOLD, block[:middle], roll_lanes(block[middle:], FOLD)
    )


def unfold_halves(block):
    return jnp.concatenate([block, roll_lanes(block, FOLD)], axis=0)


def pick_columns(table, ids):
    lane = jnp.broadcast_to(ids % 128, (TILE, 128))
    block = ids // 128
    value = jnp.zeros((TILE, 128), F32)
    for b, part in enumerate(table):
        part = jnp.take_along_axis(part, lane, axis=1, mode="promise_in_bounds")
        value = jnp.where(block == b, part, value)
    return value


def pack_send(field_ref, send_id, codes, tiles_ref, send_ref, edge_ref, sizes, ship):
    cap, halo = sizes
    groups = send_ref.shape[0]
    traces = all_traces(field_ref)
    table = [traces[:, b : b + 128] for b in range(0, traces.shape[1], 128)]
    rows, plan = fold_plan(2 * cap)
    picked, done, sent = [], [], 0
    count = send_id.shape[1] // 128
    for part, start in enumerate(range(0, count, CHUNK)):
        lanes = slice(start * 128, min(start + CHUNK, count) * 128)
        for b in range(lanes.start, lanes.stop, 128):
            picked.append(pick_columns(table, send_id[:, b : b + 128]))
        high, low = split(jnp.concatenate(picked[start:], axis=1))
        masks = [one_hot(codes[:, lanes] == q) for q in range(8)]
        high_stack = jnp.concatenate([high * m for m in masks], axis=0)
        low_stack = jnp.concatenate([low * m for m in masks], axis=0)
        width = high.shape[1]
        result = mm(tiles_ref[:TILE], jnp.concatenate([high_stack, low_stack], axis=1))
        result = result[:, :width] + (result[:, width:] + mm(tiles_ref[TILE:], high_stack))
        done += [result[:, b : b + 128] for b in range(0, result.shape[1], 128)]
        ready = min(groups, lanes.stop // (2 * cap))
        for group in range(sent, ready):
            folded = [None] * (rows // 8)
            for row, height, column, width, to_row, to_lane in plan:
                piece = window(
                    done, slice(row, row + height), group * 2 * cap + column, width, to_lane
                )
                for k in range(height // 8):
                    at, value = to_row // 8 + k, piece[8 * k : 8 * k + 8]
                    if folded[at] is not None:
                        value = jnp.where(in_lanes(to_lane, width), value, folded[at])
                    folded[at] = value
            send_ref[group] = jnp.concatenate(folded, axis=0)
        if ready > sent:
            ship(part, sent, ready)
        sent = ready
    edges = window(picked, slice(None), groups * 2 * cap, 4 * halo, 0)
    edge_ref[...] = fold_halves(edges)


def unpack_received(recv_ref, edge, sizes):
    cap, halo = sizes
    groups = recv_ref.shape[0]
    plan = fold_plan(2 * cap)[1]
    wide = [[None] * (TILE // 8) for _ in range(table_lanes(groups, cap, halo) // 128)]

    def lay(value, row, count, start, width, from_lane):
        offset = start % 128
        value = roll_lanes(value, offset - from_lane)
        for block, low, high in (
            (start // 128, offset, min(128, offset + width)),
            (start // 128 + 1, 0, offset + width - 128),
        ):
            for k in range(count // 8 if high > low else 0):
                part, held = value[8 * k : 8 * k + 8], wide[block][row // 8 + k]
                if held is not None:
                    part = jnp.where(in_lanes(low, high - low), part, held)
                wide[block][row // 8 + k] = part

    for group in range(groups):
        block = recv_ref[group]
        for row, count, column, width, to_row, to_lane in plan:
            start = group * 2 * cap + column
            lay(block[to_row : to_row + count], row, count, start, width, to_lane)
    lay(unfold_halves(edge), 0, TILE, groups * 2 * cap, 4 * halo, 0)
    return jnp.concatenate([jnp.concatenate(w, axis=0) for w in wide], axis=1)


def pick_lanes(rows, ids):
    length = rows[0].shape[1]
    table = jnp.concatenate(rows + [jnp.zeros((8 - len(rows), length), jnp.int32)], axis=0)
    wide = -(-length // 128) * 128
    if wide > length:
        table = jnp.concatenate([table, jnp.zeros((8, wide - length), jnp.int32)], axis=1)
    count = ids.shape[1]
    full = -(-count // 128) * 128
    if full > count:
        ids = jnp.concatenate([ids, jnp.zeros((1, full - count), jnp.int32)], axis=1)
    picked = []
    for start in range(0, full, 128):
        wanted = ids[:, start : start + 128]
        lane = jnp.broadcast_to(wanted % 128, (8, 128))
        value = jnp.zeros((8, 128), jnp.int32)
        for b in range(wide // 128):
            part = jnp.take_along_axis(
                table[:, b * 128 : b * 128 + 128], lane, axis=1, mode="promise_in_bounds"
            )
            value = jnp.where(wanted // 128 == b, part, value)
        picked.append(value)
    return jnp.concatenate(picked, axis=1)[:, :count]


def index_tables(cap, small, outq, inc, inq, coarse, band, plane, elements, sizes):
    gx_size, groups = sizes
    gx_index = lax.axis_index("gx")
    hang, halo = coarse.shape[1], band.shape[1]
    traces = FACES * elements
    lane = lane_row(table_lanes(groups, cap, halo))
    group, within = lane // (2 * cap), lane % (2 * cap)
    is_tile, is_fine = lane < groups * 2 * cap, within < cap
    slot = group * cap + jnp.where(is_fine, within, within - cap)
    edge_lane = lane - groups * 2 * cap
    is_edge = (edge_lane >= 0) & (edge_lane < 4 * halo)
    face = edge_lane // halo
    owned = pick_lanes([coarse], jnp.minimum(inc, hang - 1))[0:1]
    owned = jnp.where(inc < hang, owned, traces)
    placed = pick_lanes([small, owned, outq, inq, inc], jnp.where(is_tile, slot, 0))
    edge = pick_lanes(
        [plane[0:1], plane[1:2], band[0:1], band[1:2]], jnp.where(is_edge, edge_lane % halo, 0)
    )
    tile_id = jnp.where(is_fine, placed[0:1], placed[1:2])
    send_id = jnp.where(is_tile, tile_id, traces)
    codes = jnp.where(is_tile, jnp.where(is_fine, placed[2:3], 4 + placed[3:4]), 8)
    first_hang = traces + 4 * halo
    mortar = placed[4:5]
    tile_recv = jnp.where(
        is_fine, jnp.where(mortar < hang, first_hang + mortar, -1), first_hang + hang + slot
    )
    recv_id = jnp.where(is_tile, tile_recv, -1)
    present = (gx_index < gx_size - 1, gx_index > 0, True, True)
    starts = (traces + halo, traces, traces + 3 * halo, traces + 2 * halo)
    for f in range(4):
        here = is_edge & (face == f)
        send_id = jnp.where(here, f * elements + edge[f : f + 1], send_id)
        recv_id = jnp.where(here & present[f], starts[f] + edge_lane - f * halo, recv_id)
    return send_id, codes, recv_id


class Refs:
    def __init__(self, plan, refs):
        arg_vmem, out_vmem = plan
        refs = list(refs)
        take = lambda n: [refs.pop(0) for _ in range(n)]
        args, outs = take(len(arg_vmem)), take(len(out_vmem))
        self.args = [a if v else refs.pop(0) for a, v in zip(args, arg_vmem)]
        self.outs = [o if v else refs.pop(0) for o, v in zip(outs, out_vmem)]
        in_sems, out_sems = take(2)
        self.work = refs
        self.pending = [
            None if v else pltpu.make_async_copy(a, b, in_sems.at[i])
            for i, (a, b, v) in enumerate(zip(args, self.args, arg_vmem))
        ]
        self.ships = [
            None if v else pltpu.make_async_copy(b, o, out_sems.at[i])
            for i, (o, b, v) in enumerate(zip(outs, self.outs, out_vmem))
        ]
        self.places = outs
        self.sent = []

    def start(self):
        for copy in self.pending:
            if copy is not None:
                copy.start()

    def get(self, i):
        if self.pending[i] is not None:
            self.pending[i].wait()
            self.pending[i] = None
        return self.args[i]

    def ship(self, i):
        if self.ships[i] is not None:
            self.ships[i].start()
            self.sent.append(self.ships[i])

    def ship_rows(self, i, sems):
        def ship(part, start, stop):
            rows = pl.ds(start, stop - start)
            copy = pltpu.make_async_copy(
                self.outs[i].at[rows], self.places[i].at[rows], sems.at[part]
            )
            copy.start()
            self.sent.append(copy)

        return ship

    def finish(self):
        for copy in self.sent:
            copy.wait()


def start_kernel(sizes, plan, *refs):
    r = Refs(plan, refs)
    r.start()
    field, send, edge, ids = r.outs
    first2, final2, part_sems = r.work
    elements = field.shape[1]
    groups = send.shape[0]
    small, outq, inc, inq, coarse, band, plane = [r.get(i) for i in range(7)]
    send_id, codes, recv_id = index_tables(
        small.shape[1] // groups,
        small[...],
        outq[...],
        inc[...],
        inq[...],
        coarse[...],
        band[0],
        plane[0],
        elements,
        sizes,
    )
    ids[...] = jnp.concatenate(
        [send_id, codes, recv_id, jnp.zeros((5, ids.shape[1]), jnp.int32)], axis=0
    )
    r.ship(3)
    first, source = r.get(7), r.get(8)
    first2[0], first2[1] = split(first[...])
    inner = mm3(first2[0], first2[1], source[...])
    final, mid = r.get(9), r.get(10)
    final2[0], final2[1] = split(final[...])
    field[...] = mm3(final2[0], final2[1], mid[...] * inner)
    r.ship(0)
    tile_sizes = (small.shape[1] // groups, plane.shape[2])
    ship = r.ship_rows(1, part_sems)
    pack_send(field, send_id, codes, r.get(11), send, edge, tile_sizes, ship)
    r.finish()


def local_part(
    field_ref, mass_ref, coupling_ref, flux_ref, adjacent_ref, volume_ref, local_ref
):
    elements = field_ref.shape[1]
    traces = all_traces(field_ref)
    columns = lax.broadcasted_iota(jnp.int32, (FACES * elements, elements), 0)
    stacked = two_pieces(traces)
    parts = []
    for a in range(VARS):
        flux = []
        for d in range(3):
            total = None
            for b in range(VARS):
                row = d * 25 + a * VARS + b
                term = flux_ref[row : row + 1, :] * field_ref[b * 64 : b * 64 + 64, :]
                total = term if total is None else total + term
            flux.append(total)
        parts.append(jnp.concatenate(flux, axis=0))
    derived = mm3(volume_ref[:64], volume_ref[64:], jnp.concatenate(parts, axis=1))
    for a in range(VARS):
        rows = slice(a * 64, a * 64 + 64)
        local_ref[rows, :] = (
            mass_ref[rows, :] * field_ref[rows, :]
            + derived[:, a * elements : (a + 1) * elements]
        )
    for f in range(FACES):
        near = mm(stacked, one_hot(columns == adjacent_ref[f : f + 1, :]))
        near = near[:TILE] + near[TILE:]
        own = traces[:, f * elements : (f + 1) * elements]
        add_to_face(
            local_ref, f, coupling_ref[f * TILE : (f + 1) * TILE, :] * (own - near)
        )


def hold(r, outs, args):
    copies = [
        pltpu.make_async_copy(r.args[arg], r.outs[out], r.work[0].at[n])
        for n, (out, arg) in enumerate(zip(outs, args))
    ]
    for copy in copies:
        copy.start()
    return copies


def fill_received_hot(ids, adjacent, hot_ref):
    elements = adjacent.shape[1]
    column = jnp.transpose(ids)[:, 2:3]
    for f in range(FACES):
        hot_ref[:, f * elements : (f + 1) * elements] = one_hot(column == adjacent[f : f + 1, :])


def local_kernel(plan, *refs):
    r = Refs(plan, refs)
    local, recv_hot, coupling, mid, first2, final2, ids = r.outs[:7]
    copies = hold(r, (2, 3), (8, 9))
    r.start()
    ids[...] = r.get(5)[...]
    fill_received_hot(ids[...], r.get(3), recv_hot)
    copies[0].wait()
    local_part(r.get(0), r.get(1), coupling, r.get(2), r.get(3), r.get(4), local)
    first2[0], first2[1] = split(r.get(6)[...])
    final2[0], final2[1] = split(r.get(7)[...])
    if len(r.outs) > 7:
        k0, k1 = r.get(10)[...], r.get(0)[...]
        r.outs[7][...] = put(
            [(0, total_of(k0 * k0)), (1, total_of(k0 * k1)), (2, total_of(k1 * k1))]
        )
    copies[1].wait()


def total_of(x):
    return jnp.sum(jnp.sum(x, axis=0, keepdims=True), axis=1, keepdims=True)


def put(values):
    lane = lane_row(128)
    row = jnp.zeros((1, 128), F32)
    for position, value in values:
        row = jnp.where(lane == position, value, row)
    return row


def finish_product(sizes, r, work_ref):
    halo = sizes[1]
    upper, lower, after, before = [r.get(i)[...] for i in range(1, 5)]
    face = lane_row(128) % FOLD // halo
    edge = jnp.where(
        face < 2, jnp.where(face < 1, upper, lower), jnp.where(face < 3, after, before)
    )
    received = unpack_received(r.get(0), edge, sizes)
    near = mm(two_pieces(received), r.get(5)[...])
    near = near[:TILE] + near[TILE:]
    coupling, local = r.get(6), r.get(7)
    elements = local.shape[1]
    work_ref[...] = local[...]
    for f in range(FACES):
        add_to_face(
            work_ref,
            f,
            -coupling[f * TILE : (f + 1) * TILE, :] * near[:, f * elements : (f + 1) * elements],
        )
    mid, first, final = r.get(8), r.get(9), r.get(10)
    inner = mm3(first[0], first[1], work_ref[...])
    return mm3(final[0], final[1], mid[...] * inner)


def middle_kernel(sizes, plan, *refs):
    r = Refs(plan, refs)
    r.start()
    field, send, edge = r.outs
    work, ids = r.work[0], r.get(11)
    ship = r.ship_rows(1, r.work[1])
    field[...] = finish_product(sizes, r, work)
    r.ship(0)
    pack_send(field, ids[0:1, :], ids[1:2, :], r.get(12), send, edge, sizes, ship)
    r.finish()


def last_kernel(sizes, plan, *refs):
    r = Refs(plan, refs)
    work = r.work[1]
    fills = hold(r, (1, 2), (11, 12))
    r.start()
    rows, k0, k1 = r.outs
    k2 = K2_SCALE * finish_product(sizes, r, work)
    for fill in fills:
        fill.wait()
    row = r.get(13)[...] + put(
        [
            (3, total_of(k2 * k0[...])),
            (4, total_of(k2 * k1[...])),
            (5, total_of(k2 * k2)),
        ]
    )
    rows[...] = jnp.broadcast_to(row.reshape(1, 1, 128), rows.shape)


def combine_kernel(plan, *refs):
    r = Refs(plan, refs)
    r.start()
    rows_ref = r.get(0)
    totals = jnp.sum(rows_ref[:, 0, :], axis=0, keepdims=True)
    lane = lane_row(128)
    g00, g01, g11, g02, g12, g22 = [
        jnp.sum(jnp.where(lane == i, totals, 0.0), axis=1, keepdims=True) for i in range(6)
    ]
    scale = 1.0 / K2_SCALE
    beta = jnp.sqrt(g00 + EPS)
    n00, n01, n11 = g00 / beta / beta, g01 / beta / beta, g11 / beta / beta
    h00 = n01
    w_sq = jnp.maximum(n11 - 2.0 * h00 * n01 + h00 * h00 * n00, 0.0)
    h10 = jnp.sqrt(w_sq + EPS)
    unit = beta * h10
    s = scale / unit
    t = h00 * K2_SCALE
    x0 = (g02 - t * g01) * s / beta
    x1 = ((g12 - t * g11) * s - h00 * ((g02 - t * g01) * s)) / unit
    xx = (((g22 - t * g12) - t * (g12 - t * g11)) * s) * s
    v01 = (n01 - h00 * n00) / h10
    v11 = w_sq / h10 / h10
    h01 = x0
    h11 = x1 - h01 * v01
    rest = xx - 2.0 * h01 * x0 + h01 * h01 * n00
    rest = rest - 2.0 * h11 * h11 + h11 * h11 * v11
    h21 = jnp.sqrt(jnp.maximum(rest, 0.0) + EPS)
    radius0 = jnp.sqrt(h00 * h00 + h10 * h10)
    c0, s0 = h00 / radius0, h10 / radius0
    target1 = -s0 * beta
    target0 = c0 * beta
    upper = c0 * h01 + s0 * h11
    lower = c0 * h11 - s0 * h01
    radius1 = jnp.sqrt(lower * lower + h21 * h21)
    y1 = (lower / radius1) * target1 / radius1
    y0 = (target0 - upper * y1) / radius0
    along1 = y1 / unit
    along0 = y0 / beta - along1 * h00
    r.outs[0][...] = along0 * r.get(1)[...] + along1 * r.get(2)[...]
    r.ship(0)
    r.finish()


def call(kernel, outs, args, arg_spaces=None, out_spaces=None, scratch=(), flags=None):
    arg_spaces = arg_spaces or "h" * len(args)
    out_spaces = out_spaces or "h" * len(outs)
    space = lambda c: pltpu.VMEM if c == "v" else pltpu.HBM
    plan = (tuple(c != "h" for c in arg_spaces), tuple(c != "h" for c in out_spaces))
    buffers = [
        pltpu.VMEM(a.shape, a.dtype)
        for a, c in zip(tuple(args) + tuple(outs), arg_spaces + out_spaces)
        if c == "h"
    ]
    buffers += [pltpu.SemaphoreType.DMA((len(args),)), pltpu.SemaphoreType.DMA((len(outs),))]
    return pl.pallas_call(
        functools.partial(kernel, plan),
        out_shape=tuple(space(c)(o.shape, o.dtype) for o, c in zip(outs, out_spaces)),
        in_specs=[pl.BlockSpec(memory_space=space(c)) for c in arg_spaces],
        out_specs=tuple(pl.BlockSpec(memory_space=space(c)) for c in out_spaces),
        scratch_shapes=buffers + list(scratch),
        cost_estimate=pl.CostEstimate(
            flops=10**9,
            bytes_accessed=sum(a.size * a.dtype.itemsize for a in args),
            transcendentals=0,
        ),
        compiler_params=pltpu.CompilerParams(vmem_limit_bytes=VMEM_LIMIT, flags=flags),
    )(*[pltpu.with_memory_space_constraint(a, space(c)) for a, c in zip(args, arg_spaces)])


def on_device(
    source,
    mass,
    coupling,
    flux,
    first,
    final,
    mid,
    adjacent,
    plane,
    band,
    small,
    proprietor,
    outq,
    inc,
    inq,
    coarse,
):
    del proprietor
    tiles, volume = constant_matrices()
    gx_size, groups = lax.axis_size("gx"), lax.axis_size("yz")
    elements = source.shape[1]
    traces = FACES * elements
    cap, halo = small.shape[1] // groups, plane.shape[2]
    lanes = table_lanes(groups, cap, halo)
    struct = jax.ShapeDtypeStruct
    field = struct((DOFS, elements), F32)
    send = struct((groups, fold_plan(2 * cap)[0], 128), F32)
    edge = struct((TILE // 2, 128), F32)

    part_sems = pltpu.SemaphoreType.DMA((-(-lanes // (128 * CHUNK)),))
    pieces2 = pltpu.VMEM((2, DOFS, DOFS), BF16)
    k0, send0, edge0, ids = call(
        functools.partial(start_kernel, (gx_size, groups)),
        (
            field,
            send,
            edge,
            struct((8, lanes), jnp.int32),
        ),
        (small, outq, inc, inq, coarse, band, plane, first, source, final, mid, tiles),
        out_spaces="hhvh",
        scratch=[pieces2, pieces2, part_sems],
    )

    up = [(i, i + 1) for i in range(gx_size - 1)]
    down = [(j, i) for i, j in up]
    ring = [(i, (i + 1) % groups) for i in range(groups)]
    back = [(j, i) for i, j in ring]

    def exchange(send, edge):
        if gx_size == 2:
            upper = lower = lax.ppermute(edge, "gx", up + down)
        else:
            upper, lower = lax.ppermute(edge, "gx", down), lax.ppermute(edge, "gx", up)
        before, after = lax.ppermute(edge, "yz", ring), lax.ppermute(edge, "yz", back)
        return lax.all_to_all(send, "yz", 0, 0, tiled=True), upper, lower, after, before

    came = exchange(send0, edge0)
    copy_sems = pltpu.SemaphoreType.DMA((2,))
    work = pltpu.VMEM((DOFS, elements), F32)

    def local_step(u, start=()):
        factor = struct((2, DOFS, DOFS), BF16)
        outs = (field, struct((lanes, traces), BF16), struct(coupling.shape, F32), field)
        outs += (factor, factor, struct(ids.shape, jnp.int32))
        outs += (struct((1, 128), F32),) * len(start)
        return call(
            local_kernel,
            outs,
            (u, mass, flux, adjacent, volume, ids, first, final, coupling, mid) + start,
            "hhhhhhhhrr" + "h" * len(start),
            "v" * len(outs),
            scratch=[copy_sems],
        )

    local, recv_hot, near, *factors, near_ids = local_step(k0)
    k1, send1, edge1 = call(
        functools.partial(middle_kernel, (cap, halo)),
        (field, send, edge),
        came + (recv_hot, near, local, *factors, near_ids, tiles),
        "v" * 12 + "h",
        "hhv",
        scratch=[work, part_sems],
    )
    came = exchange(send1, edge1)
    local, recv_hot, near, *factors, near_ids, partial = local_step(k1, (k0,))
    rows, k0, k1 = call(
        functools.partial(last_kernel, (cap, halo)),
        (struct((gx_size * groups, 1, 128), F32), field, field),
        came + (recv_hot, near, local, *factors, k0, k1, partial),
        "v" * 11 + "rrv",
        "vvv",
        scratch=[copy_sems, work],
    )
    rows = lax.all_to_all(rows, ("gx", "yz"), 0, 0, tiled=True)
    (update,) = call(combine_kernel, (field,), (rows, k0, k1), "vvv")
    return update


def solution(mesh):
    by_column = P(None, ("gx", "yz"))
    by_row = P(("gx", "yz"), None)
    by_plane = P(("gx", "yz"), None, None)
    return jax.shard_map(
        on_device,
        mesh=mesh,
        in_specs=(by_column,) * 4
        + (P(), P())
        + (by_column,) * 2
        + (by_plane,) * 2
        + (by_row,) * 6,
        out_specs=by_column,
        check_vma=False,
    )
```
